32 devices in a mesh: node: 8 (over z, y), rep: 4 (over x, core).
Axes of the slice: x: 2, y: 2, z: 4, core: 2. Of those that a mesh axis runs over, the one named last changes fastest.
Arguments:
- tokens: bfloat16 [4096, 8192], P(('node', 'rep')), may hold values from -6 to 6
- norm_gain: float32 [8192], replicated, may hold values from 0.5 to 1.5
- key_cotangent: bfloat16 [4096, 512], P(('node', 'rep')), may hold values from -6 to 6
- secondary: bfloat16 [8192, 512], P('node'), may hold values from -0.0625 to 0.0625
- master: float32 [8192, 512], P(('node', 'rep')), may hold values from -0.0625 to 0.0625
- moment_first: float32 [4096, 1024], P(('node', 'rep')), may hold values from -0.09375 to 0.09375
- moment_second: float32 [4096, 1024], P(('node', 'rep')), may hold values from 6.1035156e-05 to 0.0009765625
- signs: int32 [1024], replicated, may hold values from 0 to 1
Outputs:
- keys: bfloat16 [4096, 512], P(('node', 'rep'))
- token_grad: bfloat16 [4096, 8192], P(('node', 'rep'))
- new_master: float32 [8192, 512], P(('node', 'rep'))
- new_first: float32 [4096, 1024], P(('node', 'rep'))
- new_second: float32 [4096, 1024], P(('node', 'rep'))
- new_secondary: bfloat16 [8192, 512], P('node')
The draws below stay inside these ranges and needn't reach their ends.
All inputs are finite; a program needn't handle non-finite values.
Results may differ from the reference program's by a relative error of at most 0.0049.
Values may be sent and summed in bfloat16 or wider, within the bound.
A program may use at most 128 MiB of HBM per device.

```python
import math
import jax
import jax.numpy as jnp
from jax import lax

D = 8192
KV = 512
TOK_DEV = 128
PAIR_GAP = 16
TOKENS = 4096
N_NODE = 8
N_REP = 4


def with_ends(entries, own_key, low, high):
    longest = entries.shape.index(max(entries.shape))
    spots = []
    for shift in (0, 1):
        where = [jax.random.randint(jax.random.fold_in(own_key, axis), (), 0, length) for axis, length in enumerate(entries.shape)]
        where[longest] = (where[longest] + shift) % entries.shape[longest]
        spots.append(tuple(where))
    return entries.at[spots[0]].set(low).at[spots[1]].set(high)


def strengthened(drawn, key, source, target, blocks, factor):
    def block_of(dim):
        return (jnp.arange(drawn.shape[dim]) // (drawn.shape[dim] // blocks)).reshape((-1,) + (1,) * (drawn.ndim - 1 - dim))

    near = jax.random.permutation(key, blocks)[block_of(target)]
    second = (block_of(target) + blocks // 2) % blocks
    return jnp.where((block_of(source) == near) | (block_of(source) == second), factor * drawn, drawn)


def block_scale(key, dims, split, low, largest):
    gain = 1.0
    for axis_at, blocks in split:
        draws = jax.random.uniform(jax.random.fold_in(jax.random.fold_in(key, 6), axis_at), (blocks,), jnp.float32, low / len(split), largest / len(split))
        gain = gain * jnp.repeat(jnp.exp(draws), dims[axis_at] // blocks).reshape((-1,) + (1,) * (len(dims) - 1 - axis_at))
    return gain


def normal_values(own_key, dims, deviation, limit, pieces=(), kind=jnp.bfloat16):
    drawn = deviation * jax.random.normal(own_key, dims, jnp.float32)
    if pieces:
        drawn = drawn * block_scale(own_key, dims, pieces, -0.22, 0.18)
    return jnp.clip(drawn, -limit, limit).astype(kind)


def heavy_noise(key, shape, deviation, bound, shards, heavy, kind=jnp.bfloat16):
    array = deviation * jax.random.normal(key, shape, jnp.float32)
    if shards:
        array = array * block_scale(key, shape, shards, -0.22, 0.18)
    return jnp.clip(strengthened(array, jax.random.fold_in(key, 3), *heavy), -bound, bound).astype(kind)


def setup_inputs(seed: int = 0) -> dict:
    key_of = jax.random.split(jax.random.key(seed), 9)
    tokens = heavy_noise(key_of[0], (TOKENS, D), 1.0, 6.0, ((0, 32),), (0, 1, 32, 2.75))
    norm_gain = jnp.clip(1.0 + 0.1 * jax.random.normal(key_of[1], (D,), jnp.float32), 0.5, 1.5)
    key_cotangent = normal_values(key_of[2], (TOKENS, KV), 1.0, 6.0, ((0, 32),))
    secondary = normal_values(key_of[3], (D, KV), D ** -0.5, 0.0625, ((0, 8),))
    master = normal_values(key_of[4], (D, KV), D ** -0.5, 0.0625, ((0, 32),), jnp.float32)
    moment_first = normal_values(key_of[5], (D // 2, 2 * KV), (1.0 / (TOK_DEV * N_NODE * N_REP) ** 0.5), 0.09375, ((0, 32),), jnp.float32)
    moment_second = jnp.clip(jnp.exp(math.log(0.0009765625) - 2.7725887 * jax.random.uniform(key_of[6], (D // 2, 2 * KV), jnp.float32) ** block_scale(key_of[6], (D // 2, 2 * KV), ((0, 32),), -0.2, 0.2)), 6.103515625e-05, 0.0009765625)
    signs = with_ends(jax.random.randint(key_of[7], (2 * KV,), 0, 2), jax.random.fold_in(key_of[7], 1), 0, 1).astype(jnp.int32)
    return dict(tokens=tokens, norm_gain=norm_gain, key_cotangent=key_cotangent, secondary=secondary, master=master, moment_first=moment_first, moment_second=moment_second, signs=signs)


norm_eps = 1e-05
adam_eps = 1e-08
beta_first = 0.9
beta_second = 0.95
adam_steps = 10
learn_rate = 0.002
weight_decay = 0.1

def sylvester(extent):
    position = jnp.arange(extent, dtype=jnp.int32)
    parity = jnp.zeros((extent, extent), jnp.int32)
    for bit_place in range(extent.bit_length() - 1):
        parity = parity + (position[:, None] >> bit_place & 1) * (position[None, :] >> bit_place & 1)
    return (1 - 2 * (parity % 2)).astype(jnp.float32)

def reference(tokens, norm_gain, key_cotangent, secondary, master, moment_first, moment_second, signs):
    devices = N_NODE * N_REP
    had_table = sylvester(KV)
    sign_rows = (1 - 2 * signs).astype(jnp.float32).reshape(2, KV)
    rot_scale = 1.0 / (math.sqrt(2 * KV) * TOK_DEV * devices)
    token_blocks = tokens.reshape(devices, TOK_DEV, D)
    cot_blocks = key_cotangent.reshape(devices, TOK_DEV, KV)

    def device_step(running, block):
        activations, cotangent = block
        floats = activations.astype(jnp.float32)
        inverse = lax.rsqrt(lax.optimization_barrier(jnp.mean(floats * floats, axis=-1, keepdims=True)) + norm_eps)
        normed = floats * inverse
        hidden = (normed * norm_gain).astype(jnp.bfloat16)
        keys = jnp.dot(hidden, secondary, preferred_element_type=jnp.float32).astype(jnp.bfloat16)
        hidden_grad = jnp.dot(cotangent, secondary.T, preferred_element_type=jnp.float32)
        scaled = hidden_grad * norm_gain
        token_grad = (inverse * (scaled - normed * lax.optimization_barrier(jnp.mean(scaled * normed, axis=-1, keepdims=True)))).astype(jnp.bfloat16)
        flipped = cotangent.astype(jnp.float32)[:, None, :] * sign_rows
        rotated = (jnp.einsum('tak,kl->tal', flipped, had_table, precision=lax.Precision.HIGHEST) * rot_scale).astype(jnp.bfloat16)
        grouped = hidden.reshape(TOK_DEV, D // (2 * PAIR_GAP), 2, PAIR_GAP).astype(jnp.float32)
        halves = jnp.einsum('tgaj,tak->agjk', grouped, rotated.astype(jnp.float32), precision=lax.Precision.HIGHEST)
        term = jnp.concatenate([halves[0] + halves[1], halves[0] - halves[1]], axis=-1).reshape(D // 2, 2 * KV)
        coded_term = lax.optimization_barrier(term.astype(jnp.bfloat16)).astype(jnp.float32)
        return (running + coded_term, (keys, token_grad))
    start_sum = jnp.zeros((D // 2, 2 * KV), jnp.float32)
    coded, (all_keys, all_grads) = lax.scan(device_step, start_sum, (token_blocks, cot_blocks))
    new_first = beta_first * moment_first + (1.0 - beta_first) * coded
    new_second = beta_second * moment_second + (1.0 - beta_second) * coded * coded
    first_hat = new_first / (1.0 - beta_first ** adam_steps)
    second_hat = new_second / (1.0 - beta_second ** adam_steps)
    ratio = first_hat / (jnp.sqrt(second_hat) + adam_eps)
    lower = ratio[:, :KV]
    upper = ratio[:, KV:]
    norm_root = math.sqrt(2 * KV)
    row_even = jnp.dot(lower + upper, had_table, precision=lax.Precision.HIGHEST) / norm_root * sign_rows[0]
    row_odd = jnp.dot(lower - upper, had_table, precision=lax.Precision.HIGHEST) / norm_root * sign_rows[1]
    stacked = jnp.stack([row_even, row_odd], axis=1)
    update = stacked.reshape(D // (2 * PAIR_GAP), PAIR_GAP, 2, KV).transpose(0, 2, 1, 3).reshape(D, KV)
    new_master = master - learn_rate * (update + weight_decay * master)
    keys_out = all_keys.reshape(devices * TOK_DEV, KV)
    grads_out = all_grads.reshape(devices * TOK_DEV, D)
    return (keys_out, grads_out, new_master, new_first, new_second, new_master.astype(jnp.bfloat16))
```

```python
import functools
import math

import jax
import jax.numpy as jnp
from jax import lax
from jax.experimental import pallas as pl
from jax.experimental.pallas import tpu as pltpu
from jax.sharding import PartitionSpec as P

PAIR_GAP = 16
MESH = pl.DeviceIdType.MESH

norm_eps = 1e-05
adam_eps = 1e-08
beta_first = 0.9
beta_second = 0.95
adam_steps = 10
learn_rate = 0.002
weight_decay = 0.1

ANY = pl.BlockSpec(memory_space=pl.ANY)
HBM = pl.BlockSpec(memory_space=pltpu.HBM)
VMEM = pl.BlockSpec(memory_space=pltpu.VMEM)


def sylvester(extent):
    position = jnp.arange(extent, dtype=jnp.int32)
    parity = jnp.zeros((extent, extent), jnp.int32)
    for bit_place in range(extent.bit_length() - 1):
        parity = parity + (position[:, None] >> bit_place & 1) * (
            position[None, :] >> bit_place & 1
        )
    return (1 - 2 * (parity % 2)).astype(jnp.float32)


def split(index):
    return index // 2, lax.rem(index, 2)


def greet(peers):
    barrier = pltpu.get_barrier_semaphore()
    for peer in peers:
        pl.semaphore_signal(barrier, inc=1, device_id=peer, device_id_type=MESH)
    pl.semaphore_wait(barrier, len(peers))


def remote(src, dst, send, recv, peer):
    return pltpu.make_async_remote_copy(
        src_ref=src,
        dst_ref=dst,
        send_sem=send,
        recv_sem=recv,
        device_id=peer,
        device_id_type=MESH,
    )


def axis_peers(axis, size):
    me = lax.axis_index(axis)
    return [{axis: lax.rem(me + k, size)} for k in range(1, size)]


def pair_peers(axis, size):
    high, low = split(lax.axis_index(axis))
    half = size // 2
    partner = {axis: high * 2 + 1 - low}
    same = [{axis: lax.rem(high + k, half) * 2 + low} for k in range(1, half)]
    return partner, same


class PairGather:
    def __init__(self, axis, size, src, out, local_sem, send, recv):
        self.half = size // 2
        me = lax.axis_index(axis)
        high, low = split(me)
        partner, same = pair_peers(axis, size)
        self.local = pltpu.make_async_copy(src, out.at[me], local_sem)
        self.first = [
            remote(src, out.at[me], send.at[0, k], recv.at[0, k], same[k - 1])
            for k in range(1, self.half)
        ]
        self.second = [remote(src, out.at[me], send.at[1, 0], recv.at[1, 0], partner)]
        for k in range(1, self.half):
            origin = lax.rem(high + self.half - k, self.half) * 2 + low
            self.second.append(
                remote(out.at[origin], out.at[origin], send.at[1, k], recv.at[1, k], partner)
            )

    def start(self):
        for copy in self.first:
            copy.start()
        self.second[0].start()
        self.local.start()

    def forward(self, k):
        self.first[k - 1].wait_recv()
        self.second[k].start()

    def finish(self):
        for copy in self.second:
            copy.wait_recv()
        for copy in self.first + self.second:
            copy.wait_send()
        self.local.wait()


def step_kernel(
    nodes, reps, aligned, scale, hid, cot, sec, table, coded, keys, grad_out,
    hid_in, cot_in, sec_in, rot, term, grad, acc, part,
    from_pair, to_same, from_same, key_in,
    cs, cr, hs, hr, ss, sr, ps, pr, zs, zr, gs, gr, ks, kr, cot_own, hid_own, sec_own, grad_own,
):
    f32 = jnp.float32
    rep = lax.axis_index("rep")
    high, low = split(lax.axis_index("node"))
    half = nodes // 2
    partner, same = pair_peers("node", nodes)
    rep_peers = axis_peers("rep", reps)
    columns, key_width = sec_in.shape[1:]
    tok_rows = cot_in.shape[1]
    group_tokens = reps * tok_rows

    def piece(ref, node, owner):
        index = node * reps + owner
        if aligned:
            return ref.at[:, pl.ds(pl.multiple_of(index * columns, columns), columns)]
        return ref.at[index]

    greet(rep_peers + [partner] + same)
    weights = PairGather(
        "node", nodes, sec.at[pl.ds(pl.multiple_of(rep * columns, columns), columns)], sec_in,
        sec_own.at[0], ss, sr,
    )
    weights.start()
    cot_moves = [
        remote(cot, cot_in.at[rep], cs.at[k], cr.at[k], peer) for k, peer in enumerate(rep_peers)
    ]
    cot_moves.append(pltpu.make_async_copy(cot, cot_in.at[rep], cot_own.at[0]))
    for copy in cot_moves:
        copy.start()
    turns = list(range(1, half)) + [0]
    order = [lax.rem(high + k, half) * 2 + 1 - low for k in turns]
    order += [lax.rem(high + k, half) * 2 + low for k in turns]
    hid_moves = []
    for i, node in enumerate(order):
        moves = [
            remote(
                piece(hid, node, peer["rep"]), hid_in.at[node, rep], hs.at[k, i], hr.at[k, i], peer
            )
            for k, peer in enumerate(rep_peers)
        ]
        moves.append(
            pltpu.make_async_copy(piece(hid, node, rep), hid_in.at[node, rep], hid_own.at[i])
        )
        for copy in moves:
            copy.start()
        hid_moves.append(moves)

    for copy in cot_moves:
        copy.wait()
    group_cot = cot_in[...].reshape(group_tokens, key_width)
    shape = (key_width, key_width)
    parity = lax.broadcasted_iota(jnp.int32, shape, 0) & lax.broadcasted_iota(jnp.int32, shape, 1)
    for shift in (8, 4, 2, 1):
        parity = parity ^ (parity >> shift)
    had = (1 - 2 * (parity & 1)).astype(f32).astype(rot.dtype)
    for a in range(2):
        flipped = (group_cot.astype(f32) * table[a : a + 1, :]).astype(rot.dtype)
        rot[:, a * key_width : (a + 1) * key_width] = (
            jnp.dot(flipped, had, preferred_element_type=f32) * scale
        ).astype(rot.dtype)
    acc[...] = jnp.zeros_like(acc)

    def make_term(i):
        for copy in hid_moves[i]:
            copy.wait()
        chunk = hid_in[order[i]].reshape(group_tokens, columns)
        product = lax.dot_general(
            chunk, rot[...], (((0,), (0,)), ((), ())), preferred_element_type=f32
        ).reshape(columns // (2 * PAIR_GAP), 2, PAIR_GAP, 2 * key_width)
        first = product[:, 0, :, :key_width].reshape(columns // 2, key_width)
        second = product[:, 1, :, key_width:].reshape(columns // 2, key_width)
        term[i, :, :key_width] = (first + second).astype(term.dtype)
        term[i, :, key_width:] = (first - second).astype(term.dtype)

    swaps = []
    stays = []

    def use_weights(count, node):
        block = sec_in[node]
        rows = lax.dot_general(
            cot_in[...].reshape(group_tokens, key_width), block, (((1,), (1,)), ((), ())),
            preferred_element_type=f32,
        )
        grad[node] = rows.astype(grad.dtype).reshape(reps, tok_rows, columns)
        for k, peer in enumerate(rep_peers):
            copy = remote(
                grad.at[node, peer["rep"]], piece(grad_out, node, rep),
                gs.at[k, count], gr.at[k, count], peer,
            )
            copy.start()
            swaps.append(copy)
        copy = pltpu.make_async_copy(
            grad.at[node, rep], piece(grad_out, node, rep), grad_own.at[count]
        )
        copy.start()
        stays.append(copy)
        chunk = hid_in[node].reshape(group_tokens, columns)
        acc[...] += jnp.dot(chunk, block, preferred_element_type=f32)

    pairs = []
    for i in range(half):
        make_term(i)
        pairs.append(remote(term.at[i], from_pair.at[i], ps.at[i], pr.at[i], partner))
        pairs[-1].start()
        if i:
            weights.forward(i)
    weights.local.wait()
    onward = []
    for j, k in enumerate(turns):
        make_term(half + j)
        pairs[j].wait_recv()
        total = term[half + j].astype(f32) + from_pair[j].astype(f32)
        if k:
            to_same[j] = total.astype(to_same.dtype)
            onward.append(remote(to_same.at[j], from_same.at[j], zs.at[j], zr.at[j], same[k - 1]))
            onward[-1].start()
        else:
            coded[...] = total
        use_weights(j, order[half + j])
    for j in range(half):
        weights.second[j].wait_recv()
        use_weights(half + j, lax.rem(high + half - j, half) * 2 + 1 - low)
    part[...] = acc[...].astype(part.dtype).reshape(part.shape)
    key_moves = [
        remote(part.at[peer["rep"]], key_in.at[k], ks.at[k], kr.at[k], peer)
        for k, peer in enumerate(rep_peers)
    ]
    for copy in key_moves:
        copy.start()
    for j, copy in enumerate(onward):
        copy.wait_recv()
        coded[...] += from_same[j].astype(f32)
    total = part[rep].astype(f32)
    for k, copy in enumerate(key_moves):
        copy.wait_recv()
        total = total + key_in[k].astype(f32)
    keys[...] = total.astype(keys.dtype)
    for copy in swaps:
        copy.wait()
    for copy in stays:
        copy.wait()
    for copy in weights.first + weights.second + pairs + onward + key_moves:
        copy.wait_send()


def step(nodes, reps, aligned, scale, hid, cot, sec, table):
    dma = pltpu.SemaphoreType.DMA
    half = nodes // 2
    columns = sec.shape[0] // reps
    tok_rows, key_width = cot.shape
    group_tokens = reps * tok_rows
    block = (columns // 2, 2 * key_width)
    bf16 = jnp.bfloat16
    return pl.pallas_call(
        functools.partial(step_kernel, nodes, reps, aligned, scale),
        out_shape=(
            jax.ShapeDtypeStruct(block, jnp.float32),
            jax.ShapeDtypeStruct(cot.shape, bf16),
            jax.ShapeDtypeStruct(hid.shape, bf16),
        ),
        in_specs=[ANY, ANY, ANY, VMEM],
        out_specs=(VMEM,) * 3,
        scratch_shapes=[
            pltpu.VMEM((nodes, reps, tok_rows, columns), bf16),
            pltpu.VMEM((reps, tok_rows, key_width), bf16),
            pltpu.VMEM((nodes, columns, key_width), bf16),
            pltpu.VMEM((group_tokens, 2 * key_width), bf16),
            pltpu.VMEM((nodes,) + block, bf16),
            pltpu.VMEM((nodes, reps, tok_rows, columns), bf16),
            pltpu.VMEM((group_tokens, key_width), jnp.float32),
            pltpu.VMEM((reps, tok_rows, key_width), bf16),
            pltpu.VMEM((half,) + block, bf16),
            pltpu.VMEM((half - 1,) + block, bf16),
            pltpu.VMEM((half - 1,) + block, bf16),
            pltpu.VMEM((reps - 1, tok_rows, key_width), bf16),
        ]
        + [dma((reps - 1,))] * 2
        + [dma((reps - 1, nodes))] * 2
        + [dma((2, half))] * 2
        + [dma((half,))] * 2
        + [dma((half - 1,))] * 2
        + [dma((reps - 1, nodes))] * 2
        + [dma((reps - 1,))] * 2
        + [dma((1,)), dma((nodes,)), dma((1,)), dma((nodes,))],
        compiler_params=pltpu.CompilerParams(collective_id=0, has_side_effects=True),
    )(hid, cot, sec, table)


def spread_kernel(reps, src, out, send, recv, local):
    partner, same = pair_peers("rep", reps)
    greet([partner] + same)
    rows = PairGather("rep", reps, src, out, local.at[0], send, recv)
    rows.start()
    for k in range(1, reps // 2):
        rows.forward(k)
    rows.finish()


def spread(reps, rows):
    dma = pltpu.SemaphoreType.DMA
    return pl.pallas_call(
        functools.partial(spread_kernel, reps),
        out_shape=jax.ShapeDtypeStruct((reps,) + rows.shape, rows.dtype),
        in_specs=[VMEM],
        out_specs=VMEM,
        scratch_shapes=[dma((2, reps // 2))] * 2 + [dma((1,))],
        compiler_params=pltpu.CompilerParams(collective_id=1, has_side_effects=True),
    )(rows)


def flip(index, bits):
    for bit in (1, 2, 4):
        if bits & bit:
            index = index + bit * (1 - 2 * lax.rem(lax.div(index, bit), 2))
    return index


def fused_kernel(
    nodes, reps, scale,
    tok, gain, cot, sec, master, first, second, signs,
    keys_out, grad_out, master_out, first_out, second_out, sec_out,
    x_in, hid, hid_in, cot_in, sec_in, sec_own, rot, had, term, total, from_pair,
    to_near, from_near, to_far, from_far, grad, grad_in, acc, inv,
    part, part_in, cross, cross_in, master_in, first_in, second_in,
    xl, ll, cs, cr, hs, hr, ws, wr, ps, pr, zs, zr, gs, gr, ks, kr, ss, sr,
):
    f32, bf16 = jnp.float32, jnp.bfloat16
    rep = lax.axis_index("rep")
    me = lax.axis_index("node")
    pieces, tok_rows, columns = x_in.shape
    key_width = cot_in.shape[2]
    group_tokens = reps * tok_rows
    half = columns // 2
    rep_kinds = (2, 3, 1)
    rep_peer = {k: {"rep": flip(rep, k)} for k in rep_kinds}
    node_peer = {k: {"node": flip(me, k)} for k in (1, 2, 4)}

    loads = [
        pltpu.make_async_copy(tok.at[:, pl.ds(columns * i, columns)], x_in.at[i], xl.at[i])
        for i in range(pieces)
    ]
    own_cot = pltpu.make_async_copy(cot, cot_in.at[rep], ll.at[0])
    own_sec = pltpu.make_async_copy(sec, sec_own, ll.at[1])
    state = [
        pltpu.make_async_copy(master, master_in, ll.at[2]),
        pltpu.make_async_copy(first, first_in, ll.at[3]),
        pltpu.make_async_copy(second, second_in, ll.at[4]),
    ]
    for copy in loads + [own_cot, own_sec] + state:
        copy.start()
    greet([rep_peer[k] for k in rep_kinds] + [node_peer[k] for k in (1, 2, 4)])

    sent = []

    def go(copy):
        copy.start()
        sent.append(copy)
        return copy

    quarter = sec.at[pl.ds(pl.multiple_of(rep * columns, columns), columns)]
    slots = {}

    def weight(source, via):
        slot = len(slots)
        src = sec_in.at[flip(me, source)] if source else quarter
        copy = remote(src, sec_in.at[flip(me, source)], ws.at[slot], wr.at[slot], node_peer[via])
        slots[source ^ via] = go(copy)

    held = set()

    def arrived(bits):
        if bits not in held:
            held.add(bits)
            slots[bits].wait_recv()

    weight(0, 4)
    weight(0, 1)
    weight(0, 2)
    cot_moves = {
        2: go(remote(cot, cot_in.at[rep], cs.at[0], cr.at[0], rep_peer[2])),
        1: go(remote(cot, cot_in.at[rep], cs.at[1], cr.at[1], rep_peer[1])),
    }

    for copy in loads:
        copy.wait()

    def squares(i, running):
        x = x_in[i].astype(f32)
        x = x * x
        for lane in range(0, columns, 128):
            running = running + x[:, lane : lane + 128]
        return running

    squared = lax.fori_loop(0, pieces, squares, jnp.zeros((tok_rows, 128), f32))
    mean = jnp.sum(squared, axis=-1, keepdims=True) * (1.0 / (pieces * columns))
    inv[...] = jnp.broadcast_to(lax.rsqrt(mean + norm_eps), inv.shape)

    order = [7, 3, 5, 1, 6, 2, 4, 0]
    hid_moves = []
    for i, bits in enumerate(order):
        node = flip(me, bits)
        moves = []
        for k in rep_kinds + (0,):
            owner = flip(rep, k)
            index = node * reps + owner
            value = (x_in[index].astype(f32) * inv[...] * gain[index]).astype(bf16)
            if k:
                hid[node, owner] = value
                moves.append(
                    go(
                        remote(
                            hid.at[node, owner], hid_in.at[node, rep],
                            hs.at[k - 1, i], hr.at[k - 1, i], rep_peer[k],
                        )
                    )
                )
            else:
                hid_in[node, rep] = value
        hid_moves.append(moves)

    shape = (key_width, key_width)
    parity = lax.broadcasted_iota(jnp.int32, shape, 0) & lax.broadcasted_iota(jnp.int32, shape, 1)
    for shift in (8, 4, 2, 1):
        parity = parity ^ (parity >> shift)
    had[...] = (1 - 2 * (parity & 1)).astype(f32).astype(bf16)
    chunks = key_width // 128
    sign_row = []
    for a in range(2):
        bits = [signs[a * chunks + c : a * chunks + c + 1, :] for c in range(chunks)]
        sign_row.append((1 - 2 * jnp.concatenate(bits, axis=1)).astype(f32))

    cot_moves[2].wait_recv()
    across = cot_in.at[flip(rep, 2)]
    cot_moves[3] = go(remote(across, across, cs.at[2], cr.at[2], rep_peer[1]))
    own_cot.wait()
    cot_moves[1].wait_recv()
    cot_moves[3].wait_recv()
    for a in range(2):
        flipped = (cot_in[...].reshape(group_tokens, key_width).astype(f32) * sign_row[a]).astype(bf16)
        rot[:, a * key_width : (a + 1) * key_width] = (
            jnp.dot(flipped, had[...], preferred_element_type=f32) * scale
        ).astype(bf16)

    def make_term(i):
        for copy in hid_moves[i]:
            copy.wait_recv()
        chunk = hid_in[flip(me, order[i])].reshape(group_tokens, columns)
        product = lax.dot_general(
            chunk, rot[...], (((0,), (0,)), ((), ())), preferred_element_type=f32
        ).reshape(columns // (2 * PAIR_GAP), 2, PAIR_GAP, 2 * key_width)
        upper = product[:, 0, :, :key_width].reshape(half, key_width)
        lower = product[:, 1, :, key_width:].reshape(half, key_width)
        return upper + lower, upper - lower

    def halves(ref):
        return ref[:, :key_width].astype(f32), ref[:, key_width:].astype(f32)

    def put(ref, pair):
        ref[:, :key_width] = pair[0].astype(ref.dtype)
        ref[:, key_width:] = pair[1].astype(ref.dtype)

    def plus(a, b):
        return a[0] + b[0], a[1] + b[1]

    grad_moves = {}

    def local_grads():
        own_sec.wait()
        for k in range(reps):
            block = sec_own[pl.ds(k * columns, columns)]
            grad_in[me * reps + k] = lax.dot_general(
                cot_in[rep], block, (((1,), (1,)), ((), ())), preferred_element_type=f32
            ).astype(bf16)
        grad_moves[0] = []

    def use_grads(bits):
        arrived(bits)
        node = flip(me, bits)
        rows = lax.dot_general(
            cot_in[...].reshape(group_tokens, key_width), sec_in[node], (((1,), (1,)), ((), ())),
            preferred_element_type=f32,
        )
        grad[node] = rows.astype(bf16).reshape(reps, tok_rows, columns)
        slot = len(grad_moves)
        grad_moves[bits] = [
            go(
                remote(
                    grad.at[node, flip(rep, k)], grad_in.at[node * reps + rep],
                    gs.at[k - 1, slot], gr.at[k - 1, slot], rep_peer[k],
                )
            )
            for k in rep_kinds
        ]
        grad_in[node * reps + rep] = grad[node, rep]

    def use_keys(bits, start=False):
        node = flip(me, bits)
        block = sec_in[node] if bits else sec_own[pl.ds(pl.multiple_of(rep * columns, columns), columns)]
        product = jnp.dot(
            hid_in[node].reshape(group_tokens, columns), block, preferred_element_type=f32
        )
        if start:
            acc[...] = product
        else:
            acc[...] += product

    pairs = []
    for i in range(4):
        put(term.at[i], make_term(i))
        pairs.append(go(remote(term.at[i], from_pair.at[i], ps.at[i], pr.at[i], node_peer[1])))
        if i == 0:
            arrived(4)
            weight(4, 2)
            local_grads()
        if i == 1:
            arrived(1)
            weight(1, 2)
            use_grads(1)
        if i == 2:
            use_grads(4)
        if i == 3:
            weight(4, 1)
            use_grads(2)
            use_keys(1, True)
    near = []
    for j in range(2):
        value = make_term(4 + j)
        pairs[j].wait_recv()
        put(to_near.at[j], plus(value, halves(from_pair.at[j])))
        near.append(go(remote(to_near.at[j], from_near.at[j], zs.at[j], zr.at[j], node_peer[2])))
        if j == 0:
            arrived(6)
            weight(6, 1)
            use_grads(6)
            use_keys(6)
        if j == 1:
            use_keys(2)
    put(total.at[0], make_term(6))
    use_keys(4)
    use_grads(3)
    use_keys(3)
    put(total.at[1], make_term(7))
    use_keys(0)
    pairs[2].wait_recv()
    near[0].wait_recv()
    put(
        to_far,
        plus(halves(total.at[0]), plus(halves(from_pair.at[2]), halves(from_near.at[0]))),
    )
    far = go(remote(to_far, from_far, zs.at[2], zr.at[2], node_peer[4]))
    pairs[3].wait_recv()
    near[1].wait_recv()
    put(
        total.at[1],
        plus(halves(total.at[1]), plus(halves(from_pair.at[3]), halves(from_near.at[1]))),
    )
    use_grads(5)
    use_keys(5)

    for copy in state:
        copy.wait()
    far.wait_recv()
    coded = total[1] + from_far[...].astype(f32)
    new_first = beta_first * first_in[...] + (1.0 - beta_first) * coded
    new_second = beta_second * second_in[...] + (1.0 - beta_second) * coded * coded
    first_out[...] = new_first
    second_out[...] = new_second
    first_hat = new_first / (1.0 - beta_first**adam_steps)
    second_hat = new_second / (1.0 - beta_second**adam_steps)
    ratio = first_hat / (jnp.sqrt(second_hat) + adam_eps)
    norm_root = math.sqrt(2 * key_width)
    rows = []
    for a in range(2):
        if a:
            mixed = ratio[:, :key_width] - ratio[:, key_width:]
        else:
            mixed = ratio[:, :key_width] + ratio[:, key_width:]
        turned = jnp.zeros_like(mixed)
        for _ in range(3):
            high = mixed.astype(bf16)
            mixed = mixed - high.astype(f32)
            turned = turned + jnp.dot(high, had[...], preferred_element_type=f32)
        rows.append(
            (turned * (1.0 / norm_root) * sign_row[a]).reshape(
                half // PAIR_GAP, 1, PAIR_GAP, key_width
            )
        )
    update = jnp.concatenate(rows, axis=1).reshape(columns, key_width)
    new_master = master_in[...] - learn_rate * (update + weight_decay * master_in[...])
    master_out[...] = new_master
    sec_out[rep] = new_master.astype(bf16)
    mine = sec_out.at[rep]
    spread_moves = {
        k: go(remote(mine, mine, ss.at[k - 1], sr.at[k - 1], rep_peer[k])) for k in (2, 1)
    }

    use_grads(7)
    use_keys(7)
    for i, k in enumerate((3, 1)):
        owner = flip(rep, k)
        part[i] = acc[pl.ds(pl.multiple_of(owner * tok_rows, tok_rows), tok_rows)].astype(bf16)
    part_move = go(remote(part, part_in, ks.at[0], kr.at[0], rep_peer[1]))
    part_move.wait_recv()
    away = flip(rep, 2)
    cross[...] = (
        acc[pl.ds(pl.multiple_of(away * tok_rows, tok_rows), tok_rows)] + part_in[0].astype(f32)
    ).astype(bf16)
    cross_move = go(remote(cross, cross_in, ks.at[1], kr.at[1], rep_peer[2]))

    def overlap(node):
        def add(k, running):
            index = node * reps + k
            value = grad_in[index].astype(f32) * gain[index] * x_in[index].astype(f32)
            for lane in range(0, columns, 128):
                running = running + value[:, lane : lane + 128]
            return running

        return add

    running = jnp.zeros((tok_rows, 128), f32)
    for bits, moves in grad_moves.items():
        for copy in moves:
            copy.wait_recv()
        running = lax.fori_loop(0, reps, overlap(flip(me, bits)), running)
    against = jnp.sum(running, axis=-1, keepdims=True) * (1.0 / (pieces * columns))
    one = inv[:, :1]
    factor = jnp.broadcast_to(one * one * one * against, (tok_rows, columns))

    def finish(i, carry):
        scaled = grad_in[i].astype(f32) * gain[i]
        grad_out[i] = (inv[...] * scaled - x_in[i].astype(f32) * factor).astype(bf16)
        return carry

    lax.fori_loop(0, pieces, finish, 0)

    spread_moves[2].wait_recv()
    across = sec_out.at[flip(rep, 2)]
    spread_moves[3] = go(remote(across, across, ss.at[2], sr.at[2], rep_peer[1]))
    cross_move.wait_recv()
    keys_out[...] = (
        acc[pl.ds(pl.multiple_of(rep * tok_rows, tok_rows), tok_rows)]
        + part_in[1].astype(f32)
        + cross_in[...].astype(f32)
    ).astype(keys_out.dtype)
    spread_moves[1].wait_recv()
    spread_moves[3].wait_recv()
    for copy in sent:
        copy.wait_send()


def store_kernel(keys, grad, master, first, second, sec, *refs):
    keys_out, grad_out, master_out, first_out, second_out, sec_out, sems = refs
    pieces, _, columns = grad.shape
    rows = sec.shape[1]
    moves = [
        pltpu.make_async_copy(grad.at[i], grad_out.at[:, pl.ds(columns * i, columns)], sems.at[i])
        for i in range(pieces)
    ]
    pairs = [(keys, keys_out), (master, master_out), (first, first_out), (second, second_out)]
    pairs += [(sec.at[i], sec_out.at[pl.ds(rows * i, rows)]) for i in range(sec.shape[0])]
    for i, (src, dst) in enumerate(pairs):
        moves.append(pltpu.make_async_copy(src, dst, sems.at[pieces + i]))
    for copy in moves:
        copy.start()
    for copy in moves:
        copy.wait()


def fused(nodes, reps, scale, tokens, gain, cot, sec, master, first, second, signs):
    dma = pltpu.SemaphoreType.DMA
    f32, bf16 = jnp.float32, jnp.bfloat16
    tok_rows, model_width = tokens.shape
    key_width = cot.shape[1]
    columns = master.shape[0]
    pieces = model_width // columns
    block = first.shape
    group_tokens = reps * tok_rows
    vmem = pltpu.VMEM
    far = functools.partial(pltpu.with_memory_space_constraint, memory_space=pltpu.HBM)
    results = pl.pallas_call(
        functools.partial(fused_kernel, nodes, reps, scale),
        out_shape=(
            vmem(cot.shape, bf16),
            vmem((pieces, tok_rows, columns), bf16),
            vmem(master.shape, f32),
            vmem(block, f32),
            vmem(block, f32),
            vmem((reps,) + master.shape, bf16),
        ),
        in_specs=[HBM, VMEM, HBM, HBM, HBM, HBM, HBM, VMEM],
        out_specs=(VMEM,) * 6,
        scratch_shapes=[
            vmem((pieces, tok_rows, columns), bf16),
            vmem((nodes, reps, tok_rows, columns), bf16),
            vmem((nodes, reps, tok_rows, columns), bf16),
            vmem((reps, tok_rows, key_width), bf16),
            vmem((nodes, columns, key_width), bf16),
            vmem(sec.shape, bf16),
            vmem((group_tokens, 2 * key_width), bf16),
            vmem((key_width, key_width), bf16),
            vmem((4,) + block, bf16),
            vmem((2,) + block, f32),
            vmem((4,) + block, bf16),
            vmem((2,) + block, bf16),
            vmem((2,) + block, bf16),
            vmem(block, bf16),
            vmem(block, bf16),
            vmem((nodes, reps, tok_rows, columns), bf16),
            vmem((pieces, tok_rows, columns), bf16),
            vmem((group_tokens, key_width), f32),
            vmem((tok_rows, columns), f32),
            vmem((2, tok_rows, key_width), bf16),
            vmem((2, tok_rows, key_width), bf16),
            vmem((tok_rows, key_width), bf16),
            vmem((tok_rows, key_width), bf16),
            vmem(master.shape, f32),
            vmem(block, f32),
            vmem(block, f32),
        ]
        + [dma((pieces,)), dma((5,))]
        + [dma((3,))] * 2
        + [dma((3, nodes))] * 2
        + [dma((nodes - 1,))] * 2
        + [dma((4,))] * 2
        + [dma((3,))] * 2
        + [dma((3, nodes))] * 2
        + [dma((2,))] * 2
        + [dma((3,))] * 2,
        compiler_params=pltpu.CompilerParams(
            collective_id=2, has_side_effects=True, vmem_limit_bytes=56 << 20
        ),
    )(
        far(tokens), gain.reshape(pieces, 1, columns), far(cot), far(sec), far(master),
        far(first), far(second), signs.reshape(-1, 128),
    )
    held = [pltpu.with_memory_space_constraint(value, pltpu.VMEM) for value in results]
    like = jax.ShapeDtypeStruct
    return pl.pallas_call(
        store_kernel,
        out_shape=(
            like(cot.shape, bf16),
            like(tokens.shape, bf16),
            like(master.shape, f32),
            like(block, f32),
            like(block, f32),
            like(sec.shape, bf16),
        ),
        in_specs=[VMEM] * 6,
        out_specs=(ANY,) * 6,
        scratch_shapes=[dma((pieces + 4 + reps,))],
        compiler_params=pltpu.CompilerParams(vmem_limit_bytes=1 << 20),
    )(*held)


def shards(tokens, norm_gain, key_cotangent, secondary, master, moment_first, moment_second, signs):
    tok_rows, model_width = tokens.shape
    key_width = key_cotangent.shape[1]
    nodes = lax.axis_size("node")
    reps = lax.axis_size("rep")
    all_tokens = tok_rows * nodes * reps
    master_rows = master.shape[0]
    rot_scale = 1.0 / (math.sqrt(2 * key_width) * all_tokens)
    aligned = master_rows % 128 == 0
    if aligned and (nodes, reps) == (8, 4):
        return fused(
            nodes, reps, rot_scale, tokens, norm_gain, key_cotangent, secondary, master,
            moment_first, moment_second, signs,
        )
    had_table = sylvester(key_width)
    sign_rows = (1 - 2 * signs).astype(jnp.float32).reshape(2, key_width)
    floats = tokens.astype(jnp.float32)
    inverse = lax.rsqrt(jnp.mean(floats * floats, axis=-1, keepdims=True) + norm_eps)
    normed = floats * inverse
    hidden = (normed * norm_gain).astype(jnp.bfloat16)
    if not aligned:
        hidden = hidden.reshape(tok_rows, nodes * reps, master_rows).transpose(1, 0, 2)
    coded, keys, hidden_grad = step(
        nodes, reps, aligned, rot_scale, hidden, key_cotangent, secondary,
        sign_rows,
    )
    if not aligned:
        hidden_grad = hidden_grad.transpose(1, 0, 2).reshape(tok_rows, model_width)
    hidden_grad = hidden_grad.astype(jnp.float32)
    new_first = beta_first * moment_first + (1.0 - beta_first) * coded
    new_second = beta_second * moment_second + (1.0 - beta_second) * coded * coded
    first_hat = new_first / (1.0 - beta_first**adam_steps)
    second_hat = new_second / (1.0 - beta_second**adam_steps)
    ratio = first_hat / (jnp.sqrt(second_hat) + adam_eps)
    lower = ratio[:, :key_width]
    upper = ratio[:, key_width:]
    norm_root = math.sqrt(2 * key_width)
    row_even = (
        jnp.dot(lower + upper, had_table, precision=lax.Precision.HIGHEST)
        / norm_root
        * sign_rows[0]
    )
    row_odd = (
        jnp.dot(lower - upper, had_table, precision=lax.Precision.HIGHEST)
        / norm_root
        * sign_rows[1]
    )
    groups = master_rows // (2 * PAIR_GAP)
    update = jnp.stack(
        [
            row_even.reshape(groups, PAIR_GAP, key_width),
            row_odd.reshape(groups, PAIR_GAP, key_width),
        ],
        axis=1,
    ).reshape(master_rows, key_width)
    new_master = master - learn_rate * (update + weight_decay * master)
    new_secondary = spread(reps, new_master.astype(jnp.bfloat16)).reshape(
        reps * master_rows, key_width
    )
    scaled = hidden_grad * norm_gain
    token_grad = (
        inverse * (scaled - normed * jnp.mean(scaled * normed, axis=-1, keepdims=True))
    ).astype(jnp.bfloat16)
    return (keys, token_grad, new_master, new_first, new_second, new_secondary)


def solution(mesh):
    return jax.shard_map(
        shards,
        mesh=mesh,
        in_specs=(
            P(("node", "rep"), None),
            P(),
            P(("node", "rep"), None),
            P("node", None),
            P(("node", "rep"), None),
            P(("node", "rep"), None),
            P(("node", "rep"), None),
            P(),
        ),
        out_specs=(
            P(("node", "rep"), None),
            P(("node", "rep"), None),
            P(("node", "rep"), None),
            P(("node", "rep"), None),
            P(("node", "rep"), None),
            P("node", None),
        ),
        check_vma=False,
    )
```

```python
import functools
import math

import jax
import jax.numpy as jnp
from jax import lax
from jax.experimental import pallas as pl
from jax.experimental.pallas import tpu as pltpu
from jax.sharding import PartitionSpec as P

PAIR_GAP = 16
MESH = pl.DeviceIdType.MESH

norm_eps = 1e-05
adam_eps = 1e-08
beta_first = 0.9
beta_second = 0.95
adam_steps = 10
learn_rate = 0.002
weight_decay = 0.1

ANY = pl.BlockSpec(memory_space=pl.ANY)
HBM = pl.BlockSpec(memory_space=pltpu.HBM)
VMEM = pl.BlockSpec(memory_space=pltpu.VMEM)


def sylvester(extent):
    position = jnp.arange(extent, dtype=jnp.int32)
    parity = jnp.zeros((extent, extent), jnp.int32)
    for bit_place in range(extent.bit_length() - 1):
        parity = parity + (position[:, None] >> bit_place & 1) * (
            position[None, :] >> bit_place & 1
        )
    return (1 - 2 * (parity % 2)).astype(jnp.float32)


def split(index):
    return index // 2, lax.rem(index, 2)


def greet(peers):
    barrier = pltpu.get_barrier_semaphore()
    for peer in peers:
        pl.semaphore_signal(barrier, inc=1, device_id=peer, device_id_type=MESH)
    pl.semaphore_wait(barrier, len(peers))


def remote(src, dst, send, recv, peer):
    return pltpu.make_async_remote_copy(
        src_ref=src,
        dst_ref=dst,
        send_sem=send,
        recv_sem=recv,
        device_id=peer,
        device_id_type=MESH,
    )


def axis_peers(axis, size):
    me = lax.axis_index(axis)
    return [{axis: lax.rem(me + k, size)} for k in range(1, size)]


def pair_peers(axis, size):
    high, low = split(lax.axis_index(axis))
    half = size // 2
    partner = {axis: high * 2 + 1 - low}
    same = [{axis: lax.rem(high + k, half) * 2 + low} for k in range(1, half)]
    return partner, same


class PairGather:
    def __init__(self, axis, size, src, out, local_sem, send, recv):
        self.half = size // 2
        me = lax.axis_index(axis)
        high, low = split(me)
        partner, same = pair_peers(axis, size)
        self.local = pltpu.make_async_copy(src, out.at[me], local_sem)
        self.first = [
            remote(src, out.at[me], send.at[0, k], recv.at[0, k], same[k - 1])
            for k in range(1, self.half)
        ]
        self.second = [remote(src, out.at[me], send.at[1, 0], recv.at[1, 0], partner)]
        for k in range(1, self.half):
            origin = lax.rem(high + self.half - k, self.half) * 2 + low
            self.second.append(
                remote(out.at[origin], out.at[origin], send.at[1, k], recv.at[1, k], partner)
            )

    def start(self):
        for copy in self.first:
            copy.start()
        self.second[0].start()
        self.local.start()

    def forward(self, k):
        self.first[k - 1].wait_recv()
        self.second[k].start()

    def finish(self):
        for copy in self.second:
            copy.wait_recv()
        for copy in self.first + self.second:
            copy.wait_send()
        self.local.wait()


def step_kernel(
    nodes, reps, aligned, scale, hid, cot, sec, table, coded, keys, grad_out,
    hid_in, cot_in, sec_in, rot, term, grad, acc, part,
    from_pair, to_same, from_same, key_in,
    cs, cr, hs, hr, ss, sr, ps, pr, zs, zr, gs, gr, ks, kr, cot_own, hid_own, sec_own, grad_own,
):
    f32 = jnp.float32
    rep = lax.axis_index("rep")
    high, low = split(lax.axis_index("node"))
    half = nodes // 2
    partner, same = pair_peers("node", nodes)
    rep_peers = axis_peers("rep", reps)
    columns, key_width = sec_in.shape[1:]
    tok_rows = cot_in.shape[1]
    group_tokens = reps * tok_rows

    def piece(ref, node, owner):
        index = node * reps + owner
        if aligned:
            return ref.at[:, pl.ds(pl.multiple_of(index * columns, columns), columns)]
        return ref.at[index]

    greet(rep_peers + [partner] + same)
    weights = PairGather(
        "node", nodes, sec.at[pl.ds(pl.multiple_of(rep * columns, columns), columns)], sec_in,
        sec_own.at[0], ss, sr,
    )
    weights.start()
    cot_moves = [
        remote(cot, cot_in.at[rep], cs.at[k], cr.at[k], peer) for k, peer in enumerate(rep_peers)
    ]
    cot_moves.append(pltpu.make_async_copy(cot, cot_in.at[rep], cot_own.at[0]))
    for copy in cot_moves:
        copy.start()
    turns = list(range(1, half)) + [0]
    order = [lax.rem(high + k, half) * 2 + 1 - low for k in turns]
    order += [lax.rem(high + k, half) * 2 + low for k in turns]
    hid_moves = []
    for i, node in enumerate(order):
        moves = [
            remote(
                piece(hid, node, peer["rep"]), hid_in.at[node, rep], hs.at[k, i], hr.at[k, i], peer
            )
            for k, peer in enumerate(rep_peers)
        ]
        moves.append(
            pltpu.make_async_copy(piece(hid, node, rep), hid_in.at[node, rep], hid_own.at[i])
        )
        for copy in moves:
            copy.start()
        hid_moves.append(moves)

    for copy in cot_moves:
        copy.wait()
    group_cot = cot_in[...].reshape(group_tokens, key_width)
    shape = (key_width, key_width)
    parity = lax.broadcasted_iota(jnp.int32, shape, 0) & lax.broadcasted_iota(jnp.int32, shape, 1)
    for shift in (8, 4, 2, 1):
        parity = parity ^ (parity >> shift)
    had = (1 - 2 * (parity & 1)).astype(f32).astype(rot.dtype)
    for a in range(2):
        flipped = (group_cot.astype(f32) * table[a : a + 1, :]).astype(rot.dtype)
        rot[:, a * key_width : (a + 1) * key_width] = (
            jnp.dot(flipped, had, preferred_element_type=f32) * scale
        ).astype(rot.dtype)
    acc[...] = jnp.zeros_like(acc)

    def make_term(i):
        for copy in hid_moves[i]:
            copy.wait()
        chunk = hid_in[order[i]].reshape(group_tokens, columns)
        product = lax.dot_general(
            chunk, rot[...], (((0,), (0,)), ((), ())), preferred_element_type=f32
        ).reshape(columns // (2 * PAIR_GAP), 2, PAIR_GAP, 2 * key_width)
        first = product[:, 0, :, :key_width].reshape(columns // 2, key_width)
        second = product[:, 1, :, key_width:].reshape(columns // 2, key_width)
        term[i, :, :key_width] = (first + second).astype(term.dtype)
        term[i, :, key_width:] = (first - second).astype(term.dtype)

    swaps = []
    stays = []

    def use_weights(count, node):
        block = sec_in[node]
        rows = lax.dot_general(
            cot_in[...].reshape(group_tokens, key_width), block, (((1,), (1,)), ((), ())),
            preferred_element_type=f32,
        )
        grad[node] = rows.astype(grad.dtype).reshape(reps, tok_rows, columns)
        for k, peer in enumerate(rep_peers):
            copy = remote(
                grad.at[node, peer["rep"]], piece(grad_out, node, rep),
                gs.at[k, count], gr.at[k, count], peer,
            )
            copy.start()
            swaps.append(copy)
        copy = pltpu.make_async_copy(
            grad.at[node, rep], piece(grad_out, node, rep), grad_own.at[count]
        )
        copy.start()
        stays.append(copy)
        chunk = hid_in[node].reshape(group_tokens, columns)
        acc[...] += jnp.dot(chunk, block, preferred_element_type=f32)

    pairs = []
    for i in range(half):
        make_term(i)
        pairs.append(remote(term.at[i], from_pair.at[i], ps.at[i], pr.at[i], partner))
        pairs[-1].start()
        if i:
            weights.forward(i)
    weights.local.wait()
    onward = []
    for j, k in enumerate(turns):
        make_term(half + j)
        pairs[j].wait_recv()
        total = term[half + j].astype(f32) + from_pair[j].astype(f32)
        if k:
            to_same[j] = total.astype(to_same.dtype)
            onward.append(remote(to_same.at[j], from_same.at[j], zs.at[j], zr.at[j], same[k - 1]))
            onward[-1].start()
        else:
            coded[...] = total
        use_weights(j, order[half + j])
    for j in range(half):
        weights.second[j].wait_recv()
        use_weights(half + j, lax.rem(high + half - j, half) * 2 + 1 - low)
    part[...] = acc[...].astype(part.dtype).reshape(part.shape)
    key_moves = [
        remote(part.at[peer["rep"]], key_in.at[k], ks.at[k], kr.at[k], peer)
        for k, peer in enumerate(rep_peers)
    ]
    for copy in key_moves:
        copy.start()
    for j, copy in enumerate(onward):
        copy.wait_recv()
        coded[...] += from_same[j].astype(f32)
    total = part[rep].astype(f32)
    for k, copy in enumerate(key_moves):
        copy.wait_recv()
        total = total + key_in[k].astype(f32)
    keys[...] = total.astype(keys.dtype)
    for copy in swaps:
        copy.wait()
    for copy in stays:
        copy.wait()
    for copy in weights.first + weights.second + pairs + onward + key_moves:
        copy.wait_send()


def step(nodes, reps, aligned, scale, hid, cot, sec, table):
    dma = pltpu.SemaphoreType.DMA
    half = nodes // 2
    columns = sec.shape[0] // reps
    tok_rows, key_width = cot.shape
    group_tokens = reps * tok_rows
    block = (columns // 2, 2 * key_width)
    bf16 = jnp.bfloat16
    return pl.pallas_call(
        functools.partial(step_kernel, nodes, reps, aligned, scale),
        out_shape=(
            jax.ShapeDtypeStruct(block, jnp.float32),
            jax.ShapeDtypeStruct(cot.shape, bf16),
            jax.ShapeDtypeStruct(hid.shape, bf16),
        ),
        in_specs=[ANY, ANY, ANY, VMEM],
        out_specs=(VMEM,) * 3,
        scratch_shapes=[
            pltpu.VMEM((nodes, reps, tok_rows, columns), bf16),
            pltpu.VMEM((reps, tok_rows, key_width), bf16),
            pltpu.VMEM((nodes, columns, key_width), bf16),
            pltpu.VMEM((group_tokens, 2 * key_width), bf16),
            pltpu.VMEM((nodes,) + block, bf16),
            pltpu.VMEM((nodes, reps, tok_rows, columns), bf16),
            pltpu.VMEM((group_tokens, key_width), jnp.float32),
            pltpu.VMEM((reps, tok_rows, key_width), bf16),
            pltpu.VMEM((half,) + block, bf16),
            pltpu.VMEM((half - 1,) + block, bf16),
            pltpu.VMEM((half - 1,) + block, bf16),
            pltpu.VMEM((reps - 1, tok_rows, key_width), bf16),
        ]
        + [dma((reps - 1,))] * 2
        + [dma((reps - 1, nodes))] * 2
        + [dma((2, half))] * 2
        + [dma((half,))] * 2
        + [dma((half - 1,))] * 2
        + [dma((reps - 1, nodes))] * 2
        + [dma((reps - 1,))] * 2
        + [dma((1,)), dma((nodes,)), dma((1,)), dma((nodes,))],
        compiler_params=pltpu.CompilerParams(collective_id=0, has_side_effects=True),
    )(hid, cot, sec, table)


def spread_kernel(reps, src, out, send, recv, local):
    partner, same = pair_peers("rep", reps)
    greet([partner] + same)
    rows = PairGather("rep", reps, src, out, local.at[0], send, recv)
    rows.start()
    for k in range(1, reps // 2):
        rows.forward(k)
    rows.finish()


def spread(reps, rows):
    dma = pltpu.SemaphoreType.DMA
    return pl.pallas_call(
        functools.partial(spread_kernel, reps),
        out_shape=jax.ShapeDtypeStruct((reps,) + rows.shape, rows.dtype),
        in_specs=[VMEM],
        out_specs=VMEM,
        scratch_shapes=[dma((2, reps // 2))] * 2 + [dma((1,))],
        compiler_params=pltpu.CompilerParams(collective_id=1, has_side_effects=True),
    )(rows)


def flip(index, bits):
    for bit in (1, 2, 4):
        if bits & bit:
            index = index + bit * (1 - 2 * lax.rem(lax.div(index, bit), 2))
    return index


def fused_kernel(
    nodes, reps, scale,
    tok, gain, cot, sec, master, first, second, signs,
    keys_out, grad_out, master_out, first_out, second_out, sec_out,
    x_in, hid, hid_in, cot_in, sec_in, sec_own, rot, had, term, total, from_pair,
    to_near, from_near, to_far, from_far, grad, grad_in, acc, inv,
    part, part_in, cross, cross_in, master_in, first_in, second_in, ext,
    xl, ll, cs, cr, hs, hr, ws, wr, ps, pr, zs, zr, gs, gr, ks, kr, ss, sr, es, er,
):
    f32, bf16 = jnp.float32, jnp.bfloat16
    rep = lax.axis_index("rep")
    me = lax.axis_index("node")
    pieces, tok_rows, columns = x_in.shape
    key_width = cot_in.shape[2]
    group_tokens = reps * tok_rows
    half = columns // 2
    rep_kinds = (2, 3, 1)
    rep_peer = {k: {"rep": flip(rep, k)} for k in rep_kinds}
    node_peer = {k: {"node": flip(me, k)} for k in (1, 2, 4)}

    loads = [
        pltpu.make_async_copy(tok.at[:, pl.ds(columns * i, columns)], x_in.at[i], xl.at[i])
        for i in range(pieces)
    ]
    own_cot = pltpu.make_async_copy(cot, cot_in.at[rep], ll.at[0])
    own_sec = pltpu.make_async_copy(sec, sec_own, ll.at[1])
    state = [
        pltpu.make_async_copy(master, master_in, ll.at[2]),
        pltpu.make_async_copy(first, first_in, ll.at[3]),
        pltpu.make_async_copy(second, second_in, ll.at[4]),
    ]
    for copy in loads + [own_cot, own_sec] + state:
        copy.start()
    greet([rep_peer[k] for k in rep_kinds] + [node_peer[k] for k in (1, 2, 4)])

    sent = []

    def go(copy):
        copy.start()
        sent.append(copy)
        return copy

    quarter = sec.at[pl.ds(pl.multiple_of(rep * columns, columns), columns)]
    slots = {}

    def weight(source, via):
        slot = len(slots)
        src = sec_in.at[flip(me, source)] if source else quarter
        copy = remote(src, sec_in.at[flip(me, source)], ws.at[slot], wr.at[slot], node_peer[via])
        slots[source ^ via] = go(copy)

    held = set()

    def arrived(bits):
        if bits not in held:
            held.add(bits)
            slots[bits].wait_recv()

    weight(0, 4)
    weight(0, 1)
    weight(0, 2)
    cot_moves = {
        2: go(remote(cot, cot_in.at[rep], cs.at[0], cr.at[0], rep_peer[2])),
        1: go(remote(cot, cot_in.at[rep], cs.at[1], cr.at[1], rep_peer[1])),
    }

    for copy in loads:
        copy.wait()

    def squares(i, running):
        x = x_in[i].astype(f32)
        x = x * x
        for lane in range(0, columns, 128):
            running = running + x[:, lane : lane + 128]
        return running

    squared = lax.fori_loop(0, pieces, squares, jnp.zeros((tok_rows, 128), f32))
    mean = jnp.sum(squared, axis=-1, keepdims=True) * (1.0 / (pieces * columns))
    inv[...] = jnp.broadcast_to(lax.rsqrt(mean + norm_eps), inv.shape)

    order = [7, 6, 3, 2, 5, 4, 1, 0]
    place = {bits: i for i, bits in enumerate(order)}
    hid_moves = []
    for i, bits in enumerate(order):
        node = flip(me, bits)
        moves = []
        for k in rep_kinds + (0,):
            owner = flip(rep, k)
            index = node * reps + owner
            value = (x_in[index].astype(f32) * inv[...] * gain[index]).astype(bf16)
            if k:
                hid[node, owner] = value
                moves.append(
                    go(
                        remote(
                            hid.at[node, owner], hid_in.at[node, rep],
                            hs.at[k - 1, i], hr.at[k - 1, i], rep_peer[k],
                        )
                    )
                )
            else:
                hid_in[node, rep] = value
        hid_moves.append(moves)

    shape = (key_width, key_width)
    parity = lax.broadcasted_iota(jnp.int32, shape, 0) & lax.broadcasted_iota(jnp.int32, shape, 1)
    for shift in (8, 4, 2, 1):
        parity = parity ^ (parity >> shift)
    had[...] = (1 - 2 * (parity & 1)).astype(f32).astype(bf16)
    chunks = key_width // 128
    sign_row = []
    for a in range(2):
        bits = [signs[a * chunks + c : a * chunks + c + 1, :] for c in range(chunks)]
        sign_row.append((1 - 2 * jnp.concatenate(bits, axis=1)).astype(f32))

    cot_moves[2].wait_recv()
    across = cot_in.at[flip(rep, 2)]
    cot_moves[3] = go(remote(across, across, cs.at[2], cr.at[2], rep_peer[1]))
    own_cot.wait()
    cot_moves[1].wait_recv()
    cot_moves[3].wait_recv()
    for a in range(2):
        flipped = (cot_in[...].reshape(group_tokens, key_width).astype(f32) * sign_row[a]).astype(bf16)
        rot[:, a * key_width : (a + 1) * key_width] = (
            jnp.dot(flipped, had[...], preferred_element_type=f32) * scale
        ).astype(bf16)

    def make_term(bits):
        for copy in hid_moves[place[bits]]:
            copy.wait_recv()
        chunk = hid_in[flip(me, bits)].reshape(group_tokens, columns)
        product = lax.dot_general(
            chunk, rot[...], (((0,), (0,)), ((), ())), preferred_element_type=f32
        ).reshape(columns // (2 * PAIR_GAP), 2, PAIR_GAP, 2 * key_width)
        upper = product[:, 0, :, :key_width].reshape(half, key_width)
        lower = product[:, 1, :, key_width:].reshape(half, key_width)
        return upper + lower, upper - lower

    def add_up(dst, *parts):
        value = parts[0].astype(f32)
        for other in parts[1:]:
            value = value + other.astype(f32)
        dst[...] = value.astype(dst.dtype)

    grad_moves = {}

    def local_grads():
        own_sec.wait()
        for k in range(reps):
            block = sec_own[pl.ds(k * columns, columns)]
            grad_in[me * reps + k] = lax.dot_general(
                cot_in[rep], block, (((1,), (1,)), ((), ())), preferred_element_type=f32
            ).astype(bf16)
        grad_moves[0] = []

    def use_grads(bits):
        arrived(bits)
        node = flip(me, bits)
        rows = lax.dot_general(
            cot_in[...].reshape(group_tokens, key_width), sec_in[node], (((1,), (1,)), ((), ())),
            preferred_element_type=f32,
        )
        grad[node] = rows.astype(bf16).reshape(reps, tok_rows, columns)
        slot = len(grad_moves)
        grad_moves[bits] = [
            go(
                remote(
                    grad.at[node, flip(rep, k)], grad_in.at[node * reps + rep],
                    gs.at[k - 1, slot], gr.at[k - 1, slot], rep_peer[k],
                )
            )
            for k in rep_kinds
        ]
        grad_in[node * reps + rep] = grad[node, rep]

    def use_keys(bits, start=False):
        node = flip(me, bits)
        block = sec_in[node] if bits else sec_own[pl.ds(pl.multiple_of(rep * columns, columns), columns)]
        product = jnp.dot(
            hid_in[node].reshape(group_tokens, columns), block, preferred_element_type=f32
        )
        if start:
            acc[...] = product
        else:
            acc[...] += product

    near_nodes = (2,)
    extra = {}

    def fetch(e):
        other = sec.at[pl.ds(pl.multiple_of(flip(rep, 2) * columns, columns), columns)]
        bits = near_nodes[e]
        extra[e] = [go(remote(other, ext.at[e, 2], es.at[e, 2], er.at[e, 2], node_peer[bits]))]

    def pass_on(e):
        node = flip(me, near_nodes[e])
        arrived(near_nodes[e])
        extra[e][0].wait_recv()
        for k, src in ((1, sec_in.at[node]), (3, ext.at[e, 2])):
            extra[e].append(go(remote(src, ext.at[e, k], es.at[e, k], er.at[e, k], rep_peer[1])))

    def extra_grads(e):
        node = flip(me, near_nodes[e])
        for copy in extra[e][1:]:
            copy.wait_recv()
        for k in range(4):
            block = ext[e, k] if k else sec_in[node]
            grad_in[node * reps + flip(rep, k)] = lax.dot_general(
                cot_in[rep], block, (((1,), (1,)), ((), ())), preferred_element_type=f32
            ).astype(bf16)
        grad_moves[near_nodes[e]] = []

    pair_moves, near_moves, far_moves = {}, {}, {}

    def to_pair(i, bits):
        upper, lower = make_term(bits)
        rows = upper.shape[0] // 2
        for h in range(2):
            term[i, h, :, :key_width] = upper[h * rows : (h + 1) * rows].astype(bf16)
            term[i, h, :, key_width:] = lower[h * rows : (h + 1) * rows].astype(bf16)
            pair_moves[i, h] = go(
                remote(term.at[i, h], from_pair.at[i, h], ps.at[i, h], pr.at[i, h], node_peer[1])
            )

    def keep(i, bits):
        upper, lower = make_term(bits)
        total[i, :, :key_width] = upper
        total[i, :, key_width:] = lower

    def mine(i, h):
        rows = total.shape[1] // 2
        return total[i, h * rows : (h + 1) * rows]

    def to_neighbour(i, h):
        pair_moves[i, h].wait_recv()
        add_up(to_near.at[i, h], mine(i, h), from_pair[i, h])
        near_moves[i, h] = go(
            remote(to_near.at[i, h], from_near.at[i, h], zs.at[i, h], zr.at[i, h], node_peer[2])
        )

    def to_distant(h):
        pair_moves[2, h].wait_recv()
        near_moves[0, h].wait_recv()
        add_up(to_far.at[h], mine(2, h), from_pair[2, h], from_near[0, h])
        far_moves[h] = go(remote(to_far.at[h], from_far.at[h], zs.at[2, h], zr.at[2, h], node_peer[4]))

    spread_moves = {}
    norm_root = math.sqrt(2 * key_width)
    master_half = columns // 2

    def spread_block(owner, h):
        return sec_out.at[owner, pl.ds(h * master_half, master_half)]

    def finalize(h):
        pair_moves[3, h].wait_recv()
        near_moves[1, h].wait_recv()
        coded = mine(3, h) + from_pair[3, h].astype(f32) + from_near[1, h].astype(f32)
        far_moves[h].wait_recv()
        coded = coded + from_far[h].astype(f32)
        here = pl.ds(h * (half // 2), half // 2)
        new_first = beta_first * first_in[here] + (1.0 - beta_first) * coded
        new_second = beta_second * second_in[here] + (1.0 - beta_second) * coded * coded
        first_out[here] = new_first
        second_out[here] = new_second
        first_hat = new_first / (1.0 - beta_first**adam_steps)
        second_hat = new_second / (1.0 - beta_second**adam_steps)
        ratio = first_hat / (jnp.sqrt(second_hat) + adam_eps)
        rows = []
        for a in range(2):
            if a:
                mixed = ratio[:, :key_width] - ratio[:, key_width:]
            else:
                mixed = ratio[:, :key_width] + ratio[:, key_width:]
            turned = jnp.zeros_like(mixed)
            for _ in range(3):
                high = mixed.astype(bf16)
                mixed = mixed - high.astype(f32)
                turned = turned + jnp.dot(high, had[...], preferred_element_type=f32)
            rows.append(
                (turned * (1.0 / norm_root) * sign_row[a]).reshape(
                    half // (2 * PAIR_GAP), 1, PAIR_GAP, key_width
                )
            )
        update = jnp.concatenate(rows, axis=1).reshape(master_half, key_width)
        there = pl.ds(h * master_half, master_half)
        old = master_in[there]
        new_master = old - learn_rate * (update + weight_decay * old)
        master_out[there] = new_master
        sec_out[rep, there] = new_master.astype(bf16)
        src = spread_block(rep, h)
        for k in (2, 1):
            spread_moves[k, h] = go(
                remote(src, src, ss.at[k - 1, h], sr.at[k - 1, h], rep_peer[k])
            )

    def spread_on(h):
        spread_moves[2, h].wait_recv()
        src = spread_block(flip(rep, 2), h)
        spread_moves[3, h] = go(remote(src, src, ss.at[2, h], sr.at[2, h], rep_peer[1]))

    to_pair(0, 7)
    local_grads()
    arrived(4)
    weight(4, 2)
    keep(0, 6)
    use_grads(1)
    to_neighbour(0, 0)
    to_pair(1, 3)
    to_neighbour(0, 1)
    use_grads(4)
    keep(1, 2)
    to_neighbour(1, 0)
    to_pair(2, 5)
    to_neighbour(1, 1)
    keep(2, 4)
    use_keys(4, True)
    arrived(2)
    use_keys(2)
    to_distant(0)
    to_pair(3, 1)
    weight(4, 1)
    use_keys(1)
    to_distant(1)
    weight(1, 2)
    use_grads(6)
    use_keys(6)
    weight(6, 1)
    fetch(0)
    keep(3, 0)
    use_keys(0)
    for copy in state:
        copy.wait()
    finalize(0)
    finalize(1)
    use_grads(5)
    use_keys(5)
    use_grads(3)
    use_keys(3)
    spread_on(0)
    use_grads(7)
    use_keys(7)
    for i, k in enumerate((3, 1)):
        owner = flip(rep, k)
        part[i] = acc[pl.ds(pl.multiple_of(owner * tok_rows, tok_rows), tok_rows)].astype(bf16)
    part_move = go(remote(part, part_in, ks.at[0], kr.at[0], rep_peer[1]))
    part_move.wait_recv()
    away = flip(rep, 2)
    cross[...] = (
        acc[pl.ds(pl.multiple_of(away * tok_rows, tok_rows), tok_rows)] + part_in[0].astype(f32)
    ).astype(bf16)
    cross_move = go(remote(cross, cross_in, ks.at[1], kr.at[1], rep_peer[2]))
    spread_on(1)
    pass_on(0)
    extra_grads(0)

    def overlap(node):
        def add(k, running):
            index = node * reps + k
            value = grad_in[index].astype(f32) * gain[index] * x_in[index].astype(f32)
            for lane in range(0, columns, 128):
                running = running + value[:, lane : lane + 128]
            return running

        return add

    running = jnp.zeros((tok_rows, 128), f32)
    for bits, moves in grad_moves.items():
        for copy in moves:
            copy.wait_recv()
        running = lax.fori_loop(0, reps, overlap(flip(me, bits)), running)
    against = jnp.sum(running, axis=-1, keepdims=True) * (1.0 / (pieces * columns))
    one = inv[:, :1]
    factor = jnp.broadcast_to(one * one * one * against, (tok_rows, columns))

    def finish(i, carry):
        scaled = grad_in[i].astype(f32) * gain[i]
        grad_out[i] = (inv[...] * scaled - x_in[i].astype(f32) * factor).astype(bf16)
        return carry

    lax.fori_loop(0, pieces, finish, 0)

    cross_move.wait_recv()
    keys_out[...] = (
        acc[pl.ds(pl.multiple_of(rep * tok_rows, tok_rows), tok_rows)]
        + part_in[1].astype(f32)
        + cross_in[...].astype(f32)
    ).astype(keys_out.dtype)
    for k in (1, 3):
        for h in range(2):
            spread_moves[k, h].wait_recv()
    for copy in sent:
        copy.wait_send()


def store_kernel(keys, grad, master, first, second, sec, *refs):
    keys_out, grad_out, master_out, first_out, second_out, sec_out, sems = refs
    pieces, _, columns = grad.shape
    rows = sec.shape[1]
    moves = [
        pltpu.make_async_copy(grad.at[i], grad_out.at[:, pl.ds(columns * i, columns)], sems.at[i])
        for i in range(pieces)
    ]
    pairs = [(keys, keys_out), (master, master_out), (first, first_out), (second, second_out)]
    pairs += [(sec.at[i], sec_out.at[pl.ds(rows * i, rows)]) for i in range(sec.shape[0])]
    for i, (src, dst) in enumerate(pairs):
        moves.append(pltpu.make_async_copy(src, dst, sems.at[pieces + i]))
    for copy in moves:
        copy.start()
    for copy in moves:
        copy.wait()


def fused(nodes, reps, scale, tokens, gain, cot, sec, master, first, second, signs):
    dma = pltpu.SemaphoreType.DMA
    f32, bf16 = jnp.float32, jnp.bfloat16
    tok_rows, model_width = tokens.shape
    key_width = cot.shape[1]
    columns = master.shape[0]
    pieces = model_width // columns
    block = first.shape
    part = (block[0] // 2, block[1])
    group_tokens = reps * tok_rows
    vmem = pltpu.VMEM
    far = functools.partial(pltpu.with_memory_space_constraint, memory_space=pltpu.HBM)
    results = pl.pallas_call(
        functools.partial(fused_kernel, nodes, reps, scale),
        out_shape=(
            vmem(cot.shape, bf16),
            vmem((pieces, tok_rows, columns), bf16),
            vmem(master.shape, f32),
            vmem(block, f32),
            vmem(block, f32),
            vmem((reps,) + master.shape, bf16),
        ),
        in_specs=[HBM, VMEM, HBM, HBM, HBM, HBM, HBM, VMEM],
        out_specs=(VMEM,) * 6,
        scratch_shapes=[
            vmem((pieces, tok_rows, columns), bf16),
            vmem((nodes, reps, tok_rows, columns), bf16),
            vmem((nodes, reps, tok_rows, columns), bf16),
            vmem((reps, tok_rows, key_width), bf16),
            vmem((nodes, columns, key_width), bf16),
            vmem(sec.shape, bf16),
            vmem((group_tokens, 2 * key_width), bf16),
            vmem((key_width, key_width), bf16),
            vmem((4, 2) + part, bf16),
            vmem((4,) + block, f32),
            vmem((4, 2) + part, bf16),
            vmem((2, 2) + part, bf16),
            vmem((2, 2) + part, bf16),
            vmem((2,) + part, bf16),
            vmem((2,) + part, bf16),
            vmem((nodes, reps, tok_rows, columns), bf16),
            vmem((pieces, tok_rows, columns), bf16),
            vmem((group_tokens, key_width), f32),
            vmem((tok_rows, columns), f32),
            vmem((2, tok_rows, key_width), bf16),
            vmem((2, tok_rows, key_width), bf16),
            vmem((tok_rows, key_width), bf16),
            vmem((tok_rows, key_width), bf16),
            vmem(master.shape, f32),
            vmem(block, f32),
            vmem(block, f32),
            vmem((2, 4, columns, key_width), bf16),
        ]
        + [dma((pieces,)), dma((5,))]
        + [dma((3,))] * 2
        + [dma((3, nodes))] * 2
        + [dma((nodes - 1,))] * 2
        + [dma((4, 2))] * 2
        + [dma((3, 2))] * 2
        + [dma((3, nodes))] * 2
        + [dma((2,))] * 2
        + [dma((3, 2))] * 2
        + [dma((2, 4))] * 2,
        compiler_params=pltpu.CompilerParams(
            collective_id=2, has_side_effects=True, vmem_limit_bytes=56 << 20
        ),
    )(
        far(tokens), gain.reshape(pieces, 1, columns), far(cot), far(sec), far(master),
        far(first), far(second), signs.reshape(-1, 128),
    )
    held = [pltpu.with_memory_space_constraint(value, pltpu.VMEM) for value in results]
    like = jax.ShapeDtypeStruct
    return pl.pallas_call(
        store_kernel,
        out_shape=(
            like(cot.shape, bf16),
            like(tokens.shape, bf16),
            like(master.shape, f32),
            like(block, f32),
            like(block, f32),
            like(sec.shape, bf16),
        ),
        in_specs=[VMEM] * 6,
        out_specs=(ANY,) * 6,
        scratch_shapes=[dma((pieces + 4 + reps,))],
        compiler_params=pltpu.CompilerParams(vmem_limit_bytes=1 << 20),
    )(*held)


def shards(tokens, norm_gain, key_cotangent, secondary, master, moment_first, moment_second, signs):
    tok_rows, model_width = tokens.shape
    key_width = key_cotangent.shape[1]
    nodes = lax.axis_size("node")
    reps = lax.axis_size("rep")
    all_tokens = tok_rows * nodes * reps
    master_rows = master.shape[0]
    rot_scale = 1.0 / (math.sqrt(2 * key_width) * all_tokens)
    aligned = master_rows % 128 == 0
    if aligned and (nodes, reps) == (8, 4):
        return fused(
            nodes, reps, rot_scale, tokens, norm_gain, key_cotangent, secondary, master,
            moment_first, moment_second, signs,
        )
    had_table = sylvester(key_width)
    sign_rows = (1 - 2 * signs).astype(jnp.float32).reshape(2, key_width)
    floats = tokens.astype(jnp.float32)
    inverse = lax.rsqrt(jnp.mean(floats * floats, axis=-1, keepdims=True) + norm_eps)
    normed = floats * inverse
    hidden = (normed * norm_gain).astype(jnp.bfloat16)
    if not aligned:
        hidden = hidden.reshape(tok_rows, nodes * reps, master_rows).transpose(1, 0, 2)
    coded, keys, hidden_grad = step(
        nodes, reps, aligned, rot_scale, hidden, key_cotangent, secondary,
        sign_rows,
    )
    if not aligned:
        hidden_grad = hidden_grad.transpose(1, 0, 2).reshape(tok_rows, model_width)
    hidden_grad = hidden_grad.astype(jnp.float32)
    new_first = beta_first * moment_first + (1.0 - beta_first) * coded
    new_second = beta_second * moment_second + (1.0 - beta_second) * coded * coded
    first_hat = new_first / (1.0 - beta_first**adam_steps)
    second_hat = new_second / (1.0 - beta_second**adam_steps)
    ratio = first_hat / (jnp.sqrt(second_hat) + adam_eps)
    lower = ratio[:, :key_width]
    upper = ratio[:, key_width:]
    norm_root = math.sqrt(2 * key_width)
    row_even = (
        jnp.dot(lower + upper, had_table, precision=lax.Precision.HIGHEST)
        / norm_root
        * sign_rows[0]
    )
    row_odd = (
        jnp.dot(lower - upper, had_table, precision=lax.Precision.HIGHEST)
        / norm_root
        * sign_rows[1]
    )
    groups = master_rows // (2 * PAIR_GAP)
    update = jnp.stack(
        [
            row_even.reshape(groups, PAIR_GAP, key_width),
            row_odd.reshape(groups, PAIR_GAP, key_width),
        ],
        axis=1,
    ).reshape(master_rows, key_width)
    new_master = master - learn_rate * (update + weight_decay * master)
    new_secondary = spread(reps, new_master.astype(jnp.bfloat16)).reshape(
        reps * master_rows, key_width
    )
    scaled = hidden_grad * norm_gain
    token_grad = (
        inverse * (scaled - normed * jnp.mean(scaled * normed, axis=-1, keepdims=True))
    ).astype(jnp.bfloat16)
    return (keys, token_grad, new_master, new_first, new_second, new_secondary)


def solution(mesh):
    return jax.shard_map(
        shards,
        mesh=mesh,
        in_specs=(
            P(("node", "rep"), None),
            P(),
            P(("node", "rep"), None),
            P("node", None),
            P(("node", "rep"), None),
            P(("node", "rep"), None),
            P(("node", "rep"), None),
            P(),
        ),
        out_specs=(
            P(("node", "rep"), None),
            P(("node", "rep"), None),
            P(("node", "rep"), None),
            P(("node", "rep"), None),
            P(("node", "rep"), None),
            P("node", None),
        ),
        check_vma=False,
    )
```

```python
import functools
import math

import jax
import jax.numpy as jnp
from jax import lax
from jax.experimental import pallas as pl
from jax.experimental.pallas import tpu as pltpu
from jax.sharding import PartitionSpec as P

PAIR_GAP = 16
MESH = pl.DeviceIdType.MESH

norm_eps = 1e-05
adam_eps = 1e-08
beta_first = 0.9
beta_second = 0.95
adam_steps = 10
learn_rate = 0.002
weight_decay = 0.1

ANY = pl.BlockSpec(memory_space=pl.ANY)
HBM = pl.BlockSpec(memory_space=pltpu.HBM)
VMEM = pl.BlockSpec(memory_space=pltpu.VMEM)


def sylvester(extent):
    position = jnp.arange(extent, dtype=jnp.int32)
    parity = jnp.zeros((extent, extent), jnp.int32)
    for bit_place in range(extent.bit_length() - 1):
        parity = parity + (position[:, None] >> bit_place & 1) * (
            position[None, :] >> bit_place & 1
        )
    return (1 - 2 * (parity % 2)).astype(jnp.float32)


def split(index):
    return index // 2, lax.rem(index, 2)


def greet(peers):
    barrier = pltpu.get_barrier_semaphore()
    for peer in peers:
        pl.semaphore_signal(barrier, inc=1, device_id=peer, device_id_type=MESH)
    pl.semaphore_wait(barrier, len(peers))


def remote(src, dst, send, recv, peer):
    return pltpu.make_async_remote_copy(
        src_ref=src,
        dst_ref=dst,
        send_sem=send,
        recv_sem=recv,
        device_id=peer,
        device_id_type=MESH,
    )


def axis_peers(axis, size):
    me = lax.axis_index(axis)
    return [{axis: lax.rem(me + k, size)} for k in range(1, size)]


def pair_peers(axis, size):
    high, low = split(lax.axis_index(axis))
    half = size // 2
    partner = {axis: high * 2 + 1 - low}
    same = [{axis: lax.rem(high + k, half) * 2 + low} for k in range(1, half)]
    return partner, same


class PairGather:
    def __init__(self, axis, size, src, out, local_sem, send, recv):
        self.half = size // 2
        me = lax.axis_index(axis)
        high, low = split(me)
        partner, same = pair_peers(axis, size)
        self.local = pltpu.make_async_copy(src, out.at[me], local_sem)
        self.first = [
            remote(src, out.at[me], send.at[0, k], recv.at[0, k], same[k - 1])
            for k in range(1, self.half)
        ]
        self.second = [remote(src, out.at[me], send.at[1, 0], recv.at[1, 0], partner)]
        for k in range(1, self.half):
            origin = lax.rem(high + self.half - k, self.half) * 2 + low
            self.second.append(
                remote(out.at[origin], out.at[origin], send.at[1, k], recv.at[1, k], partner)
            )

    def start(self):
        for copy in self.first:
            copy.start()
        self.second[0].start()
        self.local.start()

    def forward(self, k):
        self.first[k - 1].wait_recv()
        self.second[k].start()

    def finish(self):
        for copy in self.second:
            copy.wait_recv()
        for copy in self.first + self.second:
            copy.wait_send()
        self.local.wait()


def step_kernel(
    nodes, reps, aligned, scale, hid, cot, sec, table, coded, keys, grad_out,
    hid_in, cot_in, sec_in, rot, term, grad, acc, part,
    from_pair, to_same, from_same, key_in,
    cs, cr, hs, hr, ss, sr, ps, pr, zs, zr, gs, gr, ks, kr, cot_own, hid_own, sec_own, grad_own,
):
    f32 = jnp.float32
    rep = lax.axis_index("rep")
    high, low = split(lax.axis_index("node"))
    half = nodes // 2
    partner, same = pair_peers("node", nodes)
    rep_peers = axis_peers("rep", reps)
    columns, key_width = sec_in.shape[1:]
    tok_rows = cot_in.shape[1]
    group_tokens = reps * tok_rows

    def piece(ref, node, owner):
        index = node * reps + owner
        if aligned:
            return ref.at[:, pl.ds(pl.multiple_of(index * columns, columns), columns)]
        return ref.at[index]

    greet(rep_peers + [partner] + same)
    weights = PairGather(
        "node", nodes, sec.at[pl.ds(pl.multiple_of(rep * columns, columns), columns)], sec_in,
        sec_own.at[0], ss, sr,
    )
    weights.start()
    cot_moves = [
        remote(cot, cot_in.at[rep], cs.at[k], cr.at[k], peer) for k, peer in enumerate(rep_peers)
    ]
    cot_moves.append(pltpu.make_async_copy(cot, cot_in.at[rep], cot_own.at[0]))
    for copy in cot_moves:
        copy.start()
    turns = list(range(1, half)) + [0]
    order = [lax.rem(high + k, half) * 2 + 1 - low for k in turns]
    order += [lax.rem(high + k, half) * 2 + low for k in turns]
    hid_moves = []
    for i, node in enumerate(order):
        moves = [
            remote(
                piece(hid, node, peer["rep"]), hid_in.at[node, rep], hs.at[k, i], hr.at[k, i], peer
            )
            for k, peer in enumerate(rep_peers)
        ]
        moves.append(
            pltpu.make_async_copy(piece(hid, node, rep), hid_in.at[node, rep], hid_own.at[i])
        )
        for copy in moves:
            copy.start()
        hid_moves.append(moves)

    for copy in cot_moves:
        copy.wait()
    group_cot = cot_in[...].reshape(group_tokens, key_width)
    shape = (key_width, key_width)
    parity = lax.broadcasted_iota(jnp.int32, shape, 0) & lax.broadcasted_iota(jnp.int32, shape, 1)
    for shift in (8, 4, 2, 1):
        parity = parity ^ (parity >> shift)
    had = (1 - 2 * (parity & 1)).astype(f32).astype(rot.dtype)
    for a in range(2):
        flipped = (group_cot.astype(f32) * table[a : a + 1, :]).astype(rot.dtype)
        rot[:, a * key_width : (a + 1) * key_width] = (
            jnp.dot(flipped, had, preferred_element_type=f32) * scale
        ).astype(rot.dtype)
    acc[...] = jnp.zeros_like(acc)

    def make_term(i):
        for copy in hid_moves[i]:
            copy.wait()
        chunk = hid_in[order[i]].reshape(group_tokens, columns)
        product = lax.dot_general(
            chunk, rot[...], (((0,), (0,)), ((), ())), preferred_element_type=f32
        ).reshape(columns // (2 * PAIR_GAP), 2, PAIR_GAP, 2 * key_width)
        first = product[:, 0, :, :key_width].reshape(columns // 2, key_width)
        second = product[:, 1, :, key_width:].reshape(columns // 2, key_width)
        term[i, :, :key_width] = (first + second).astype(term.dtype)
        term[i, :, key_width:] = (first - second).astype(term.dtype)

    swaps = []
    stays = []

    def use_weights(count, node):
        block = sec_in[node]
        rows = lax.dot_general(
            cot_in[...].reshape(group_tokens, key_width), block, (((1,), (1,)), ((), ())),
            preferred_element_type=f32,
        )
        grad[node] = rows.astype(grad.dtype).reshape(reps, tok_rows, columns)
        for k, peer in enumerate(rep_peers):
            copy = remote(
                grad.at[node, peer["rep"]], piece(grad_out, node, rep),
                gs.at[k, count], gr.at[k, count], peer,
            )
            copy.start()
            swaps.append(copy)
        copy = pltpu.make_async_copy(
            grad.at[node, rep], piece(grad_out, node, rep), grad_own.at[count]
        )
        copy.start()
        stays.append(copy)
        chunk = hid_in[node].reshape(group_tokens, columns)
        acc[...] += jnp.dot(chunk, block, preferred_element_type=f32)

    pairs = []
    for i in range(half):
        make_term(i)
        pairs.append(remote(term.at[i], from_pair.at[i], ps.at[i], pr.at[i], partner))
        pairs[-1].start()
        if i:
            weights.forward(i)
    weights.local.wait()
    onward = []
    for j, k in enumerate(turns):
        make_term(half + j)
        pairs[j].wait_recv()
        total = term[half + j].astype(f32) + from_pair[j].astype(f32)
        if k:
            to_same[j] = total.astype(to_same.dtype)
            onward.append(remote(to_same.at[j], from_same.at[j], zs.at[j], zr.at[j], same[k - 1]))
            onward[-1].start()
        else:
            coded[...] = total
        use_weights(j, order[half + j])
    for j in range(half):
        weights.second[j].wait_recv()
        use_weights(half + j, lax.rem(high + half - j, half) * 2 + 1 - low)
    part[...] = acc[...].astype(part.dtype).reshape(part.shape)
    key_moves = [
        remote(part.at[peer["rep"]], key_in.at[k], ks.at[k], kr.at[k], peer)
        for k, peer in enumerate(rep_peers)
    ]
    for copy in key_moves:
        copy.start()
    for j, copy in enumerate(onward):
        copy.wait_recv()
        coded[...] += from_same[j].astype(f32)
    total = part[rep].astype(f32)
    for k, copy in enumerate(key_moves):
        copy.wait_recv()
        total = total + key_in[k].astype(f32)
    keys[...] = total.astype(keys.dtype)
    for copy in swaps:
        copy.wait()
    for copy in stays:
        copy.wait()
    for copy in weights.first + weights.second + pairs + onward + key_moves:
        copy.wait_send()


def step(nodes, reps, aligned, scale, hid, cot, sec, table):
    dma = pltpu.SemaphoreType.DMA
    half = nodes // 2
    columns = sec.shape[0] // reps
    tok_rows, key_width = cot.shape
    group_tokens = reps * tok_rows
    block = (columns // 2, 2 * key_width)
    bf16 = jnp.bfloat16
    return pl.pallas_call(
        functools.partial(step_kernel, nodes, reps, aligned, scale),
        out_shape=(
            jax.ShapeDtypeStruct(block, jnp.float32),
            jax.ShapeDtypeStruct(cot.shape, bf16),
            jax.ShapeDtypeStruct(hid.shape, bf16),
        ),
        in_specs=[ANY, ANY, ANY, VMEM],
        out_specs=(VMEM,) * 3,
        scratch_shapes=[
            pltpu.VMEM((nodes, reps, tok_rows, columns), bf16),
            pltpu.VMEM((reps, tok_rows, key_width), bf16),
            pltpu.VMEM((nodes, columns, key_width), bf16),
            pltpu.VMEM((group_tokens, 2 * key_width), bf16),
            pltpu.VMEM((nodes,) + block, bf16),
            pltpu.VMEM((nodes, reps, tok_rows, columns), bf16),
            pltpu.VMEM((group_tokens, key_width), jnp.float32),
            pltpu.VMEM((reps, tok_rows, key_width), bf16),
            pltpu.VMEM((half,) + block, bf16),
            pltpu.VMEM((half - 1,) + block, bf16),
            pltpu.VMEM((half - 1,) + block, bf16),
            pltpu.VMEM((reps - 1, tok_rows, key_width), bf16),
        ]
        + [dma((reps - 1,))] * 2
        + [dma((reps - 1, nodes))] * 2
        + [dma((2, half))] * 2
        + [dma((half,))] * 2
        + [dma((half - 1,))] * 2
        + [dma((reps - 1, nodes))] * 2
        + [dma((reps - 1,))] * 2
        + [dma((1,)), dma((nodes,)), dma((1,)), dma((nodes,))],
        compiler_params=pltpu.CompilerParams(collective_id=0, has_side_effects=True),
    )(hid, cot, sec, table)


def spread_kernel(reps, src, out, send, recv, local):
    partner, same = pair_peers("rep", reps)
    greet([partner] + same)
    rows = PairGather("rep", reps, src, out, local.at[0], send, recv)
    rows.start()
    for k in range(1, reps // 2):
        rows.forward(k)
    rows.finish()


def spread(reps, rows):
    dma = pltpu.SemaphoreType.DMA
    return pl.pallas_call(
        functools.partial(spread_kernel, reps),
        out_shape=jax.ShapeDtypeStruct((reps,) + rows.shape, rows.dtype),
        in_specs=[VMEM],
        out_specs=VMEM,
        scratch_shapes=[dma((2, reps // 2))] * 2 + [dma((1,))],
        compiler_params=pltpu.CompilerParams(collective_id=1, has_side_effects=True),
    )(rows)


def flip(index, bits):
    for bit in (1, 2, 4):
        if bits & bit:
            index = index + bit * (1 - 2 * lax.rem(lax.div(index, bit), 2))
    return index


def fused_kernel(
    nodes, reps, scale,
    tok, gain_hbm, cot, sec, master, first, second, signs_hbm,
    keys_out, grad_out, master_out, first_out, second_out, sec_out,
    x_in, hid, hid_in, cot_in, sec_in, sec_own, rot, had, term, total, from_pair,
    to_chain, from_chain, grad, grad_in, acc, inv,
    part, part_in, cross, cross_in, master_in, first_in, second_in, ext, gain, signs,
    xl, ll, cs, cr, hs, hr, ws, wr, ps, pr, zs, zr, gs, gr, ks, kr, ss, sr, es, er,
):
    f32, bf16 = jnp.float32, jnp.bfloat16
    rep = lax.axis_index("rep")
    me = lax.axis_index("node")
    pieces, tok_rows, columns = x_in.shape
    key_width = cot_in.shape[2]
    group_tokens = reps * tok_rows
    half = columns // 2
    rep_kinds = (2, 3, 1)
    rep_peer = {k: {"rep": flip(rep, k)} for k in rep_kinds}
    level, side = split(me)
    upper, odd = split(level)
    inner = upper + odd - 2 * upper * odd
    beside = {"node": flip(me, 1)}
    next_to = {"node": flip(me, 2)}
    middle = {"node": 2 * (nodes // 2 - 1 - level) + side}

    def inside(body):
        pl.when(inner == 1)(body)

    def at_end(body):
        pl.when(inner == 0)(body)

    last = nodes // 2 - 1
    source = [level + 1 - 2 * odd, 2 - upper, last - last * upper]
    target = [last - last * upper, 2 + upper - 2 * odd, 1 + odd, level]

    def node_at(z, other):
        return 2 * z + (1 - side if other else side)

    loads = [
        pltpu.make_async_copy(tok.at[:, pl.ds(columns * i, columns)], x_in.at[i], xl.at[i])
        for i in range(pieces)
    ]
    own_cot = pltpu.make_async_copy(cot, cot_in.at[rep], ll.at[0])
    own_sec = pltpu.make_async_copy(sec, sec_own, ll.at[1])
    state = [
        pltpu.make_async_copy(master, master_in, ll.at[2]),
        pltpu.make_async_copy(first, first_in, ll.at[3]),
        pltpu.make_async_copy(second, second_in, ll.at[4]),
    ]
    small = [
        pltpu.make_async_copy(gain_hbm, gain, ll.at[5]),
        pltpu.make_async_copy(signs_hbm, signs, ll.at[6]),
    ]
    for copy in [own_cot] + loads + small + [own_sec] + state:
        copy.start()
    barrier = pltpu.get_barrier_semaphore()
    common = [rep_peer[k] for k in rep_kinds] + [beside, next_to]
    for peer in common:
        pl.semaphore_signal(barrier, inc=1, device_id=peer, device_id_type=MESH)

    @inside
    def _():
        pl.semaphore_signal(barrier, inc=1, device_id=middle, device_id_type=MESH)

    pl.semaphore_wait(barrier, len(common) + inner)

    sent = []
    sent_inside = []
    sent_at_end = []

    def go(copy, where=sent):
        copy.start()
        where.append(copy)
        return copy

    quarter = sec.at[pl.ds(pl.multiple_of(rep * columns, columns), columns)]
    counter = []

    def weight(z, other, peer, slot, where=sent):
        node = me if z is None else node_at(z, other)
        src = quarter if z is None else sec_in.at[node]
        index = len(counter)
        counter.append(index)
        copy = remote(src, sec_in.at[node], ws.at[index], wr.at[slot], peer)
        where.append(copy)
        return copy

    def arrived(slot):
        block = sec_in.at[me]
        remote(block, block, ws.at[0], wr.at[slot], beside).wait_recv()

    weight(None, 0, next_to, (0, 0)).start()
    weight(None, 0, beside, (0, 3)).start()
    inside(weight(None, 0, middle, (0, 1), sent_inside).start)

    cot_moves = {
        2: go(remote(cot, cot_in.at[rep], cs.at[0], cr.at[0], rep_peer[2])),
        1: go(remote(cot, cot_in.at[rep], cs.at[1], cr.at[1], rep_peer[1])),
    }

    for copy in loads + small:
        copy.wait()

    def squares(i, running):
        x = x_in[i].astype(f32)
        x = x * x
        for lane in range(0, columns, 128):
            running = running + x[:, lane : lane + 128]
        return running

    squared = lax.fori_loop(0, pieces, squares, jnp.zeros((tok_rows, 128), f32))
    mean = jnp.sum(squared, axis=-1, keepdims=True) * (1.0 / (pieces * columns))
    inv[...] = jnp.broadcast_to(lax.rsqrt(mean + norm_eps), inv.shape)

    order = [node_at(z, other) for z in target for other in (1, 0)]
    hid_moves = []
    for i, node in enumerate(order):
        moves = []
        for k in rep_kinds + (0,):
            owner = flip(rep, k)
            index = node * reps + owner
            value = (x_in[index].astype(f32) * inv[...] * gain[index]).astype(bf16)
            if k:
                hid[node, owner] = value
                moves.append(
                    go(
                        remote(
                            hid.at[node, owner], hid_in.at[node, rep],
                            hs.at[k - 1, i], hr.at[k - 1, i], rep_peer[k],
                        )
                    )
                )
            else:
                hid_in[node, rep] = value
        hid_moves.append(moves)

    shape = (key_width, key_width)
    parity = lax.broadcasted_iota(jnp.int32, shape, 0) & lax.broadcasted_iota(jnp.int32, shape, 1)
    for shift in (8, 4, 2, 1):
        parity = parity ^ (parity >> shift)
    had[...] = (1 - 2 * (parity & 1)).astype(f32).astype(bf16)
    chunks = key_width // 128
    sign_row = []
    for a in range(2):
        bits = [signs[a * chunks + c : a * chunks + c + 1, :] for c in range(chunks)]
        sign_row.append((1 - 2 * jnp.concatenate(bits, axis=1)).astype(f32))

    cot_moves[2].wait_recv()
    across = cot_in.at[flip(rep, 2)]
    cot_moves[3] = go(remote(across, across, cs.at[2], cr.at[2], rep_peer[1]))
    own_cot.wait()
    cot_moves[1].wait_recv()
    cot_moves[3].wait_recv()
    for a in range(2):
        flipped = (cot_in[...].reshape(group_tokens, key_width).astype(f32) * sign_row[a]).astype(bf16)
        rot[:, a * key_width : (a + 1) * key_width] = (
            jnp.dot(flipped, had[...], preferred_element_type=f32) * scale
        ).astype(bf16)

    def make_term(i):
        for copy in hid_moves[i]:
            copy.wait_recv()
        chunk = hid_in[order[i]].reshape(group_tokens, columns)
        product = lax.dot_general(
            chunk, rot[...], (((0,), (0,)), ((), ())), preferred_element_type=f32
        ).reshape(columns // (2 * PAIR_GAP), 2, PAIR_GAP, 2 * key_width)
        upper = product[:, 0, :, :key_width].reshape(half, key_width)
        lower = product[:, 1, :, key_width:].reshape(half, key_width)
        return upper + lower, upper - lower

    def add_up(dst, *parts):
        value = parts[0].astype(f32)
        for other in parts[1:]:
            value = value + other.astype(f32)
        dst[...] = value.astype(dst.dtype)

    grad_moves = []

    def local_grads():
        own_sec.wait()
        for k in range(reps):
            block = sec_own[pl.ds(k * columns, columns)]
            grad_in[me * reps + k] = lax.dot_general(
                cot_in[rep], block, (((1,), (1,)), ((), ())), preferred_element_type=f32
            ).astype(bf16)

    def use_grads(node):
        rows = lax.dot_general(
            cot_in[...].reshape(group_tokens, key_width), sec_in[node], (((1,), (1,)), ((), ())),
            preferred_element_type=f32,
        )
        grad[node] = rows.astype(bf16).reshape(reps, tok_rows, columns)
        slot = len(grad_moves)
        moves = [
            go(
                remote(
                    grad.at[node, flip(rep, k)], grad_in.at[node * reps + rep],
                    gs.at[k - 1, slot], gr.at[k - 1, slot], rep_peer[k],
                )
            )
            for k in rep_kinds
        ]
        grad_moves.append((node, moves))
        grad_in[node * reps + rep] = grad[node, rep]

    def use_keys(node, start=False):
        if node is me:
            block = sec_own[pl.ds(pl.multiple_of(rep * columns, columns), columns)]
        else:
            block = sec_in[node]
        product = jnp.dot(
            hid_in[node].reshape(group_tokens, columns), block, preferred_element_type=f32
        )
        if start:
            acc[...] = product
        else:
            acc[...] += product

    extra_nodes = [node_at(level, 1), node_at(source[0], 0)]
    extra = [[], []]

    def fetch(e):
        other = sec.at[pl.ds(pl.multiple_of(flip(rep, 2) * columns, columns), columns)]
        peer = next_to if e else beside
        extra[e].append(go(remote(other, ext.at[e, 2], es.at[e, 2], er.at[e, 2], peer)))

    def pass_on(e):
        extra[e][0].wait_recv()
        for k, src in ((1, sec_in.at[extra_nodes[e]]), (3, ext.at[e, 2])):
            extra[e].append(go(remote(src, ext.at[e, k], es.at[e, k], er.at[e, k], rep_peer[1])))

    def extra_grads(e):
        node = extra_nodes[e]
        for copy in extra[e][1:]:
            copy.wait_recv()
        for k in range(4):
            block = ext[e, k] if k else sec_in[node]
            grad_in[node * reps + flip(rep, k)] = lax.dot_general(
                cot_in[rep], block, (((1,), (1,)), ((), ())), preferred_element_type=f32
            ).astype(bf16)

    pair_moves = {}

    def to_pair(i):
        upper_half, lower_half = make_term(2 * i)
        rows = upper_half.shape[0] // 2
        for h in range(2):
            term[i, h, :, :key_width] = upper_half[h * rows : (h + 1) * rows].astype(bf16)
            term[i, h, :, key_width:] = lower_half[h * rows : (h + 1) * rows].astype(bf16)
            pair_moves[i, h] = go(
                remote(term.at[i, h], from_pair.at[i, h], ps.at[i, h], pr.at[i, h], beside)
            )

    def keep(i):
        upper_half, lower_half = make_term(2 * i + 1)
        total[i, :, :key_width] = upper_half
        total[i, :, key_width:] = lower_half

    def mine(i, h):
        rows = total.shape[1] // 2
        return total[i, h * rows : (h + 1) * rows]

    def chained(index, h):
        dst = from_chain.at[index, h]
        remote(dst, dst, zs.at[0, h], zr.at[index, h], next_to).wait_recv()
        return from_chain[index, h]

    def pass_sum(i, h, within):
        other = middle if within else next_to
        peer, index = [(other, within), (next_to, 2 + within), (other, 3 + within)][i]
        copy = remote(
            to_chain.at[i, h], from_chain.at[index, h], zs.at[i, h], zr.at[index, h], peer
        )
        (sent_inside if within else sent_at_end).append(copy)

        def body():
            pair_moves[i, h].wait_recv()
            parts = [mine(i, h), from_pair[i, h]]
            if within:
                parts.append(chained(i, h))
            add_up(to_chain.at[i, h], *parts)
            copy.start()

        (inside if within else at_end)(body)

    spread_moves = {}
    norm_root = math.sqrt(2 * key_width)
    master_half = columns // 2

    def spread_block(owner, h):
        return sec_out.at[owner, pl.ds(h * master_half, master_half)]

    def finalize(h):
        pair_moves[3, h].wait_recv()
        rows = total.shape[1] // 2
        total[3, h * rows : (h + 1) * rows] = (
            mine(3, h) + from_pair[3, h].astype(f32) + chained(3, h).astype(f32)
        )

        @inside
        def _():
            total[3, h * rows : (h + 1) * rows] += chained(4, h).astype(f32)

        coded = mine(3, h)
        here = pl.ds(h * (half // 2), half // 2)
        new_first = beta_first * first_in[here] + (1.0 - beta_first) * coded
        new_second = beta_second * second_in[here] + (1.0 - beta_second) * coded * coded
        first_out[here] = new_first
        second_out[here] = new_second
        first_hat = new_first / (1.0 - beta_first**adam_steps)
        second_hat = new_second / (1.0 - beta_second**adam_steps)
        ratio = first_hat / (jnp.sqrt(second_hat) + adam_eps)
        rows = []
        for a in range(2):
            if a:
                mixed = ratio[:, :key_width] - ratio[:, key_width:]
            else:
                mixed = ratio[:, :key_width] + ratio[:, key_width:]
            turned = jnp.zeros_like(mixed)
            for _ in range(3):
                high = mixed.astype(bf16)
                mixed = mixed - high.astype(f32)
                turned = turned + jnp.dot(high, had[...], preferred_element_type=f32)
            rows.append(
                (turned * (1.0 / norm_root) * sign_row[a]).reshape(
                    half // (2 * PAIR_GAP), 1, PAIR_GAP, key_width
                )
            )
        update = jnp.concatenate(rows, axis=1).reshape(master_half, key_width)
        there = pl.ds(h * master_half, master_half)
        old = master_in[there]
        new_master = old - learn_rate * (update + weight_decay * old)
        master_out[there] = new_master
        sec_out[rep, there] = new_master.astype(bf16)
        src = spread_block(rep, h)
        for k in (2, 1):
            spread_moves[k, h] = go(
                remote(src, src, ss.at[k - 1, h], sr.at[k - 1, h], rep_peer[k])
            )

    def spread_on(h):
        spread_moves[2, h].wait_recv()
        src = spread_block(flip(rep, 2), h)
        spread_moves[3, h] = go(remote(src, src, ss.at[2, h], sr.at[2, h], rep_peer[1]))

    to_pair(0)
    local_grads()
    arrived((0, 0))

    first_on = weight(source[0], 0, middle, (0, 2), sent_inside)
    second_on = weight(source[1], 0, next_to, (0, 1), sent_inside)

    @inside
    def _():
        first_on.start()
        arrived((0, 1))
        second_on.start()

    arrived((0, 3))
    at_end(weight(level, 1, next_to, (1, 0), sent_at_end).start)

    keep(0)
    pass_sum(0, 0, 0)
    to_pair(1)
    pass_sum(0, 1, 0)

    onwards = [
        weight(source[2], 0, next_to, (0, 2), sent_inside),
        weight(level, 1, next_to, (1, 0), sent_inside),
        weight(level, 1, middle, (1, 1), sent_inside),
    ]

    @inside
    def _():
        arrived((0, 2))
        for copy in onwards:
            copy.start()

    keep(1)
    pass_sum(0, 0, 1)
    pass_sum(1, 0, 0)

    @at_end
    def _():
        arrived((0, 1))

    use_grads(node_at(source[1], 0))
    to_pair(2)
    pass_sum(0, 1, 1)
    pass_sum(1, 1, 0)
    keep(2)
    use_keys(node_at(source[0], 0), True)
    use_keys(node_at(source[1], 0))
    pass_sum(1, 0, 1)
    pass_sum(2, 0, 0)
    to_pair(3)
    pass_sum(1, 1, 1)
    pass_sum(2, 1, 0)

    sideways = weight(source[2], 0, beside, (1, 2), sent_at_end)

    @at_end
    def _():
        arrived((0, 2))
        sideways.start()

    fetch(0)
    use_grads(node_at(source[2], 0))
    pass_sum(2, 0, 1)
    arrived((1, 0))
    use_grads(node_at(source[0], 1))
    pass_sum(2, 1, 1)

    third_on = weight(source[0], 1, middle, (1, 2), sent_inside)
    fourth_on = weight(source[1], 1, next_to, (1, 1), sent_inside)

    @inside
    def _():
        third_on.start()
        arrived((1, 1))
        fourth_on.start()

    fetch(1)
    keep(3)
    use_keys(node_at(source[2], 0))
    use_keys(node_at(level, 1))
    use_keys(me)
    use_keys(node_at(source[0], 1))
    for copy in state:
        copy.wait()
    finalize(0)
    finalize(1)

    @at_end
    def _():
        arrived((1, 1))

    use_grads(node_at(source[1], 1))
    use_keys(node_at(source[1], 1))
    spread_on(0)
    arrived((1, 2))
    use_grads(node_at(source[2], 1))
    use_keys(node_at(source[2], 1))
    for i, k in enumerate((3, 1)):
        owner = flip(rep, k)
        part[i] = acc[pl.ds(pl.multiple_of(owner * tok_rows, tok_rows), tok_rows)].astype(bf16)
    part_move = go(remote(part, part_in, ks.at[0], kr.at[0], rep_peer[1]))
    part_move.wait_recv()
    away = flip(rep, 2)
    cross[...] = (
        acc[pl.ds(pl.multiple_of(away * tok_rows, tok_rows), tok_rows)] + part_in[0].astype(f32)
    ).astype(bf16)
    cross_move = go(remote(cross, cross_in, ks.at[1], kr.at[1], rep_peer[2]))
    spread_on(1)
    for e in range(2):
        pass_on(e)
    for e in range(2):
        extra_grads(e)

    def overlap(node):
        def add(k, running):
            index = node * reps + k
            value = grad_in[index].astype(f32) * gain[index] * x_in[index].astype(f32)
            for lane in range(0, columns, 128):
                running = running + value[:, lane : lane + 128]
            return running

        return add

    running = jnp.zeros((tok_rows, 128), f32)
    for node, moves in [(node, []) for node in [me] + extra_nodes] + grad_moves:
        for copy in moves:
            copy.wait_recv()
        running = lax.fori_loop(0, reps, overlap(node), running)
    against = jnp.sum(running, axis=-1, keepdims=True) * (1.0 / (pieces * columns))
    one = inv[:, :1]
    factor = jnp.broadcast_to(one * one * one * against, (tok_rows, columns))

    def finish(i, carry):
        scaled = grad_in[i].astype(f32) * gain[i]
        grad_out[i] = (inv[...] * scaled - x_in[i].astype(f32) * factor).astype(bf16)
        return carry

    lax.fori_loop(0, pieces, finish, 0)

    late = [cross_move] + [spread_moves[3, h] for h in range(2)]
    for copy in sent:
        if not any(copy is other for other in late):
            copy.wait_send()
    cross_move.wait_recv()
    keys_out[...] = (
        acc[pl.ds(pl.multiple_of(rep * tok_rows, tok_rows), tok_rows)]
        + part_in[1].astype(f32)
        + cross_in[...].astype(f32)
    ).astype(keys_out.dtype)
    for k in (1, 3):
        for h in range(2):
            spread_moves[k, h].wait_recv()
    for copy in late:
        copy.wait_send()

    @inside
    def _():
        for copy in sent_inside:
            copy.wait_send()

    @at_end
    def _():
        for copy in sent_at_end:
            copy.wait_send()


def store_kernel(keys, grad, master, first, second, sec, *refs):
    keys_out, grad_out, master_out, first_out, second_out, sec_out, sems = refs
    pieces, _, columns = grad.shape
    rows = sec.shape[1]
    moves = [
        pltpu.make_async_copy(grad.at[i], grad_out.at[:, pl.ds(columns * i, columns)], sems.at[i])
        for i in range(pieces)
    ]
    pairs = [(keys, keys_out), (master, master_out), (first, first_out), (second, second_out)]
    pairs += [(sec.at[i], sec_out.at[pl.ds(rows * i, rows)]) for i in range(sec.shape[0])]
    for i, (src, dst) in enumerate(pairs):
        moves.append(pltpu.make_async_copy(src, dst, sems.at[pieces + i]))
    for copy in moves:
        copy.start()
    for copy in moves:
        copy.wait()


def fused(nodes, reps, scale, tokens, gain, cot, sec, master, first, second, signs):
    dma = pltpu.SemaphoreType.DMA
    f32, bf16 = jnp.float32, jnp.bfloat16
    tok_rows, model_width = tokens.shape
    key_width = cot.shape[1]
    columns = master.shape[0]
    pieces = model_width // columns
    block = first.shape
    part = (block[0] // 2, block[1])
    group_tokens = reps * tok_rows
    vmem = pltpu.VMEM
    far = functools.partial(pltpu.with_memory_space_constraint, memory_space=pltpu.HBM)
    results = pl.pallas_call(
        functools.partial(fused_kernel, nodes, reps, scale),
        out_shape=(
            vmem(cot.shape, bf16),
            vmem((pieces, tok_rows, columns), bf16),
            vmem(master.shape, f32),
            vmem(block, f32),
            vmem(block, f32),
            vmem((reps,) + master.shape, bf16),
        ),
        in_specs=[HBM] * 8,
        out_specs=(VMEM,) * 6,
        scratch_shapes=[
            vmem((pieces, tok_rows, columns), bf16),
            vmem((nodes, reps, tok_rows, columns), bf16),
            vmem((nodes, reps, tok_rows, columns), bf16),
            vmem((reps, tok_rows, key_width), bf16),
            vmem((nodes, columns, key_width), bf16),
            vmem(sec.shape, bf16),
            vmem((group_tokens, 2 * key_width), bf16),
            vmem((key_width, key_width), bf16),
            vmem((4, 2) + part, bf16),
            vmem((4,) + block, f32),
            vmem((4, 2) + part, bf16),
            vmem((3, 2) + part, bf16),
            vmem((5, 2) + part, bf16),
            vmem((nodes, reps, tok_rows, columns), bf16),
            vmem((pieces, tok_rows, columns), bf16),
            vmem((group_tokens, key_width), f32),
            vmem((tok_rows, columns), f32),
            vmem((2, tok_rows, key_width), bf16),
            vmem((2, tok_rows, key_width), bf16),
            vmem((tok_rows, key_width), bf16),
            vmem((tok_rows, key_width), bf16),
            vmem(master.shape, f32),
            vmem(block, f32),
            vmem(block, f32),
            vmem((2, 4, columns, key_width), bf16),
            vmem((pieces, 1, columns), f32),
            vmem((2 * key_width // 128, 128), jnp.int32),
        ]
        + [dma((pieces,)), dma((7,))]
        + [dma((3,))] * 2
        + [dma((3, nodes))] * 2
        + [dma((12,)), dma((2, 4))]
        + [dma((4, 2))] * 2
        + [dma((3, 2)), dma((5, 2))]
        + [dma((3, nodes))] * 2
        + [dma((2,))] * 2
        + [dma((3, 2))] * 2
        + [dma((2, 4))] * 2,
        compiler_params=pltpu.CompilerParams(
            collective_id=2, has_side_effects=True, vmem_limit_bytes=56 << 20
        ),
    )(
        far(tokens), far(gain.reshape(pieces, 1, columns)), far(cot), far(sec), far(master),
        far(first), far(second), far(signs.reshape(-1, 128)),
    )
    held = [pltpu.with_memory_space_constraint(value, pltpu.VMEM) for value in results]
    like = jax.ShapeDtypeStruct
    return pl.pallas_call(
        store_kernel,
        out_shape=(
            like(cot.shape, bf16),
            like(tokens.shape, bf16),
            like(master.shape, f32),
            like(block, f32),
            like(block, f32),
            like(sec.shape, bf16),
        ),
        in_specs=[VMEM] * 6,
        out_specs=(ANY,) * 6,
        scratch_shapes=[dma((pieces + 4 + reps,))],
        compiler_params=pltpu.CompilerParams(vmem_limit_bytes=1 << 20),
    )(*held)


def shards(tokens, norm_gain, key_cotangent, secondary, master, moment_first, moment_second, signs):
    tok_rows, model_width = tokens.shape
    key_width = key_cotangent.shape[1]
    nodes = lax.axis_size("node")
    reps = lax.axis_size("rep")
    all_tokens = tok_rows * nodes * reps
    master_rows = master.shape[0]
    rot_scale = 1.0 / (math.sqrt(2 * key_width) * all_tokens)
    aligned = master_rows % 128 == 0
    if aligned and (nodes, reps) == (8, 4):
        return fused(
            nodes, reps, rot_scale, tokens, norm_gain, key_cotangent, secondary, master,
            moment_first, moment_second, signs,
        )
    had_table = sylvester(key_width)
    sign_rows = (1 - 2 * signs).astype(jnp.float32).reshape(2, key_width)
    floats = tokens.astype(jnp.float32)
    inverse = lax.rsqrt(jnp.mean(floats * floats, axis=-1, keepdims=True) + norm_eps)
    normed = floats * inverse
    hidden = (normed * norm_gain).astype(jnp.bfloat16)
    if not aligned:
        hidden = hidden.reshape(tok_rows, nodes * reps, master_rows).transpose(1, 0, 2)
    coded, keys, hidden_grad = step(
        nodes, reps, aligned, rot_scale, hidden, key_cotangent, secondary,
        sign_rows,
    )
    if not aligned:
        hidden_grad = hidden_grad.transpose(1, 0, 2).reshape(tok_rows, model_width)
    hidden_grad = hidden_grad.astype(jnp.float32)
    new_first = beta_first * moment_first + (1.0 - beta_first) * coded
    new_second = beta_second * moment_second + (1.0 - beta_second) * coded * coded
    first_hat = new_first / (1.0 - beta_first**adam_steps)
    second_hat = new_second / (1.0 - beta_second**adam_steps)
    ratio = first_hat / (jnp.sqrt(second_hat) + adam_eps)
    lower = ratio[:, :key_width]
    upper = ratio[:, key_width:]
    norm_root = math.sqrt(2 * key_width)
    row_even = (
        jnp.dot(lower + upper, had_table, precision=lax.Precision.HIGHEST)
        / norm_root
        * sign_rows[0]
    )
    row_odd = (
        jnp.dot(lower - upper, had_table, precision=lax.Precision.HIGHEST)
        / norm_root
        * sign_rows[1]
    )
    groups = master_rows // (2 * PAIR_GAP)
    update = jnp.stack(
        [
            row_even.reshape(groups, PAIR_GAP, key_width),
            row_odd.reshape(groups, PAIR_GAP, key_width),
        ],
        axis=1,
    ).reshape(master_rows, key_width)
    new_master = master - learn_rate * (update + weight_decay * master)
    new_secondary = spread(reps, new_master.astype(jnp.bfloat16)).reshape(
        reps * master_rows, key_width
    )
    scaled = hidden_grad * norm_gain
    token_grad = (
        inverse * (scaled - normed * jnp.mean(scaled * normed, axis=-1, keepdims=True))
    ).astype(jnp.bfloat16)
    return (keys, token_grad, new_master, new_first, new_second, new_secondary)


def solution(mesh):
    return jax.shard_map(
        shards,
        mesh=mesh,
        in_specs=(
            P(("node", "rep"), None),
            P(),
            P(("node", "rep"), None),
            P("node", None),
            P(("node", "rep"), None),
            P(("node", "rep"), None),
            P(("node", "rep"), None),
            P(),
        ),
        out_specs=(
            P(("node", "rep"), None),
            P(("node", "rep"), None),
            P(("node", "rep"), None),
            P(("node", "rep"), None),
            P(("node", "rep"), None),
            P("node", None),
        ),
        check_vma=False,
    )
```

```python
import functools
import math

import jax
import jax.numpy as jnp
from jax import lax
from jax.experimental import pallas as pl
from jax.experimental.pallas import tpu as pltpu
from jax.sharding import PartitionSpec as P

PAIR_GAP = 16
MESH = pl.DeviceIdType.MESH

norm_eps = 1e-05
adam_eps = 1e-08
beta_first = 0.9
beta_second = 0.95
adam_steps = 10
learn_rate = 0.002
weight_decay = 0.1

ANY = pl.BlockSpec(memory_space=pl.ANY)
HBM = pl.BlockSpec(memory_space=pltpu.HBM)
VMEM = pl.BlockSpec(memory_space=pltpu.VMEM)


def sylvester(extent):
    position = jnp.arange(extent, dtype=jnp.int32)
    parity = jnp.zeros((extent, extent), jnp.int32)
    for bit_place in range(extent.bit_length() - 1):
        parity = parity + (position[:, None] >> bit_place & 1) * (
            position[None, :] >> bit_place & 1
        )
    return (1 - 2 * (parity % 2)).astype(jnp.float32)


def split(index):
    return index // 2, lax.rem(index, 2)


def greet(peers):
    barrier = pltpu.get_barrier_semaphore()
    for peer in peers:
        pl.semaphore_signal(barrier, inc=1, device_id=peer, device_id_type=MESH)
    pl.semaphore_wait(barrier, len(peers))


def remote(src, dst, send, recv, peer):
    return pltpu.make_async_remote_copy(
        src_ref=src,
        dst_ref=dst,
        send_sem=send,
        recv_sem=recv,
        device_id=peer,
        device_id_type=MESH,
    )


def axis_peers(axis, size):
    me = lax.axis_index(axis)
    return [{axis: lax.rem(me + k, size)} for k in range(1, size)]


def pair_peers(axis, size):
    high, low = split(lax.axis_index(axis))
    half = size // 2
    partner = {axis: high * 2 + 1 - low}
    same = [{axis: lax.rem(high + k, half) * 2 + low} for k in range(1, half)]
    return partner, same


class PairGather:
    def __init__(self, axis, size, src, out, local_sem, send, recv):
        self.half = size // 2
        me = lax.axis_index(axis)
        high, low = split(me)
        partner, same = pair_peers(axis, size)
        self.local = pltpu.make_async_copy(src, out.at[me], local_sem)
        self.first = [
            remote(src, out.at[me], send.at[0, k], recv.at[0, k], same[k - 1])
            for k in range(1, self.half)
        ]
        self.second = [remote(src, out.at[me], send.at[1, 0], recv.at[1, 0], partner)]
        for k in range(1, self.half):
            origin = lax.rem(high + self.half - k, self.half) * 2 + low
            self.second.append(
                remote(out.at[origin], out.at[origin], send.at[1, k], recv.at[1, k], partner)
            )

    def start(self):
        for copy in self.first:
            copy.start()
        self.second[0].start()
        self.local.start()

    def forward(self, k):
        self.first[k - 1].wait_recv()
        self.second[k].start()

    def finish(self):
        for copy in self.second:
            copy.wait_recv()
        for copy in self.first + self.second:
            copy.wait_send()
        self.local.wait()


def step_kernel(
    nodes, reps, aligned, scale, hid, cot, sec, table, coded, keys, grad_out,
    hid_in, cot_in, sec_in, rot, term, grad, acc, part,
    from_pair, to_same, from_same, key_in,
    cs, cr, hs, hr, ss, sr, ps, pr, zs, zr, gs, gr, ks, kr, cot_own, hid_own, sec_own, grad_own,
):
    f32 = jnp.float32
    rep = lax.axis_index("rep")
    high, low = split(lax.axis_index("node"))
    half = nodes // 2
    partner, same = pair_peers("node", nodes)
    rep_peers = axis_peers("rep", reps)
    columns, key_width = sec_in.shape[1:]
    tok_rows = cot_in.shape[1]
    group_tokens = reps * tok_rows

    def piece(ref, node, owner):
        index = node * reps + owner
        if aligned:
            return ref.at[:, pl.ds(pl.multiple_of(index * columns, columns), columns)]
        return ref.at[index]

    greet(rep_peers + [partner] + same)
    weights = PairGather(
        "node", nodes, sec.at[pl.ds(pl.multiple_of(rep * columns, columns), columns)], sec_in,
        sec_own.at[0], ss, sr,
    )
    weights.start()
    cot_moves = [
        remote(cot, cot_in.at[rep], cs.at[k], cr.at[k], peer) for k, peer in enumerate(rep_peers)
    ]
    cot_moves.append(pltpu.make_async_copy(cot, cot_in.at[rep], cot_own.at[0]))
    for copy in cot_moves:
        copy.start()
    turns = list(range(1, half)) + [0]
    order = [lax.rem(high + k, half) * 2 + 1 - low for k in turns]
    order += [lax.rem(high + k, half) * 2 + low for k in turns]
    hid_moves = []
    for i, node in enumerate(order):
        moves = [
            remote(
                piece(hid, node, peer["rep"]), hid_in.at[node, rep], hs.at[k, i], hr.at[k, i], peer
            )
            for k, peer in enumerate(rep_peers)
        ]
        moves.append(
            pltpu.make_async_copy(piece(hid, node, rep), hid_in.at[node, rep], hid_own.at[i])
        )
        for copy in moves:
            copy.start()
        hid_moves.append(moves)

    for copy in cot_moves:
        copy.wait()
    group_cot = cot_in[...].reshape(group_tokens, key_width)
    shape = (key_width, key_width)
    parity = lax.broadcasted_iota(jnp.int32, shape, 0) & lax.broadcasted_iota(jnp.int32, shape, 1)
    for shift in (8, 4, 2, 1):
        parity = parity ^ (parity >> shift)
    had = (1 - 2 * (parity & 1)).astype(f32).astype(rot.dtype)
    for a in range(2):
        flipped = (group_cot.astype(f32) * table[a : a + 1, :]).astype(rot.dtype)
        rot[:, a * key_width : (a + 1) * key_width] = (
            jnp.dot(flipped, had, preferred_element_type=f32) * scale
        ).astype(rot.dtype)
    acc[...] = jnp.zeros_like(acc)

    def make_term(i):
        for copy in hid_moves[i]:
            copy.wait()
        chunk = hid_in[order[i]].reshape(group_tokens, columns)
        product = lax.dot_general(
            chunk, rot[...], (((0,), (0,)), ((), ())), preferred_element_type=f32
        ).reshape(columns // (2 * PAIR_GAP), 2, PAIR_GAP, 2 * key_width)
        first = product[:, 0, :, :key_width].reshape(columns // 2, key_width)
        second = product[:, 1, :, key_width:].reshape(columns // 2, key_width)
        term[i, :, :key_width] = (first + second).astype(term.dtype)
        term[i, :, key_width:] = (first - second).astype(term.dtype)

    swaps = []
    stays = []

    def use_weights(count, node):
        block = sec_in[node]
        rows = lax.dot_general(
            cot_in[...].reshape(group_tokens, key_width), block, (((1,), (1,)), ((), ())),
            preferred_element_type=f32,
        )
        grad[node] = rows.astype(grad.dtype).reshape(reps, tok_rows, columns)
        for k, peer in enumerate(rep_peers):
            copy = remote(
                grad.at[node, peer["rep"]], piece(grad_out, node, rep),
                gs.at[k, count], gr.at[k, count], peer,
            )
            copy.start()
            swaps.append(copy)
        copy = pltpu.make_async_copy(
            grad.at[node, rep], piece(grad_out, node, rep), grad_own.at[count]
        )
        copy.start()
        stays.append(copy)
        chunk = hid_in[node].reshape(group_tokens, columns)
        acc[...] += jnp.dot(chunk, block, preferred_element_type=f32)

    pairs = []
    for i in range(half):
        make_term(i)
        pairs.append(remote(term.at[i], from_pair.at[i], ps.at[i], pr.at[i], partner))
        pairs[-1].start()
        if i:
            weights.forward(i)
    weights.local.wait()
    onward = []
    for j, k in enumerate(turns):
        make_term(half + j)
        pairs[j].wait_recv()
        total = term[half + j].astype(f32) + from_pair[j].astype(f32)
        if k:
            to_same[j] = total.astype(to_same.dtype)
            onward.append(remote(to_same.at[j], from_same.at[j], zs.at[j], zr.at[j], same[k - 1]))
            onward[-1].start()
        else:
            coded[...] = total
        use_weights(j, order[half + j])
    for j in range(half):
        weights.second[j].wait_recv()
        use_weights(half + j, lax.rem(high + half - j, half) * 2 + 1 - low)
    part[...] = acc[...].astype(part.dtype).reshape(part.shape)
    key_moves = [
        remote(part.at[peer["rep"]], key_in.at[k], ks.at[k], kr.at[k], peer)
        for k, peer in enumerate(rep_peers)
    ]
    for copy in key_moves:
        copy.start()
    for j, copy in enumerate(onward):
        copy.wait_recv()
        coded[...] += from_same[j].astype(f32)
    total = part[rep].astype(f32)
    for k, copy in enumerate(key_moves):
        copy.wait_recv()
        total = total + key_in[k].astype(f32)
    keys[...] = total.astype(keys.dtype)
    for copy in swaps:
        copy.wait()
    for copy in stays:
        copy.wait()
    for copy in weights.first + weights.second + pairs + onward + key_moves:
        copy.wait_send()


def step(nodes, reps, aligned, scale, hid, cot, sec, table):
    dma = pltpu.SemaphoreType.DMA
    half = nodes // 2
    columns = sec.shape[0] // reps
    tok_rows, key_width = cot.shape
    group_tokens = reps * tok_rows
    block = (columns // 2, 2 * key_width)
    bf16 = jnp.bfloat16
    return pl.pallas_call(
        functools.partial(step_kernel, nodes, reps, aligned, scale),
        out_shape=(
            jax.ShapeDtypeStruct(block, jnp.float32),
            jax.ShapeDtypeStruct(cot.shape, bf16),
            jax.ShapeDtypeStruct(hid.shape, bf16),
        ),
        in_specs=[ANY, ANY, ANY, VMEM],
        out_specs=(VMEM,) * 3,
        scratch_shapes=[
            pltpu.VMEM((nodes, reps, tok_rows, columns), bf16),
            pltpu.VMEM((reps, tok_rows, key_width), bf16),
            pltpu.VMEM((nodes, columns, key_width), bf16),
            pltpu.VMEM((group_tokens, 2 * key_width), bf16),
            pltpu.VMEM((nodes,) + block, bf16),
            pltpu.VMEM((nodes, reps, tok_rows, columns), bf16),
            pltpu.VMEM((group_tokens, key_width), jnp.float32),
            pltpu.VMEM((reps, tok_rows, key_width), bf16),
            pltpu.VMEM((half,) + block, bf16),
            pltpu.VMEM((half - 1,) + block, bf16),
            pltpu.VMEM((half - 1,) + block, bf16),
            pltpu.VMEM((reps - 1, tok_rows, key_width), bf16),
        ]
        + [dma((reps - 1,))] * 2
        + [dma((reps - 1, nodes))] * 2
        + [dma((2, half))] * 2
        + [dma((half,))] * 2
        + [dma((half - 1,))] * 2
        + [dma((reps - 1, nodes))] * 2
        + [dma((reps - 1,))] * 2
        + [dma((1,)), dma((nodes,)), dma((1,)), dma((nodes,))],
        compiler_params=pltpu.CompilerParams(collective_id=0, has_side_effects=True),
    )(hid, cot, sec, table)


def spread_kernel(reps, src, out, send, recv, local):
    partner, same = pair_peers("rep", reps)
    greet([partner] + same)
    rows = PairGather("rep", reps, src, out, local.at[0], send, recv)
    rows.start()
    for k in range(1, reps // 2):
        rows.forward(k)
    rows.finish()


def spread(reps, rows):
    dma = pltpu.SemaphoreType.DMA
    return pl.pallas_call(
        functools.partial(spread_kernel, reps),
        out_shape=jax.ShapeDtypeStruct((reps,) + rows.shape, rows.dtype),
        in_specs=[VMEM],
        out_specs=VMEM,
        scratch_shapes=[dma((2, reps // 2))] * 2 + [dma((1,))],
        compiler_params=pltpu.CompilerParams(collective_id=1, has_side_effects=True),
    )(rows)


def flip(index, bits):
    for bit in (1, 2, 4):
        if bits & bit:
            index = index + bit * (1 - 2 * lax.rem(lax.div(index, bit), 2))
    return index


def fused_kernel(
    nodes, reps, scale,
    tok, gain_hbm, cot, sec, master, first, second, signs_hbm,
    keys_out, grad_in, master_out, first_out, second_out, sec_out, x_in, gain, inv, factor,
    hid, hid_in, cot_in, sec_in, sec_own, rot, had, term, total, from_pair,
    to_chain, from_chain, grad, acc,
    part, part_in, cross, cross_in, master_in, first_in, second_in, ext, signs,
    xl, ll, cs, cr, hs, hr, ws, wr, ps, pr, zs, zr, gs, gr, ks, kr, ss, sr, es, er,
):
    f32, bf16 = jnp.float32, jnp.bfloat16
    rep = lax.axis_index("rep")
    me = lax.axis_index("node")
    pieces, tok_rows, columns = x_in.shape
    key_width = cot_in.shape[2]
    group_tokens = reps * tok_rows
    half = columns // 2
    rep_kinds = (2, 3, 1)
    rep_peer = {k: {"rep": flip(rep, k)} for k in rep_kinds}
    level, side = split(me)
    upper, odd = split(level)
    inner = upper + odd - 2 * upper * odd
    beside = {"node": flip(me, 1)}
    next_to = {"node": flip(me, 2)}
    middle = {"node": 2 * (nodes // 2 - 1 - level) + side}

    def inside(body):
        pl.when(inner == 1)(body)

    def at_end(body):
        pl.when(inner == 0)(body)

    last = nodes // 2 - 1
    source = [level + 1 - 2 * odd, 2 - upper, last - last * upper]
    target = [last - last * upper, 2 + upper - 2 * odd, 1 + odd, level]

    def node_at(z, other):
        return 2 * z + (1 - side if other else side)

    loads = [
        pltpu.make_async_copy(tok.at[:, pl.ds(columns * i, columns)], x_in.at[i], xl.at[i])
        for i in range(pieces)
    ]
    own_cot = pltpu.make_async_copy(cot, cot_in.at[rep], ll.at[0])
    own_sec = pltpu.make_async_copy(sec, sec_own, ll.at[1])
    state = [
        pltpu.make_async_copy(master, master_in, ll.at[2]),
        pltpu.make_async_copy(first, first_in, ll.at[3]),
        pltpu.make_async_copy(second, second_in, ll.at[4]),
    ]
    small = [
        pltpu.make_async_copy(gain_hbm, gain, ll.at[5]),
        pltpu.make_async_copy(signs_hbm, signs, ll.at[6]),
    ]
    for copy in [own_cot] + loads + small + [own_sec] + state:
        copy.start()
    barrier = pltpu.get_barrier_semaphore()
    common = [rep_peer[k] for k in rep_kinds] + [beside, next_to]
    for peer in common:
        pl.semaphore_signal(barrier, inc=1, device_id=peer, device_id_type=MESH)

    @inside
    def _():
        pl.semaphore_signal(barrier, inc=1, device_id=middle, device_id_type=MESH)

    pl.semaphore_wait(barrier, len(common) + inner)

    sent = []
    sent_inside = []
    sent_at_end = []

    def go(copy, where=sent):
        copy.start()
        where.append(copy)
        return copy

    quarter = sec.at[pl.ds(pl.multiple_of(rep * columns, columns), columns)]
    counter = []
    extra = [[], []]

    def fetch(e, h):
        start = pl.multiple_of(flip(rep, 2) * columns + h * half, half)
        peer = next_to if e else beside
        dst = ext.at[e, 2, pl.ds(h * half, half)]
        slot = 2 * h
        extra[e].append(
            go(remote(sec.at[pl.ds(start, half)], dst, es.at[e, slot], er.at[e, slot], peer))
        )

    def weight(z, other, peer, slot, where=sent):
        node = me if z is None else node_at(z, other)
        src = quarter if z is None else sec_in.at[node]
        index = len(counter)
        counter.append(index)
        copy = remote(src, sec_in.at[node], ws.at[index], wr.at[slot], peer)
        where.append(copy)
        return copy

    def arrived(slot):
        block = sec_in.at[me]
        remote(block, block, ws.at[0], wr.at[slot], beside).wait_recv()

    weight(None, 0, next_to, (0, 0)).start()
    weight(None, 0, beside, (0, 3)).start()
    inside(weight(None, 0, middle, (0, 1), sent_inside).start)
    for e in range(2):
        fetch(e, 0)

    cot_moves = {
        2: go(remote(cot, cot_in.at[rep], cs.at[0], cr.at[0], rep_peer[2])),
        1: go(remote(cot, cot_in.at[rep], cs.at[1], cr.at[1], rep_peer[1])),
    }

    for copy in loads + small:
        copy.wait()

    def squares(i, running):
        x = x_in[i].astype(f32)
        x = x * x
        for lane in range(0, columns, 128):
            running = running + x[:, lane : lane + 128]
        return running

    squared = lax.fori_loop(0, pieces, squares, jnp.zeros((tok_rows, 128), f32))
    mean = jnp.sum(squared, axis=-1, keepdims=True) * (1.0 / (pieces * columns))
    inv[...] = jnp.broadcast_to(lax.rsqrt(mean + norm_eps), inv.shape)

    order = [node_at(z, other) for z in target for other in (1, 0)]
    hid_moves = []
    for i, node in enumerate(order):
        moves = []
        for k in rep_kinds + (0,):
            owner = flip(rep, k)
            index = node * reps + owner
            value = (x_in[index].astype(f32) * inv[...] * gain[index]).astype(bf16)
            if k:
                hid[node, owner] = value
                moves.append(
                    go(
                        remote(
                            hid.at[node, owner], hid_in.at[node, rep],
                            hs.at[k - 1, i], hr.at[k - 1, i], rep_peer[k],
                        )
                    )
                )
            else:
                hid_in[node, rep] = value
        hid_moves.append(moves)

    shape = (key_width, key_width)
    parity = lax.broadcasted_iota(jnp.int32, shape, 0) & lax.broadcasted_iota(jnp.int32, shape, 1)
    for shift in (8, 4, 2, 1):
        parity = parity ^ (parity >> shift)
    had[...] = (1 - 2 * (parity & 1)).astype(f32).astype(bf16)
    chunks = key_width // 128
    sign_row = []
    for a in range(2):
        bits = [signs[a * chunks + c : a * chunks + c + 1, :] for c in range(chunks)]
        sign_row.append((1 - 2 * jnp.concatenate(bits, axis=1)).astype(f32))

    cot_moves[2].wait_recv()
    across = cot_in.at[flip(rep, 2)]
    cot_moves[3] = go(remote(across, across, cs.at[2], cr.at[2], rep_peer[1]))
    own_cot.wait()
    cot_moves[1].wait_recv()
    cot_moves[3].wait_recv()
    for a in range(2):
        flipped = (cot_in[...].reshape(group_tokens, key_width).astype(f32) * sign_row[a]).astype(bf16)
        rot[:, a * key_width : (a + 1) * key_width] = (
            jnp.dot(flipped, had[...], preferred_element_type=f32) * scale
        ).astype(bf16)

    def make_term(i):
        for copy in hid_moves[i]:
            copy.wait_recv()
        chunk = hid_in[order[i]].reshape(group_tokens, columns)
        product = lax.dot_general(
            chunk, rot[...], (((0,), (0,)), ((), ())), preferred_element_type=f32
        ).reshape(columns // (2 * PAIR_GAP), 2, PAIR_GAP, 2 * key_width)
        upper = product[:, 0, :, :key_width].reshape(half, key_width)
        lower = product[:, 1, :, key_width:].reshape(half, key_width)
        return upper + lower, upper - lower

    def add_up(dst, *parts):
        value = parts[0].astype(f32)
        for other in parts[1:]:
            value = value + other.astype(f32)
        dst[...] = value.astype(dst.dtype)

    grad_moves = []

    def local_grads():
        own_sec.wait()
        for k in range(reps):
            block = sec_own[pl.ds(k * columns, columns)]
            grad_in[me * reps + k] = lax.dot_general(
                cot_in[rep], block, (((1,), (1,)), ((), ())), preferred_element_type=f32
            ).astype(bf16)

    def use_grads(node):
        rows = lax.dot_general(
            cot_in[...].reshape(group_tokens, key_width), sec_in[node], (((1,), (1,)), ((), ())),
            preferred_element_type=f32,
        )
        grad[node] = rows.astype(bf16).reshape(reps, tok_rows, columns)
        slot = len(grad_moves)
        moves = [
            go(
                remote(
                    grad.at[node, flip(rep, k)], grad_in.at[node * reps + rep],
                    gs.at[k - 1, slot], gr.at[k - 1, slot], rep_peer[k],
                )
            )
            for k in rep_kinds
        ]
        grad_moves.append((node, moves))
        grad_in[node * reps + rep] = grad[node, rep]

    def use_keys(node, start=False):
        if node is me:
            block = sec_own[pl.ds(pl.multiple_of(rep * columns, columns), columns)]
        else:
            block = sec_in[node]
        product = jnp.dot(
            hid_in[node].reshape(group_tokens, columns), block, preferred_element_type=f32
        )
        if start:
            acc[...] = product
        else:
            acc[...] += product

    extra_nodes = [node_at(level, 1), node_at(source[0], 0)]
    def pass_on(e):
        for copy in extra[e]:
            copy.wait_recv()
        for k, src in ((1, sec_in.at[extra_nodes[e]]), (3, ext.at[e, 2])):
            extra[e].append(go(remote(src, ext.at[e, k], es.at[e, k], er.at[e, k], rep_peer[1])))

    def extra_grads(e):
        node = extra_nodes[e]
        for copy in extra[e][2:]:
            copy.wait_recv()
        for k in range(4):
            block = ext[e, k] if k else sec_in[node]
            grad_in[node * reps + flip(rep, k)] = lax.dot_general(
                cot_in[rep], block, (((1,), (1,)), ((), ())), preferred_element_type=f32
            ).astype(bf16)

    pair_moves = {}

    def to_pair(i):
        upper_half, lower_half = make_term(2 * i)
        rows = upper_half.shape[0] // 2
        for h in range(2):
            term[i, h, :, :key_width] = upper_half[h * rows : (h + 1) * rows].astype(bf16)
            term[i, h, :, key_width:] = lower_half[h * rows : (h + 1) * rows].astype(bf16)
            pair_moves[i, h] = go(
                remote(term.at[i, h], from_pair.at[i, h], ps.at[i, h], pr.at[i, h], beside)
            )

    def keep(i):
        upper_half, lower_half = make_term(2 * i + 1)
        total[i, :, :key_width] = upper_half
        total[i, :, key_width:] = lower_half

    def mine(i, h):
        rows = total.shape[1] // 2
        return total[i, h * rows : (h + 1) * rows]

    def chained(index, h):
        dst = from_chain.at[index, h]
        remote(dst, dst, zs.at[0, h], zr.at[index, h], next_to).wait_recv()
        return from_chain[index, h]

    def pass_sum(i, h, within):
        other = middle if within else next_to
        peer, index = [(other, within), (next_to, 2 + within), (other, 3 + within)][i]
        copy = remote(
            to_chain.at[i, h], from_chain.at[index, h], zs.at[i, h], zr.at[index, h], peer
        )
        (sent_inside if within else sent_at_end).append(copy)

        def body():
            pair_moves[i, h].wait_recv()
            parts = [mine(i, h), from_pair[i, h]]
            if within:
                parts.append(chained(i, h))
            add_up(to_chain.at[i, h], *parts)
            copy.start()

        (inside if within else at_end)(body)

    spread_moves = {}
    norm_root = math.sqrt(2 * key_width)
    master_half = columns // 2

    def spread_block(owner, h):
        return sec_out.at[owner, pl.ds(h * master_half, master_half)]

    def finalize(h):
        pair_moves[3, h].wait_recv()
        rows = total.shape[1] // 2
        total[3, h * rows : (h + 1) * rows] = (
            mine(3, h) + from_pair[3, h].astype(f32) + chained(3, h).astype(f32)
        )

        @inside
        def _():
            total[3, h * rows : (h + 1) * rows] += chained(4, h).astype(f32)

        coded = mine(3, h)
        here = pl.ds(h * (half // 2), half // 2)
        new_first = beta_first * first_in[here] + (1.0 - beta_first) * coded
        new_second = beta_second * second_in[here] + (1.0 - beta_second) * coded * coded
        first_out[here] = new_first
        second_out[here] = new_second
        first_hat = new_first / (1.0 - beta_first**adam_steps)
        second_hat = new_second / (1.0 - beta_second**adam_steps)
        ratio = first_hat / (jnp.sqrt(second_hat) + adam_eps)
        rows = []
        for a in range(2):
            if a:
                mixed = ratio[:, :key_width] - ratio[:, key_width:]
            else:
                mixed = ratio[:, :key_width] + ratio[:, key_width:]
            turned = jnp.zeros_like(mixed)
            for _ in range(3):
                high = mixed.astype(bf16)
                mixed = mixed - high.astype(f32)
                turned = turned + jnp.dot(high, had[...], preferred_element_type=f32)
            rows.append(
                (turned * (1.0 / norm_root) * sign_row[a]).reshape(
                    half // (2 * PAIR_GAP), 1, PAIR_GAP, key_width
                )
            )
        update = jnp.concatenate(rows, axis=1).reshape(master_half, key_width)
        there = pl.ds(h * master_half, master_half)
        old = master_in[there]
        new_master = old - learn_rate * (update + weight_decay * old)
        master_out[there] = new_master
        sec_out[rep, there] = new_master.astype(bf16)
        src = spread_block(rep, h)
        for k in (2, 1):
            spread_moves[k, h] = go(
                remote(src, src, ss.at[k - 1, h], sr.at[k - 1, h], rep_peer[k])
            )

    def spread_on(h):
        spread_moves[2, h].wait_recv()
        src = spread_block(flip(rep, 2), h)
        spread_moves[3, h] = go(remote(src, src, ss.at[2, h], sr.at[2, h], rep_peer[1]))

    to_pair(0)
    local_grads()
    arrived((0, 0))

    first_on = weight(source[0], 0, middle, (0, 2), sent_inside)
    second_on = weight(source[1], 0, next_to, (0, 1), sent_inside)

    @inside
    def _():
        first_on.start()
        arrived((0, 1))
        second_on.start()

    arrived((0, 3))
    at_end(weight(level, 1, next_to, (1, 0), sent_at_end).start)

    keep(0)
    pass_sum(0, 0, 0)
    to_pair(1)
    pass_sum(0, 1, 0)

    onwards = [
        weight(source[2], 0, next_to, (0, 2), sent_inside),
        weight(level, 1, next_to, (1, 0), sent_inside),
        weight(level, 1, middle, (1, 1), sent_inside),
    ]

    @inside
    def _():
        arrived((0, 2))
        for copy in onwards:
            copy.start()

    keep(1)
    pass_sum(0, 0, 1)
    pass_sum(1, 0, 0)

    @at_end
    def _():
        arrived((0, 1))

    use_grads(node_at(source[1], 0))
    to_pair(2)
    pass_sum(0, 1, 1)
    pass_sum(1, 1, 0)
    keep(2)
    use_keys(node_at(source[0], 0), True)
    use_keys(node_at(source[1], 0))
    pass_sum(1, 0, 1)
    pass_sum(2, 0, 0)

    @at_end
    def _():
        arrived((0, 2))

    use_grads(node_at(source[2], 0))
    to_pair(3)
    pass_sum(1, 1, 1)
    pass_sum(2, 1, 0)

    sideways = weight(source[2], 0, beside, (1, 2), sent_at_end)

    at_end(sideways.start)

    fetch(0, 1)
    pass_sum(2, 0, 1)
    arrived((1, 0))
    use_grads(node_at(source[0], 1))
    pass_sum(2, 1, 1)

    third_on = weight(source[0], 1, middle, (1, 2), sent_inside)
    fourth_on = weight(source[1], 1, next_to, (1, 1), sent_inside)

    @inside
    def _():
        third_on.start()
        arrived((1, 1))
        fourth_on.start()

    fetch(1, 1)
    keep(3)
    use_keys(node_at(source[2], 0))
    use_keys(node_at(level, 1))
    use_keys(me)
    use_keys(node_at(source[0], 1))
    for copy in state:
        copy.wait()
    finalize(0)
    finalize(1)

    sooner = node_at(inner * source[1] + (1 - inner) * source[2], 1)
    later = node_at(inner * source[2] + (1 - inner) * source[1], 1)

    @at_end
    def _():
        arrived((1, 2))

    use_grads(sooner)
    use_keys(sooner)
    spread_on(0)
    arrived((1, 2 * inner + 1 - inner))
    use_grads(later)
    use_keys(later)
    for i, k in enumerate((3, 1)):
        owner = flip(rep, k)
        part[i] = acc[pl.ds(pl.multiple_of(owner * tok_rows, tok_rows), tok_rows)].astype(bf16)
    part_move = go(remote(part, part_in, ks.at[0], kr.at[0], rep_peer[1]))
    part_move.wait_recv()
    away = flip(rep, 2)
    cross[...] = (
        acc[pl.ds(pl.multiple_of(away * tok_rows, tok_rows), tok_rows)] + part_in[0].astype(f32)
    ).astype(bf16)
    cross_move = go(remote(cross, cross_in, ks.at[1], kr.at[1], rep_peer[2]))
    spread_on(1)
    for e in range(2):
        pass_on(e)
    for e in range(2):
        extra_grads(e)

    def overlap(node):
        def add(k, running):
            index = node * reps + k
            value = grad_in[index].astype(f32) * gain[index] * x_in[index].astype(f32)
            for lane in range(0, columns, 128):
                running = running + value[:, lane : lane + 128]
            return running

        return add

    running = jnp.zeros((tok_rows, 128), f32)
    for node, moves in [(node, []) for node in [me] + extra_nodes] + grad_moves:
        for copy in moves:
            copy.wait_recv()
        running = lax.fori_loop(0, reps, overlap(node), running)
    against = jnp.sum(running, axis=-1, keepdims=True) * (1.0 / (pieces * columns))
    one = inv[:, :1]
    factor[...] = jnp.broadcast_to(one * one * one * against, factor.shape)

    late = [cross_move] + [spread_moves[3, h] for h in range(2)]
    for copy in sent:
        if not any(copy is other for other in late):
            copy.wait_send()
    cross_move.wait_recv()
    keys_out[...] = (
        acc[pl.ds(pl.multiple_of(rep * tok_rows, tok_rows), tok_rows)]
        + part_in[1].astype(f32)
        + cross_in[...].astype(f32)
    ).astype(keys_out.dtype)
    for k in (1, 3):
        for h in range(2):
            spread_moves[k, h].wait_recv()
    for copy in late:
        copy.wait_send()

    @inside
    def _():
        for copy in sent_inside:
            copy.wait_send()

    @at_end
    def _():
        for copy in sent_at_end:
            copy.wait_send()


def store_kernel(keys, grad, master, first, second, sec, x, gain, inv, factor, *refs):
    keys_out, grad_out, master_out, first_out, second_out, sec_out, done, sems = refs
    pieces, _, columns = grad.shape
    rows = sec.shape[1]
    pairs = [(keys, keys_out), (master, master_out), (first, first_out), (second, second_out)]
    pairs += [(sec.at[i], sec_out.at[pl.ds(rows * i, rows)]) for i in range(sec.shape[0])]
    moves = [
        pltpu.make_async_copy(src, dst, sems.at[pieces + i]) for i, (src, dst) in enumerate(pairs)
    ]
    for copy in moves:
        copy.start()
    for i in range(pieces):
        scaled = grad[i].astype(jnp.float32) * gain[i]
        done[i] = (inv[...] * scaled - x[i].astype(jnp.float32) * factor[...]).astype(done.dtype)
        moves.append(
            pltpu.make_async_copy(
                done.at[i], grad_out.at[:, pl.ds(columns * i, columns)], sems.at[i]
            )
        )
        moves[-1].start()
    for copy in moves:
        copy.wait()


def fused(nodes, reps, scale, tokens, gain, cot, sec, master, first, second, signs):
    dma = pltpu.SemaphoreType.DMA
    f32, bf16 = jnp.float32, jnp.bfloat16
    tok_rows, model_width = tokens.shape
    key_width = cot.shape[1]
    columns = master.shape[0]
    pieces = model_width // columns
    block = first.shape
    part = (block[0] // 2, block[1])
    group_tokens = reps * tok_rows
    vmem = pltpu.VMEM
    far = functools.partial(pltpu.with_memory_space_constraint, memory_space=pltpu.HBM)
    results = pl.pallas_call(
        functools.partial(fused_kernel, nodes, reps, scale),
        out_shape=(
            vmem(cot.shape, bf16),
            vmem((pieces, tok_rows, columns), bf16),
            vmem(master.shape, f32),
            vmem(block, f32),
            vmem(block, f32),
            vmem((reps,) + master.shape, bf16),
            vmem((pieces, tok_rows, columns), bf16),
            vmem((pieces, 1, columns), f32),
            vmem((tok_rows, columns), f32),
            vmem((tok_rows, columns), f32),
        ),
        in_specs=[HBM] * 8,
        out_specs=(VMEM,) * 10,
        scratch_shapes=[
            vmem((nodes, reps, tok_rows, columns), bf16),
            vmem((nodes, reps, tok_rows, columns), bf16),
            vmem((reps, tok_rows, key_width), bf16),
            vmem((nodes, columns, key_width), bf16),
            vmem(sec.shape, bf16),
            vmem((group_tokens, 2 * key_width), bf16),
            vmem((key_width, key_width), bf16),
            vmem((4, 2) + part, bf16),
            vmem((4,) + block, f32),
            vmem((4, 2) + part, bf16),
            vmem((3, 2) + part, bf16),
            vmem((5, 2) + part, bf16),
            vmem((nodes, reps, tok_rows, columns), bf16),
            vmem((group_tokens, key_width), f32),
            vmem((2, tok_rows, key_width), bf16),
            vmem((2, tok_rows, key_width), bf16),
            vmem((tok_rows, key_width), bf16),
            vmem((tok_rows, key_width), bf16),
            vmem(master.shape, f32),
            vmem(block, f32),
            vmem(block, f32),
            vmem((2, 4, columns, key_width), bf16),
            vmem((2 * key_width // 128, 128), jnp.int32),
        ]
        + [dma((pieces,)), dma((7,))]
        + [dma((3,))] * 2
        + [dma((3, nodes))] * 2
        + [dma((12,)), dma((2, 4))]
        + [dma((4, 2))] * 2
        + [dma((3, 2)), dma((5, 2))]
        + [dma((3, nodes))] * 2
        + [dma((2,))] * 2
        + [dma((3, 2))] * 2
        + [dma((2, 4))] * 2,
        compiler_params=pltpu.CompilerParams(
            collective_id=2, has_side_effects=True, vmem_limit_bytes=48 << 20
        ),
    )(
        far(tokens), far(gain.reshape(pieces, 1, columns)), far(cot), far(sec), far(master),
        far(first), far(second), far(signs.reshape(-1, 128)),
    )
    held = [pltpu.with_memory_space_constraint(value, pltpu.VMEM) for value in results]
    like = jax.ShapeDtypeStruct
    return pl.pallas_call(
        store_kernel,
        out_shape=(
            like(cot.shape, bf16),
            like(tokens.shape, bf16),
            like(master.shape, f32),
            like(block, f32),
            like(block, f32),
            like(sec.shape, bf16),
        ),
        in_specs=[VMEM] * 10,
        out_specs=(ANY,) * 6,
        scratch_shapes=[vmem((pieces, tok_rows, columns), bf16), dma((pieces + 4 + reps,))],
        compiler_params=pltpu.CompilerParams(vmem_limit_bytes=6 << 20),
    )(*held)


def shards(tokens, norm_gain, key_cotangent, secondary, master, moment_first, moment_second, signs):
    tok_rows, model_width = tokens.shape
    key_width = key_cotangent.shape[1]
    nodes = lax.axis_size("node")
    reps = lax.axis_size("rep")
    all_tokens = tok_rows * nodes * reps
    master_rows = master.shape[0]
    rot_scale = 1.0 / (math.sqrt(2 * key_width) * all_tokens)
    aligned = master_rows % 128 == 0
    if aligned and (nodes, reps) == (8, 4):
        return fused(
            nodes, reps, rot_scale, tokens, norm_gain, key_cotangent, secondary, master,
            moment_first, moment_second, signs,
        )
    had_table = sylvester(key_width)
    sign_rows = (1 - 2 * signs).astype(jnp.float32).reshape(2, key_width)
    floats = tokens.astype(jnp.float32)
    inverse = lax.rsqrt(jnp.mean(floats * floats, axis=-1, keepdims=True) + norm_eps)
    normed = floats * inverse
    hidden = (normed * norm_gain).astype(jnp.bfloat16)
    if not aligned:
        hidden = hidden.reshape(tok_rows, nodes * reps, master_rows).transpose(1, 0, 2)
    coded, keys, hidden_grad = step(
        nodes, reps, aligned, rot_scale, hidden, key_cotangent, secondary,
        sign_rows,
    )
    if not aligned:
        hidden_grad = hidden_grad.transpose(1, 0, 2).reshape(tok_rows, model_width)
    hidden_grad = hidden_grad.astype(jnp.float32)
    new_first = beta_first * moment_first + (1.0 - beta_first) * coded
    new_second = beta_second * moment_second + (1.0 - beta_second) * coded * coded
    first_hat = new_first / (1.0 - beta_first**adam_steps)
    second_hat = new_second / (1.0 - beta_second**adam_steps)
    ratio = first_hat / (jnp.sqrt(second_hat) + adam_eps)
    lower = ratio[:, :key_width]
    upper = ratio[:, key_width:]
    norm_root = math.sqrt(2 * key_width)
    row_even = (
        jnp.dot(lower + upper, had_table, precision=lax.Precision.HIGHEST)
        / norm_root
        * sign_rows[0]
    )
    row_odd = (
        jnp.dot(lower - upper, had_table, precision=lax.Precision.HIGHEST)
        / norm_root
        * sign_rows[1]
    )
    groups = master_rows // (2 * PAIR_GAP)
    update = jnp.stack(
        [
            row_even.reshape(groups, PAIR_GAP, key_width),
            row_odd.reshape(groups, PAIR_GAP, key_width),
        ],
        axis=1,
    ).reshape(master_rows, key_width)
    new_master = master - learn_rate * (update + weight_decay * master)
    new_secondary = spread(reps, new_master.astype(jnp.bfloat16)).reshape(
        reps * master_rows, key_width
    )
    scaled = hidden_grad * norm_gain
    token_grad = (
        inverse * (scaled - normed * jnp.mean(scaled * normed, axis=-1, keepdims=True))
    ).astype(jnp.bfloat16)
    return (keys, token_grad, new_master, new_first, new_second, new_secondary)


def solution(mesh):
    return jax.shard_map(
        shards,
        mesh=mesh,
        in_specs=(
            P(("node", "rep"), None),
            P(),
            P(("node", "rep"), None),
            P("node", None),
            P(("node", "rep"), None),
            P(("node", "rep"), None),
            P(("node", "rep"), None),
            P(),
        ),
        out_specs=(
            P(("node", "rep"), None),
            P(("node", "rep"), None),
            P(("node", "rep"), None),
            P(("node", "rep"), None),
            P(("node", "rep"), None),
            P("node", None),
        ),
        check_vma=False,
    )
```

```python
import functools
import math

import jax
import jax.numpy as jnp
from jax import lax
from jax.experimental import pallas as pl
from jax.experimental.pallas import tpu as pltpu
from jax.sharding import PartitionSpec as P

PAIR_GAP = 16
MESH = pl.DeviceIdType.MESH

norm_eps = 1e-05
adam_eps = 1e-08
beta_first = 0.9
beta_second = 0.95
adam_steps = 10
learn_rate = 0.002
weight_decay = 0.1

ANY = pl.BlockSpec(memory_space=pl.ANY)
HBM = pl.BlockSpec(memory_space=pltpu.HBM)
VMEM = pl.BlockSpec(memory_space=pltpu.VMEM)


def sylvester(extent):
    position = jnp.arange(extent, dtype=jnp.int32)
    parity = jnp.zeros((extent, extent), jnp.int32)
    for bit_place in range(extent.bit_length() - 1):
        parity = parity + (position[:, None] >> bit_place & 1) * (
            position[None, :] >> bit_place & 1
        )
    return (1 - 2 * (parity % 2)).astype(jnp.float32)


def split(index):
    return index // 2, lax.rem(index, 2)


def greet(peers):
    barrier = pltpu.get_barrier_semaphore()
    for peer in peers:
        pl.semaphore_signal(barrier, inc=1, device_id=peer, device_id_type=MESH)
    pl.semaphore_wait(barrier, len(peers))


def remote(src, dst, send, recv, peer):
    return pltpu.make_async_remote_copy(
        src_ref=src,
        dst_ref=dst,
        send_sem=send,
        recv_sem=recv,
        device_id=peer,
        device_id_type=MESH,
    )


def axis_peers(axis, size):
    me = lax.axis_index(axis)
    return [{axis: lax.rem(me + k, size)} for k in range(1, size)]


def pair_peers(axis, size):
    high, low = split(lax.axis_index(axis))
    half = size // 2
    partner = {axis: high * 2 + 1 - low}
    same = [{axis: lax.rem(high + k, half) * 2 + low} for k in range(1, half)]
    return partner, same


class PairGather:
    def __init__(self, axis, size, src, out, local_sem, send, recv):
        self.half = size // 2
        me = lax.axis_index(axis)
        high, low = split(me)
        partner, same = pair_peers(axis, size)
        self.local = pltpu.make_async_copy(src, out.at[me], local_sem)
        self.first = [
            remote(src, out.at[me], send.at[0, k], recv.at[0, k], same[k - 1])
            for k in range(1, self.half)
        ]
        self.second = [remote(src, out.at[me], send.at[1, 0], recv.at[1, 0], partner)]
        for k in range(1, self.half):
            origin = lax.rem(high + self.half - k, self.half) * 2 + low
            self.second.append(
                remote(out.at[origin], out.at[origin], send.at[1, k], recv.at[1, k], partner)
            )

    def start(self):
        for copy in self.first:
            copy.start()
        self.second[0].start()
        self.local.start()

    def forward(self, k):
        self.first[k - 1].wait_recv()
        self.second[k].start()

    def finish(self):
        for copy in self.second:
            copy.wait_recv()
        for copy in self.first + self.second:
            copy.wait_send()
        self.local.wait()


def step_kernel(
    nodes, reps, aligned, scale, hid, cot, sec, table, coded, keys, grad_out,
    hid_in, cot_in, sec_in, rot, term, grad, acc, part,
    from_pair, to_same, from_same, key_in,
    cs, cr, hs, hr, ss, sr, ps, pr, zs, zr, gs, gr, ks, kr, cot_own, hid_own, sec_own, grad_own,
):
    f32 = jnp.float32
    rep = lax.axis_index("rep")
    high, low = split(lax.axis_index("node"))
    half = nodes // 2
    partner, same = pair_peers("node", nodes)
    rep_peers = axis_peers("rep", reps)
    columns, key_width = sec_in.shape[1:]
    tok_rows = cot_in.shape[1]
    group_tokens = reps * tok_rows

    def piece(ref, node, owner):
        index = node * reps + owner
        if aligned:
            return ref.at[:, pl.ds(pl.multiple_of(index * columns, columns), columns)]
        return ref.at[index]

    greet(rep_peers + [partner] + same)
    weights = PairGather(
        "node", nodes, sec.at[pl.ds(pl.multiple_of(rep * columns, columns), columns)], sec_in,
        sec_own.at[0], ss, sr,
    )
    weights.start()
    cot_moves = [
        remote(cot, cot_in.at[rep], cs.at[k], cr.at[k], peer) for k, peer in enumerate(rep_peers)
    ]
    cot_moves.append(pltpu.make_async_copy(cot, cot_in.at[rep], cot_own.at[0]))
    for copy in cot_moves:
        copy.start()
    turns = list(range(1, half)) + [0]
    order = [lax.rem(high + k, half) * 2 + 1 - low for k in turns]
    order += [lax.rem(high + k, half) * 2 + low for k in turns]
    hid_moves = []
    for i, node in enumerate(order):
        moves = [
            remote(
                piece(hid, node, peer["rep"]), hid_in.at[node, rep], hs.at[k, i], hr.at[k, i], peer
            )
            for k, peer in enumerate(rep_peers)
        ]
        moves.append(
            pltpu.make_async_copy(piece(hid, node, rep), hid_in.at[node, rep], hid_own.at[i])
        )
        for copy in moves:
            copy.start()
        hid_moves.append(moves)

    for copy in cot_moves:
        copy.wait()
    group_cot = cot_in[...].reshape(group_tokens, key_width)
    shape = (key_width, key_width)
    parity = lax.broadcasted_iota(jnp.int32, shape, 0) & lax.broadcasted_iota(jnp.int32, shape, 1)
    for shift in (8, 4, 2, 1):
        parity = parity ^ (parity >> shift)
    had = (1 - 2 * (parity & 1)).astype(f32).astype(rot.dtype)
    for a in range(2):
        flipped = (group_cot.astype(f32) * table[a : a + 1, :]).astype(rot.dtype)
        rot[:, a * key_width : (a + 1) * key_width] = (
            jnp.dot(flipped, had, preferred_element_type=f32) * scale
        ).astype(rot.dtype)
    acc[...] = jnp.zeros_like(acc)

    def make_term(i):
        for copy in hid_moves[i]:
            copy.wait()
        chunk = hid_in[order[i]].reshape(group_tokens, columns)
        product = lax.dot_general(
            chunk, rot[...], (((0,), (0,)), ((), ())), preferred_element_type=f32
        ).reshape(columns // (2 * PAIR_GAP), 2, PAIR_GAP, 2 * key_width)
        first = product[:, 0, :, :key_width].reshape(columns // 2, key_width)
        second = product[:, 1, :, key_width:].reshape(columns // 2, key_width)
        term[i, :, :key_width] = (first + second).astype(term.dtype)
        term[i, :, key_width:] = (first - second).astype(term.dtype)

    swaps = []
    stays = []

    def use_weights(count, node):
        block = sec_in[node]
        rows = lax.dot_general(
            cot_in[...].reshape(group_tokens, key_width), block, (((1,), (1,)), ((), ())),
            preferred_element_type=f32,
        )
        grad[node] = rows.astype(grad.dtype).reshape(reps, tok_rows, columns)
        for k, peer in enumerate(rep_peers):
            copy = remote(
                grad.at[node, peer["rep"]], piece(grad_out, node, rep),
                gs.at[k, count], gr.at[k, count], peer,
            )
            copy.start()
            swaps.append(copy)
        copy = pltpu.make_async_copy(
            grad.at[node, rep], piece(grad_out, node, rep), grad_own.at[count]
        )
        copy.start()
        stays.append(copy)
        chunk = hid_in[node].reshape(group_tokens, columns)
        acc[...] += jnp.dot(chunk, block, preferred_element_type=f32)

    pairs = []
    for i in range(half):
        make_term(i)
        pairs.append(remote(term.at[i], from_pair.at[i], ps.at[i], pr.at[i], partner))
        pairs[-1].start()
        if i:
            weights.forward(i)
    weights.local.wait()
    onward = []
    for j, k in enumerate(turns):
        make_term(half + j)
        pairs[j].wait_recv()
        total = term[half + j].astype(f32) + from_pair[j].astype(f32)
        if k:
            to_same[j] = total.astype(to_same.dtype)
            onward.append(remote(to_same.at[j], from_same.at[j], zs.at[j], zr.at[j], same[k - 1]))
            onward[-1].start()
        else:
            coded[...] = total
        use_weights(j, order[half + j])
    for j in range(half):
        weights.second[j].wait_recv()
        use_weights(half + j, lax.rem(high + half - j, half) * 2 + 1 - low)
    part[...] = acc[...].astype(part.dtype).reshape(part.shape)
    key_moves = [
        remote(part.at[peer["rep"]], key_in.at[k], ks.at[k], kr.at[k], peer)
        for k, peer in enumerate(rep_peers)
    ]
    for copy in key_moves:
        copy.start()
    for j, copy in enumerate(onward):
        copy.wait_recv()
        coded[...] += from_same[j].astype(f32)
    total = part[rep].astype(f32)
    for k, copy in enumerate(key_moves):
        copy.wait_recv()
        total = total + key_in[k].astype(f32)
    keys[...] = total.astype(keys.dtype)
    for copy in swaps:
        copy.wait()
    for copy in stays:
        copy.wait()
    for copy in weights.first + weights.second + pairs + onward + key_moves:
        copy.wait_send()


def step(nodes, reps, aligned, scale, hid, cot, sec, table):
    dma = pltpu.SemaphoreType.DMA
    half = nodes // 2
    columns = sec.shape[0] // reps
    tok_rows, key_width = cot.shape
    group_tokens = reps * tok_rows
    block = (columns // 2, 2 * key_width)
    bf16 = jnp.bfloat16
    return pl.pallas_call(
        functools.partial(step_kernel, nodes, reps, aligned, scale),
        out_shape=(
            jax.ShapeDtypeStruct(block, jnp.float32),
            jax.ShapeDtypeStruct(cot.shape, bf16),
            jax.ShapeDtypeStruct(hid.shape, bf16),
        ),
        in_specs=[ANY, ANY, ANY, VMEM],
        out_specs=(VMEM,) * 3,
        scratch_shapes=[
            pltpu.VMEM((nodes, reps, tok_rows, columns), bf16),
            pltpu.VMEM((reps, tok_rows, key_width), bf16),
            pltpu.VMEM((nodes, columns, key_width), bf16),
            pltpu.VMEM((group_tokens, 2 * key_width), bf16),
            pltpu.VMEM((nodes,) + block, bf16),
            pltpu.VMEM((nodes, reps, tok_rows, columns), bf16),
            pltpu.VMEM((group_tokens, key_width), jnp.float32),
            pltpu.VMEM((reps, tok_rows, key_width), bf16),
            pltpu.VMEM((half,) + block, bf16),
            pltpu.VMEM((half - 1,) + block, bf16),
            pltpu.VMEM((half - 1,) + block, bf16),
            pltpu.VMEM((reps - 1, tok_rows, key_width), bf16),
        ]
        + [dma((reps - 1,))] * 2
        + [dma((reps - 1, nodes))] * 2
        + [dma((2, half))] * 2
        + [dma((half,))] * 2
        + [dma((half - 1,))] * 2
        + [dma((reps - 1, nodes))] * 2
        + [dma((reps - 1,))] * 2
        + [dma((1,)), dma((nodes,)), dma((1,)), dma((nodes,))],
        compiler_params=pltpu.CompilerParams(collective_id=0, has_side_effects=True),
    )(hid, cot, sec, table)


def spread_kernel(reps, src, out, send, recv, local):
    partner, same = pair_peers("rep", reps)
    greet([partner] + same)
    rows = PairGather("rep", reps, src, out, local.at[0], send, recv)
    rows.start()
    for k in range(1, reps // 2):
        rows.forward(k)
    rows.finish()


def spread(reps, rows):
    dma = pltpu.SemaphoreType.DMA
    return pl.pallas_call(
        functools.partial(spread_kernel, reps),
        out_shape=jax.ShapeDtypeStruct((reps,) + rows.shape, rows.dtype),
        in_specs=[VMEM],
        out_specs=VMEM,
        scratch_shapes=[dma((2, reps // 2))] * 2 + [dma((1,))],
        compiler_params=pltpu.CompilerParams(collective_id=1, has_side_effects=True),
    )(rows)


def flip(index, bits):
    for bit in (1, 2, 4):
        if bits & bit:
            index = index + bit * (1 - 2 * lax.rem(lax.div(index, bit), 2))
    return index


def fused_kernel(
    nodes, reps, scale,
    tok, gain_hbm, cot, sec, master, first, second, signs_hbm,
    keys_out, grad_in, master_out, first_out, second_out, sec_out, x_in, gain, inv, factor,
    hid, hid_in, cot_in, sec_in, sec_own, rot, had, term, total, from_pair,
    to_chain, from_chain, grad, acc,
    part, part_in, cross, cross_in, master_in, first_in, second_in, ext, ext_half, signs,
    xl, ll, cs, cr, hs, hr, ws, wr, ps, pr, zs, zr, gs, gr, ks, kr, ss, sr, es, er, fs, fr,
):
    f32, bf16 = jnp.float32, jnp.bfloat16
    rep = lax.axis_index("rep")
    me = lax.axis_index("node")
    pieces, tok_rows, columns = x_in.shape
    key_width = cot_in.shape[2]
    group_tokens = reps * tok_rows
    half = columns // 2
    rep_kinds = (2, 3, 1)
    rep_peer = {k: {"rep": flip(rep, k)} for k in rep_kinds}
    level, side = split(me)
    upper, odd = split(level)
    inner = upper + odd - 2 * upper * odd
    beside = {"node": flip(me, 1)}
    next_to = {"node": flip(me, 2)}
    middle = {"node": 2 * (nodes // 2 - 1 - level) + side}

    def inside(body):
        pl.when(inner == 1)(body)

    def at_end(body):
        pl.when(inner == 0)(body)

    last = nodes // 2 - 1
    source = [level + 1 - 2 * odd, 2 - upper, last - last * upper]
    target = [last - last * upper, 2 + upper - 2 * odd, 1 + odd, level]

    def node_at(z, other):
        return 2 * z + (1 - side if other else side)

    loads = [
        pltpu.make_async_copy(tok.at[:, pl.ds(columns * i, columns)], x_in.at[i], xl.at[i])
        for i in range(pieces)
    ]
    own_cot = pltpu.make_async_copy(cot, cot_in.at[rep], ll.at[0])
    own_sec = pltpu.make_async_copy(sec, sec_own, ll.at[1])
    state = [
        pltpu.make_async_copy(master, master_in, ll.at[2]),
        pltpu.make_async_copy(first, first_in, ll.at[3]),
        pltpu.make_async_copy(second, second_in, ll.at[4]),
    ]
    small = [
        pltpu.make_async_copy(gain_hbm, gain, ll.at[5]),
        pltpu.make_async_copy(signs_hbm, signs, ll.at[6]),
    ]
    for copy in [own_cot] + loads + small + [own_sec] + state:
        copy.start()
    barrier = pltpu.get_barrier_semaphore()
    common = [rep_peer[k] for k in rep_kinds] + [beside, next_to]
    for peer in common:
        pl.semaphore_signal(barrier, inc=1, device_id=peer, device_id_type=MESH)

    @inside
    def _():
        pl.semaphore_signal(barrier, inc=1, device_id=middle, device_id_type=MESH)

    pl.semaphore_wait(barrier, len(common) + inner)

    sent = []
    sent_inside = []
    sent_at_end = []

    def go(copy, where=sent):
        copy.start()
        where.append(copy)
        return copy

    quarter = sec.at[pl.ds(pl.multiple_of(rep * columns, columns), columns)]
    counter = []
    extra = [[], []]

    def fetch(e, h):
        start = pl.multiple_of(flip(rep, 2) * columns + h * half, half)
        peer = next_to if e else beside
        dst = ext.at[e, 2, pl.ds(h * half, half)]
        slot = 2 * h
        extra[e].append(
            go(remote(sec.at[pl.ds(start, half)], dst, es.at[e, slot], er.at[e, slot], peer))
        )

    def weight(z, other, peer, slot, where=sent):
        node = me if z is None else node_at(z, other)
        src = quarter if z is None else sec_in.at[node]
        index = len(counter)
        counter.append(index)
        copy = remote(src, sec_in.at[node], ws.at[index], wr.at[slot], peer)
        where.append(copy)
        return copy

    def arrived(slot):
        block = sec_in.at[me]
        remote(block, block, ws.at[0], wr.at[slot], beside).wait_recv()

    weight(None, 0, next_to, (0, 0)).start()
    weight(None, 0, beside, (0, 3)).start()
    inside(weight(None, 0, middle, (0, 1), sent_inside).start)
    for e in range(2):
        fetch(e, 0)

    cot_moves = {
        2: go(remote(cot, cot_in.at[rep], cs.at[0], cr.at[0], rep_peer[2])),
        1: go(remote(cot, cot_in.at[rep], cs.at[1], cr.at[1], rep_peer[1])),
    }

    for copy in loads + small:
        copy.wait()

    def squares(i, running):
        x = x_in[i].astype(f32)
        x = x * x
        for lane in range(0, columns, 128):
            running = running + x[:, lane : lane + 128]
        return running

    squared = lax.fori_loop(0, pieces, squares, jnp.zeros((tok_rows, 128), f32))
    mean = jnp.sum(squared, axis=-1, keepdims=True) * (1.0 / (pieces * columns))
    inv[...] = jnp.broadcast_to(lax.rsqrt(mean + norm_eps), inv.shape)

    order = [node_at(z, other) for z in target for other in (1, 0)]
    hid_moves = []
    for i, node in enumerate(order):
        moves = []
        for k in rep_kinds + (0,):
            owner = flip(rep, k)
            index = node * reps + owner
            value = (x_in[index].astype(f32) * inv[...] * gain[index]).astype(bf16)
            if k:
                hid[node, owner] = value
                moves.append(
                    go(
                        remote(
                            hid.at[node, owner], hid_in.at[node, rep],
                            hs.at[k - 1, i], hr.at[k - 1, i], rep_peer[k],
                        )
                    )
                )
            else:
                hid_in[node, rep] = value
        hid_moves.append(moves)

    shape = (key_width, key_width)
    parity = lax.broadcasted_iota(jnp.int32, shape, 0) & lax.broadcasted_iota(jnp.int32, shape, 1)
    for shift in (8, 4, 2, 1):
        parity = parity ^ (parity >> shift)
    had[...] = (1 - 2 * (parity & 1)).astype(f32).astype(bf16)
    chunks = key_width // 128
    sign_row = []
    for a in range(2):
        bits = [signs[a * chunks + c : a * chunks + c + 1, :] for c in range(chunks)]
        sign_row.append((1 - 2 * jnp.concatenate(bits, axis=1)).astype(f32))

    cot_moves[2].wait_recv()
    across = cot_in.at[flip(rep, 2)]
    cot_moves[3] = go(remote(across, across, cs.at[2], cr.at[2], rep_peer[1]))
    own_cot.wait()
    cot_moves[1].wait_recv()
    cot_moves[3].wait_recv()
    for a in range(2):
        flipped = (cot_in[...].reshape(group_tokens, key_width).astype(f32) * sign_row[a]).astype(bf16)
        rot[:, a * key_width : (a + 1) * key_width] = (
            jnp.dot(flipped, had[...], preferred_element_type=f32) * scale
        ).astype(bf16)

    def make_term(i):
        for copy in hid_moves[i]:
            copy.wait_recv()
        chunk = hid_in[order[i]].reshape(group_tokens, columns)
        product = lax.dot_general(
            chunk, rot[...], (((0,), (0,)), ((), ())), preferred_element_type=f32
        ).reshape(columns // (2 * PAIR_GAP), 2, PAIR_GAP, 2 * key_width)
        upper = product[:, 0, :, :key_width].reshape(half, key_width)
        lower = product[:, 1, :, key_width:].reshape(half, key_width)
        return upper + lower, upper - lower

    def add_up(dst, *parts):
        value = parts[0].astype(f32)
        for other in parts[1:]:
            value = value + other.astype(f32)
        dst[...] = value.astype(dst.dtype)

    grad_moves = []

    def local_grads():
        own_sec.wait()
        for k in range(reps):
            block = sec_own[pl.ds(k * columns, columns)]
            grad_in[me * reps + k] = lax.dot_general(
                cot_in[rep], block, (((1,), (1,)), ((), ())), preferred_element_type=f32
            ).astype(bf16)

    def use_grads(node, cut=False):
        rows = lax.dot_general(
            cot_in[...].reshape(group_tokens, key_width), sec_in[node], (((1,), (1,)), ((), ())),
            preferred_element_type=f32,
        )
        grad[node] = rows.astype(bf16).reshape(reps, tok_rows, columns)
        slot = len(grad_moves)
        moves = []
        for k in rep_kinds:
            src, dst = grad.at[node, flip(rep, k)], grad_in.at[node * reps + rep]
            if cut and k > 1:
                src, dst = src.at[:, pl.ds(half, half)], dst.at[:, pl.ds(half, half)]
            moves.append(
                go(remote(src, dst, gs.at[k - 1, slot], gr.at[k - 1, slot], rep_peer[k]))
            )
        grad_moves.append((node, moves))
        grad_in[node * reps + rep] = grad[node, rep]

    def use_keys(node, start=False):
        if node is me:
            block = sec_own[pl.ds(pl.multiple_of(rep * columns, columns), columns)]
        else:
            block = sec_in[node]
        product = jnp.dot(
            hid_in[node].reshape(group_tokens, columns), block, preferred_element_type=f32
        )
        if start:
            acc[...] = product
        else:
            acc[...] += product

    extra_nodes = [node_at(level, 1), node_at(source[0], 0)]
    def pass_on(e):
        for copy in extra[e][e:]:
            copy.wait_recv()
        for k, src in ((1, sec_in.at[extra_nodes[e]]), (3, ext.at[e, 2])):
            extra[e].append(go(remote(src, ext.at[e, k], es.at[e, k], er.at[e, k], rep_peer[1])))

    def extra_grads(e):
        node = extra_nodes[e]
        for copy in extra[e][2:]:
            copy.wait_recv()
        for k in range(4):
            block = ext[e, k] if k else sec_in[node]
            grad_in[node * reps + flip(rep, k)] = lax.dot_general(
                cot_in[rep], block, (((1,), (1,)), ((), ())), preferred_element_type=f32
            ).astype(bf16)

    half_moves = []

    def fetch_half():
        extra[1][0].wait_recv()
        src = ext.at[1, 2, pl.ds(0, half)]
        half_moves.append(go(remote(src, ext_half.at[0], fs.at[0], fr.at[0], beside)))

    def pass_half():
        half_moves[0].wait_recv()
        half_moves.append(
            go(remote(ext_half.at[0], ext_half.at[1], fs.at[1], fr.at[1], rep_peer[1]))
        )

    def half_grads():
        node = node_at(source[0], 1)
        half_moves[1].wait_recv()
        for i, k in enumerate((2, 3)):
            grad_in[node * reps + flip(rep, k), :, :half] = lax.dot_general(
                cot_in[rep], ext_half[i], (((1,), (1,)), ((), ())), preferred_element_type=f32
            ).astype(bf16)

    pair_moves = {}

    def to_pair(i):
        upper_half, lower_half = make_term(2 * i)
        rows = upper_half.shape[0] // 2
        for h in range(2):
            term[i, h, :, :key_width] = upper_half[h * rows : (h + 1) * rows].astype(bf16)
            term[i, h, :, key_width:] = lower_half[h * rows : (h + 1) * rows].astype(bf16)
            pair_moves[i, h] = go(
                remote(term.at[i, h], from_pair.at[i, h], ps.at[i, h], pr.at[i, h], beside)
            )

    def keep(i):
        upper_half, lower_half = make_term(2 * i + 1)
        total[i, :, :key_width] = upper_half
        total[i, :, key_width:] = lower_half

    def mine(i, h):
        rows = total.shape[1] // 2
        return total[i, h * rows : (h + 1) * rows]

    def chained(index, h):
        dst = from_chain.at[index, h]
        remote(dst, dst, zs.at[0, h], zr.at[index, h], next_to).wait_recv()
        return from_chain[index, h]

    def pass_sum(i, h, within):
        other = middle if within else next_to
        peer, index = [(other, within), (next_to, 2 + within), (other, 3 + within)][i]
        copy = remote(
            to_chain.at[i, h], from_chain.at[index, h], zs.at[i, h], zr.at[index, h], peer
        )
        (sent_inside if within else sent_at_end).append(copy)

        def body():
            pair_moves[i, h].wait_recv()
            parts = [mine(i, h), from_pair[i, h]]
            if within:
                parts.append(chained(i, h))
            add_up(to_chain.at[i, h], *parts)
            copy.start()

        (inside if within else at_end)(body)

    spread_moves = {}
    norm_root = math.sqrt(2 * key_width)
    master_half = columns // 2

    def spread_block(owner, h):
        return sec_out.at[owner, pl.ds(h * master_half, master_half)]

    def finalize(h):
        pair_moves[3, h].wait_recv()
        rows = total.shape[1] // 2
        total[3, h * rows : (h + 1) * rows] = (
            mine(3, h) + from_pair[3, h].astype(f32) + chained(3, h).astype(f32)
        )

        @inside
        def _():
            total[3, h * rows : (h + 1) * rows] += chained(4, h).astype(f32)

        coded = mine(3, h)
        here = pl.ds(h * (half // 2), half // 2)
        new_first = beta_first * first_in[here] + (1.0 - beta_first) * coded
        new_second = beta_second * second_in[here] + (1.0 - beta_second) * coded * coded
        first_out[here] = new_first
        second_out[here] = new_second
        first_hat = new_first / (1.0 - beta_first**adam_steps)
        second_hat = new_second / (1.0 - beta_second**adam_steps)
        ratio = first_hat / (jnp.sqrt(second_hat) + adam_eps)
        rows = []
        for a in range(2):
            if a:
                mixed = ratio[:, :key_width] - ratio[:, key_width:]
            else:
                mixed = ratio[:, :key_width] + ratio[:, key_width:]
            turned = jnp.zeros_like(mixed)
            for _ in range(3):
                high = mixed.astype(bf16)
                mixed = mixed - high.astype(f32)
                turned = turned + jnp.dot(high, had[...], preferred_element_type=f32)
            rows.append(
                (turned * (1.0 / norm_root) * sign_row[a]).reshape(
                    half // (2 * PAIR_GAP), 1, PAIR_GAP, key_width
                )
            )
        update = jnp.concatenate(rows, axis=1).reshape(master_half, key_width)
        there = pl.ds(h * master_half, master_half)
        old = master_in[there]
        new_master = old - learn_rate * (update + weight_decay * old)
        master_out[there] = new_master
        sec_out[rep, there] = new_master.astype(bf16)
        src = spread_block(rep, h)
        for k in (2, 1):
            spread_moves[k, h] = go(
                remote(src, src, ss.at[k - 1, h], sr.at[k - 1, h], rep_peer[k])
            )

    def spread_on(h):
        spread_moves[2, h].wait_recv()
        src = spread_block(flip(rep, 2), h)
        spread_moves[3, h] = go(remote(src, src, ss.at[2, h], sr.at[2, h], rep_peer[1]))

    to_pair(0)
    local_grads()
    arrived((0, 0))

    first_on = weight(source[0], 0, middle, (0, 2), sent_inside)
    second_on = weight(source[1], 0, next_to, (0, 1), sent_inside)

    @inside
    def _():
        first_on.start()
        arrived((0, 1))
        second_on.start()

    arrived((0, 3))
    at_end(weight(level, 1, next_to, (1, 0), sent_at_end).start)
    across_on = [
        weight(level, 1, middle, (1, 1), sent_inside),
        weight(level, 1, next_to, (1, 0), sent_inside),
    ]

    @inside
    def _():
        for copy in across_on:
            copy.start()


    keep(0)
    pass_sum(0, 0, 0)
    to_pair(1)
    pass_sum(0, 1, 0)

    fifth_on = weight(source[2], 0, next_to, (0, 2), sent_inside)

    @inside
    def _():
        arrived((0, 2))
        fifth_on.start()

    keep(1)
    pass_sum(0, 0, 1)
    pass_sum(1, 0, 0)

    @at_end
    def _():
        arrived((0, 1))

    use_grads(node_at(source[1], 0))
    to_pair(2)
    pass_sum(0, 1, 1)
    pass_sum(1, 1, 0)
    keep(2)
    use_keys(node_at(source[0], 0), True)
    use_keys(node_at(source[1], 0))
    pass_sum(1, 0, 1)
    pass_sum(2, 0, 0)
    arrived((1, 0))
    use_grads(node_at(source[0], 1), True)
    to_pair(3)
    pass_sum(2, 0, 1)
    pass_sum(1, 1, 1)
    pass_sum(2, 1, 0)

    sideways = weight(source[2], 0, beside, (1, 2), sent_at_end)

    @at_end
    def _():
        arrived((0, 2))

    use_grads(node_at(source[2], 0))
    at_end(sideways.start)

    fetch(0, 1)
    fetch_half()
    pass_sum(2, 1, 1)

    third_on = weight(source[0], 1, middle, (1, 2), sent_inside)
    fourth_on = weight(source[1], 1, next_to, (1, 1), sent_inside)

    @inside
    def _():
        third_on.start()
        arrived((1, 1))
        fourth_on.start()

    fetch(1, 1)
    keep(3)
    use_keys(node_at(source[2], 0))
    use_keys(node_at(level, 1))
    use_keys(me)
    use_keys(node_at(source[0], 1))
    for copy in state:
        copy.wait()
    finalize(0)
    finalize(1)

    sooner = node_at(inner * source[1] + (1 - inner) * source[2], 1)
    later = node_at(inner * source[2] + (1 - inner) * source[1], 1)

    @at_end
    def _():
        arrived((1, 2))

    use_grads(sooner)
    use_keys(sooner)
    spread_on(0)
    arrived((1, 2 * inner + 1 - inner))
    use_grads(later)
    use_keys(later)
    for i, k in enumerate((3, 1)):
        owner = flip(rep, k)
        part[i] = acc[pl.ds(pl.multiple_of(owner * tok_rows, tok_rows), tok_rows)].astype(bf16)
    part_move = go(remote(part, part_in, ks.at[0], kr.at[0], rep_peer[1]))
    part_move.wait_recv()
    away = flip(rep, 2)
    cross[...] = (
        acc[pl.ds(pl.multiple_of(away * tok_rows, tok_rows), tok_rows)] + part_in[0].astype(f32)
    ).astype(bf16)
    cross_move = go(remote(cross, cross_in, ks.at[1], kr.at[1], rep_peer[2]))
    spread_on(1)
    for e in range(2):
        pass_on(e)
    pass_half()
    for e in range(2):
        extra_grads(e)
    half_grads()

    def overlap(node):
        def add(k, running):
            index = node * reps + k
            value = grad_in[index].astype(f32) * gain[index] * x_in[index].astype(f32)
            for lane in range(0, columns, 128):
                running = running + value[:, lane : lane + 128]
            return running

        return add

    running = jnp.zeros((tok_rows, 128), f32)
    for node, moves in [(node, []) for node in [me] + extra_nodes] + grad_moves:
        for copy in moves:
            copy.wait_recv()
        running = lax.fori_loop(0, reps, overlap(node), running)
    against = jnp.sum(running, axis=-1, keepdims=True) * (1.0 / (pieces * columns))
    one = inv[:, :1]
    factor[...] = jnp.broadcast_to(one * one * one * against, factor.shape)

    late = [cross_move] + [spread_moves[3, h] for h in range(2)]
    for copy in sent:
        if not any(copy is other for other in late):
            copy.wait_send()
    cross_move.wait_recv()
    keys_out[...] = (
        acc[pl.ds(pl.multiple_of(rep * tok_rows, tok_rows), tok_rows)]
        + part_in[1].astype(f32)
        + cross_in[...].astype(f32)
    ).astype(keys_out.dtype)
    for k in (1, 3):
        for h in range(2):
            spread_moves[k, h].wait_recv()
    for copy in late:
        copy.wait_send()

    @inside
    def _():
        for copy in sent_inside:
            copy.wait_send()

    @at_end
    def _():
        for copy in sent_at_end:
            copy.wait_send()


def store_kernel(keys, grad, master, first, second, sec, x, gain, inv, factor, *refs):
    keys_out, grad_out, master_out, first_out, second_out, sec_out, done, sems = refs
    pieces, _, columns = grad.shape
    rows = sec.shape[1]
    pairs = [(keys, keys_out), (master, master_out), (first, first_out), (second, second_out)]
    pairs += [(sec.at[i], sec_out.at[pl.ds(rows * i, rows)]) for i in range(sec.shape[0])]
    moves = [
        pltpu.make_async_copy(src, dst, sems.at[pieces + i]) for i, (src, dst) in enumerate(pairs)
    ]
    for copy in moves:
        copy.start()
    for i in range(pieces):
        scaled = grad[i].astype(jnp.float32) * gain[i]
        done[i] = (inv[...] * scaled - x[i].astype(jnp.float32) * factor[...]).astype(done.dtype)
        moves.append(
            pltpu.make_async_copy(
                done.at[i], grad_out.at[:, pl.ds(columns * i, columns)], sems.at[i]
            )
        )
        moves[-1].start()
    for copy in moves:
        copy.wait()


def fused(nodes, reps, scale, tokens, gain, cot, sec, master, first, second, signs):
    dma = pltpu.SemaphoreType.DMA
    f32, bf16 = jnp.float32, jnp.bfloat16
    tok_rows, model_width = tokens.shape
    key_width = cot.shape[1]
    columns = master.shape[0]
    pieces = model_width // columns
    block = first.shape
    part = (block[0] // 2, block[1])
    group_tokens = reps * tok_rows
    vmem = pltpu.VMEM
    far = functools.partial(pltpu.with_memory_space_constraint, memory_space=pltpu.HBM)
    results = pl.pallas_call(
        functools.partial(fused_kernel, nodes, reps, scale),
        out_shape=(
            vmem(cot.shape, bf16),
            vmem((pieces, tok_rows, columns), bf16),
            vmem(master.shape, f32),
            vmem(block, f32),
            vmem(block, f32),
            vmem((reps,) + master.shape, bf16),
            vmem((pieces, tok_rows, columns), bf16),
            vmem((pieces, 1, columns), f32),
            vmem((tok_rows, columns), f32),
            vmem((tok_rows, columns), f32),
        ),
        in_specs=[HBM] * 8,
        out_specs=(VMEM,) * 10,
        scratch_shapes=[
            vmem((nodes, reps, tok_rows, columns), bf16),
            vmem((nodes, reps, tok_rows, columns), bf16),
            vmem((reps, tok_rows, key_width), bf16),
            vmem((nodes, columns, key_width), bf16),
            vmem(sec.shape, bf16),
            vmem((group_tokens, 2 * key_width), bf16),
            vmem((key_width, key_width), bf16),
            vmem((4, 2) + part, bf16),
            vmem((4,) + block, f32),
            vmem((4, 2) + part, bf16),
            vmem((3, 2) + part, bf16),
            vmem((5, 2) + part, bf16),
            vmem((nodes, reps, tok_rows, columns), bf16),
            vmem((group_tokens, key_width), f32),
            vmem((2, tok_rows, key_width), bf16),
            vmem((2, tok_rows, key_width), bf16),
            vmem((tok_rows, key_width), bf16),
            vmem((tok_rows, key_width), bf16),
            vmem(master.shape, f32),
            vmem(block, f32),
            vmem(block, f32),
            vmem((2, 4, columns, key_width), bf16),
            vmem((2, columns // 2, key_width), bf16),
            vmem((2 * key_width // 128, 128), jnp.int32),
        ]
        + [dma((pieces,)), dma((7,))]
        + [dma((3,))] * 2
        + [dma((3, nodes))] * 2
        + [dma((12,)), dma((2, 4))]
        + [dma((4, 2))] * 2
        + [dma((3, 2)), dma((5, 2))]
        + [dma((3, nodes))] * 2
        + [dma((2,))] * 2
        + [dma((3, 2))] * 2
        + [dma((2, 4))] * 2
        + [dma((2,))] * 2,
        compiler_params=pltpu.CompilerParams(
            collective_id=2, has_side_effects=True, vmem_limit_bytes=48 << 20
        ),
    )(
        far(tokens), far(gain.reshape(pieces, 1, columns)), far(cot), far(sec), far(master),
        far(first), far(second), far(signs.reshape(-1, 128)),
    )
    held = [pltpu.with_memory_space_constraint(value, pltpu.VMEM) for value in results]
    like = jax.ShapeDtypeStruct
    return pl.pallas_call(
        store_kernel,
        out_shape=(
            like(cot.shape, bf16),
            like(tokens.shape, bf16),
            like(master.shape, f32),
            like(block, f32),
            like(block, f32),
            like(sec.shape, bf16),
        ),
        in_specs=[VMEM] * 10,
        out_specs=(ANY,) * 6,
        scratch_shapes=[vmem((pieces, tok_rows, columns), bf16), dma((pieces + 4 + reps,))],
        compiler_params=pltpu.CompilerParams(vmem_limit_bytes=6 << 20),
    )(*held)


def shards(tokens, norm_gain, key_cotangent, secondary, master, moment_first, moment_second, signs):
    tok_rows, model_width = tokens.shape
    key_width = key_cotangent.shape[1]
    nodes = lax.axis_size("node")
    reps = lax.axis_size("rep")
    all_tokens = tok_rows * nodes * reps
    master_rows = master.shape[0]
    rot_scale = 1.0 / (math.sqrt(2 * key_width) * all_tokens)
    aligned = master_rows % 128 == 0
    if aligned and (nodes, reps) == (8, 4):
        return fused(
            nodes, reps, rot_scale, tokens, norm_gain, key_cotangent, secondary, master,
            moment_first, moment_second, signs,
        )
    had_table = sylvester(key_width)
    sign_rows = (1 - 2 * signs).astype(jnp.float32).reshape(2, key_width)
    floats = tokens.astype(jnp.float32)
    inverse = lax.rsqrt(jnp.mean(floats * floats, axis=-1, keepdims=True) + norm_eps)
    normed = floats * inverse
    hidden = (normed * norm_gain).astype(jnp.bfloat16)
    if not aligned:
        hidden = hidden.reshape(tok_rows, nodes * reps, master_rows).transpose(1, 0, 2)
    coded, keys, hidden_grad = step(
        nodes, reps, aligned, rot_scale, hidden, key_cotangent, secondary,
        sign_rows,
    )
    if not aligned:
        hidden_grad = hidden_grad.transpose(1, 0, 2).reshape(tok_rows, model_width)
    hidden_grad = hidden_grad.astype(jnp.float32)
    new_first = beta_first * moment_first + (1.0 - beta_first) * coded
    new_second = beta_second * moment_second + (1.0 - beta_second) * coded * coded
    first_hat = new_first / (1.0 - beta_first**adam_steps)
    second_hat = new_second / (1.0 - beta_second**adam_steps)
    ratio = first_hat / (jnp.sqrt(second_hat) + adam_eps)
    lower = ratio[:, :key_width]
    upper = ratio[:, key_width:]
    norm_root = math.sqrt(2 * key_width)
    row_even = (
        jnp.dot(lower + upper, had_table, precision=lax.Precision.HIGHEST)
        / norm_root
        * sign_rows[0]
    )
    row_odd = (
        jnp.dot(lower - upper, had_table, precision=lax.Precision.HIGHEST)
        / norm_root
        * sign_rows[1]
    )
    groups = master_rows // (2 * PAIR_GAP)
    update = jnp.stack(
        [
            row_even.reshape(groups, PAIR_GAP, key_width),
            row_odd.reshape(groups, PAIR_GAP, key_width),
        ],
        axis=1,
    ).reshape(master_rows, key_width)
    new_master = master - learn_rate * (update + weight_decay * master)
    new_secondary = spread(reps, new_master.astype(jnp.bfloat16)).reshape(
        reps * master_rows, key_width
    )
    scaled = hidden_grad * norm_gain
    token_grad = (
        inverse * (scaled - normed * jnp.mean(scaled * normed, axis=-1, keepdims=True))
    ).astype(jnp.bfloat16)
    return (keys, token_grad, new_master, new_first, new_second, new_secondary)


def solution(mesh):
    return jax.shard_map(
        shards,
        mesh=mesh,
        in_specs=(
            P(("node", "rep"), None),
            P(),
            P(("node", "rep"), None),
            P("node", None),
            P(("node", "rep"), None),
            P(("node", "rep"), None),
            P(("node", "rep"), None),
            P(),
        ),
        out_specs=(
            P(("node", "rep"), None),
            P(("node", "rep"), None),
            P(("node", "rep"), None),
            P(("node", "rep"), None),
            P(("node", "rep"), None),
            P("node", None),
        ),
        check_vma=False,
    )
```

```python
import functools
import math

import jax
import jax.numpy as jnp
from jax import lax
from jax.experimental import pallas as pl
from jax.experimental.pallas import tpu as pltpu
from jax.sharding import PartitionSpec as P

PAIR_GAP = 16
MESH = pl.DeviceIdType.MESH

norm_eps = 1e-05
adam_eps = 1e-08
beta_first = 0.9
beta_second = 0.95
adam_steps = 10
learn_rate = 0.002
weight_decay = 0.1

ANY = pl.BlockSpec(memory_space=pl.ANY)
HBM = pl.BlockSpec(memory_space=pltpu.HBM)
VMEM = pl.BlockSpec(memory_space=pltpu.VMEM)


def sylvester(extent):
    position = jnp.arange(extent, dtype=jnp.int32)
    parity = jnp.zeros((extent, extent), jnp.int32)
    for bit_place in range(extent.bit_length() - 1):
        parity = parity + (position[:, None] >> bit_place & 1) * (
            position[None, :] >> bit_place & 1
        )
    return (1 - 2 * (parity % 2)).astype(jnp.float32)


def split(index):
    return index // 2, lax.rem(index, 2)


def greet(peers):
    barrier = pltpu.get_barrier_semaphore()
    for peer in peers:
        pl.semaphore_signal(barrier, inc=1, device_id=peer, device_id_type=MESH)
    pl.semaphore_wait(barrier, len(peers))


def remote(src, dst, send, recv, peer):
    return pltpu.make_async_remote_copy(
        src_ref=src,
        dst_ref=dst,
        send_sem=send,
        recv_sem=recv,
        device_id=peer,
        device_id_type=MESH,
    )


def axis_peers(axis, size):
    me = lax.axis_index(axis)
    return [{axis: lax.rem(me + k, size)} for k in range(1, size)]


def pair_peers(axis, size):
    high, low = split(lax.axis_index(axis))
    half = size // 2
    partner = {axis: high * 2 + 1 - low}
    same = [{axis: lax.rem(high + k, half) * 2 + low} for k in range(1, half)]
    return partner, same


class PairGather:
    def __init__(self, axis, size, src, out, local_sem, send, recv):
        self.half = size // 2
        me = lax.axis_index(axis)
        high, low = split(me)
        partner, same = pair_peers(axis, size)
        self.local = pltpu.make_async_copy(src, out.at[me], local_sem)
        self.first = [
            remote(src, out.at[me], send.at[0, k], recv.at[0, k], same[k - 1])
            for k in range(1, self.half)
        ]
        self.second = [remote(src, out.at[me], send.at[1, 0], recv.at[1, 0], partner)]
        for k in range(1, self.half):
            origin = lax.rem(high + self.half - k, self.half) * 2 + low
            self.second.append(
                remote(out.at[origin], out.at[origin], send.at[1, k], recv.at[1, k], partner)
            )

    def start(self):
        for copy in self.first:
            copy.start()
        self.second[0].start()
        self.local.start()

    def forward(self, k):
        self.first[k - 1].wait_recv()
        self.second[k].start()

    def finish(self):
        for copy in self.second:
            copy.wait_recv()
        for copy in self.first + self.second:
            copy.wait_send()
        self.local.wait()


def step_kernel(
    nodes, reps, aligned, scale, hid, cot, sec, table, coded, keys, grad_out,
    hid_in, cot_in, sec_in, rot, term, grad, acc, part,
    from_pair, to_same, from_same, key_in,
    cs, cr, hs, hr, ss, sr, ps, pr, zs, zr, gs, gr, ks, kr, cot_own, hid_own, sec_own, grad_own,
):
    f32 = jnp.float32
    rep = lax.axis_index("rep")
    high, low = split(lax.axis_index("node"))
    half = nodes // 2
    partner, same = pair_peers("node", nodes)
    rep_peers = axis_peers("rep", reps)
    columns, key_width = sec_in.shape[1:]
    tok_rows = cot_in.shape[1]
    group_tokens = reps * tok_rows

    def piece(ref, node, owner):
        index = node * reps + owner
        if aligned:
            return ref.at[:, pl.ds(pl.multiple_of(index * columns, columns), columns)]
        return ref.at[index]

    greet(rep_peers + [partner] + same)
    weights = PairGather(
        "node", nodes, sec.at[pl.ds(pl.multiple_of(rep * columns, columns), columns)], sec_in,
        sec_own.at[0], ss, sr,
    )
    weights.start()
    cot_moves = [
        remote(cot, cot_in.at[rep], cs.at[k], cr.at[k], peer) for k, peer in enumerate(rep_peers)
    ]
    cot_moves.append(pltpu.make_async_copy(cot, cot_in.at[rep], cot_own.at[0]))
    for copy in cot_moves:
        copy.start()
    turns = list(range(1, half)) + [0]
    order = [lax.rem(high + k, half) * 2 + 1 - low for k in turns]
    order += [lax.rem(high + k, half) * 2 + low for k in turns]
    hid_moves = []
    for i, node in enumerate(order):
        moves = [
            remote(
                piece(hid, node, peer["rep"]), hid_in.at[node, rep], hs.at[k, i], hr.at[k, i], peer
            )
            for k, peer in enumerate(rep_peers)
        ]
        moves.append(
            pltpu.make_async_copy(piece(hid, node, rep), hid_in.at[node, rep], hid_own.at[i])
        )
        for copy in moves:
            copy.start()
        hid_moves.append(moves)

    for copy in cot_moves:
        copy.wait()
    group_cot = cot_in[...].reshape(group_tokens, key_width)
    shape = (key_width, key_width)
    parity = lax.broadcasted_iota(jnp.int32, shape, 0) & lax.broadcasted_iota(jnp.int32, shape, 1)
    for shift in (8, 4, 2, 1):
        parity = parity ^ (parity >> shift)
    had = (1 - 2 * (parity & 1)).astype(f32).astype(rot.dtype)
    for a in range(2):
        flipped = (group_cot.astype(f32) * table[a : a + 1, :]).astype(rot.dtype)
        rot[:, a * key_width : (a + 1) * key_width] = (
            jnp.dot(flipped, had, preferred_element_type=f32) * scale
        ).astype(rot.dtype)
    acc[...] = jnp.zeros_like(acc)

    def make_term(i):
        for copy in hid_moves[i]:
            copy.wait()
        chunk = hid_in[order[i]].reshape(group_tokens, columns)
        product = lax.dot_general(
            chunk, rot[...], (((0,), (0,)), ((), ())), preferred_element_type=f32
        ).reshape(columns // (2 * PAIR_GAP), 2, PAIR_GAP, 2 * key_width)
        first = product[:, 0, :, :key_width].reshape(columns // 2, key_width)
        second = product[:, 1, :, key_width:].reshape(columns // 2, key_width)
        term[i, :, :key_width] = (first + second).astype(term.dtype)
        term[i, :, key_width:] = (first - second).astype(term.dtype)

    swaps = []
    stays = []

    def use_weights(count, node):
        block = sec_in[node]
        rows = lax.dot_general(
            cot_in[...].reshape(group_tokens, key_width), block, (((1,), (1,)), ((), ())),
            preferred_element_type=f32,
        )
        grad[node] = rows.astype(grad.dtype).reshape(reps, tok_rows, columns)
        for k, peer in enumerate(rep_peers):
            copy = remote(
                grad.at[node, peer["rep"]], piece(grad_out, node, rep),
                gs.at[k, count], gr.at[k, count], peer,
            )
            copy.start()
            swaps.append(copy)
        copy = pltpu.make_async_copy(
            grad.at[node, rep], piece(grad_out, node, rep), grad_own.at[count]
        )
        copy.start()
        stays.append(copy)
        chunk = hid_in[node].reshape(group_tokens, columns)
        acc[...] += jnp.dot(chunk, block, preferred_element_type=f32)

    pairs = []
    for i in range(half):
        make_term(i)
        pairs.append(remote(term.at[i], from_pair.at[i], ps.at[i], pr.at[i], partner))
        pairs[-1].start()
        if i:
            weights.forward(i)
    weights.local.wait()
    onward = []
    for j, k in enumerate(turns):
        make_term(half + j)
        pairs[j].wait_recv()
        total = term[half + j].astype(f32) + from_pair[j].astype(f32)
        if k:
            to_same[j] = total.astype(to_same.dtype)
            onward.append(remote(to_same.at[j], from_same.at[j], zs.at[j], zr.at[j], same[k - 1]))
            onward[-1].start()
        else:
            coded[...] = total
        use_weights(j, order[half + j])
    for j in range(half):
        weights.second[j].wait_recv()
        use_weights(half + j, lax.rem(high + half - j, half) * 2 + 1 - low)
    part[...] = acc[...].astype(part.dtype).reshape(part.shape)
    key_moves = [
        remote(part.at[peer["rep"]], key_in.at[k], ks.at[k], kr.at[k], peer)
        for k, peer in enumerate(rep_peers)
    ]
    for copy in key_moves:
        copy.start()
    for j, copy in enumerate(onward):
        copy.wait_recv()
        coded[...] += from_same[j].astype(f32)
    total = part[rep].astype(f32)
    for k, copy in enumerate(key_moves):
        copy.wait_recv()
        total = total + key_in[k].astype(f32)
    keys[...] = total.astype(keys.dtype)
    for copy in swaps:
        copy.wait()
    for copy in stays:
        copy.wait()
    for copy in weights.first + weights.second + pairs + onward + key_moves:
        copy.wait_send()


def step(nodes, reps, aligned, scale, hid, cot, sec, table):
    dma = pltpu.SemaphoreType.DMA
    half = nodes // 2
    columns = sec.shape[0] // reps
    tok_rows, key_width = cot.shape
    group_tokens = reps * tok_rows
    block = (columns // 2, 2 * key_width)
    bf16 = jnp.bfloat16
    return pl.pallas_call(
        functools.partial(step_kernel, nodes, reps, aligned, scale),
        out_shape=(
            jax.ShapeDtypeStruct(block, jnp.float32),
            jax.ShapeDtypeStruct(cot.shape, bf16),
            jax.ShapeDtypeStruct(hid.shape, bf16),
        ),
        in_specs=[ANY, ANY, ANY, VMEM],
        out_specs=(VMEM,) * 3,
        scratch_shapes=[
            pltpu.VMEM((nodes, reps, tok_rows, columns), bf16),
            pltpu.VMEM((reps, tok_rows, key_width), bf16),
            pltpu.VMEM((nodes, columns, key_width), bf16),
            pltpu.VMEM((group_tokens, 2 * key_width), bf16),
            pltpu.VMEM((nodes,) + block, bf16),
            pltpu.VMEM((nodes, reps, tok_rows, columns), bf16),
            pltpu.VMEM((group_tokens, key_width), jnp.float32),
            pltpu.VMEM((reps, tok_rows, key_width), bf16),
            pltpu.VMEM((half,) + block, bf16),
            pltpu.VMEM((half - 1,) + block, bf16),
            pltpu.VMEM((half - 1,) + block, bf16),
            pltpu.VMEM((reps - 1, tok_rows, key_width), bf16),
        ]
        + [dma((reps - 1,))] * 2
        + [dma((reps - 1, nodes))] * 2
        + [dma((2, half))] * 2
        + [dma((half,))] * 2
        + [dma((half - 1,))] * 2
        + [dma((reps - 1, nodes))] * 2
        + [dma((reps - 1,))] * 2
        + [dma((1,)), dma((nodes,)), dma((1,)), dma((nodes,))],
        compiler_params=pltpu.CompilerParams(collective_id=0, has_side_effects=True),
    )(hid, cot, sec, table)


def spread_kernel(reps, src, out, send, recv, local):
    partner, same = pair_peers("rep", reps)
    greet([partner] + same)
    rows = PairGather("rep", reps, src, out, local.at[0], send, recv)
    rows.start()
    for k in range(1, reps // 2):
        rows.forward(k)
    rows.finish()


def spread(reps, rows):
    dma = pltpu.SemaphoreType.DMA
    return pl.pallas_call(
        functools.partial(spread_kernel, reps),
        out_shape=jax.ShapeDtypeStruct((reps,) + rows.shape, rows.dtype),
        in_specs=[VMEM],
        out_specs=VMEM,
        scratch_shapes=[dma((2, reps // 2))] * 2 + [dma((1,))],
        compiler_params=pltpu.CompilerParams(collective_id=1, has_side_effects=True),
    )(rows)


def flip(index, bits):
    for bit in (1, 2, 4):
        if bits & bit:
            index = index + bit * (1 - 2 * lax.rem(lax.div(index, bit), 2))
    return index


def fused_kernel(
    nodes, reps, scale,
    tok, gain_hbm, cot, sec, master, first, second, signs_hbm,
    keys_out, grad_in, master_out, first_out, second_out, sec_out, x_in, gain, inv, factor,
    hid, hid_in, cot_in, sec_in, sec_own, rot, had, term, total, from_pair,
    to_chain, from_chain, grad, acc,
    part, part_in, cross, cross_in, master_in, first_in, second_in, ext, ext_half, signs,
    xl, ll, cs, cr, hs, hr, ws, wr, ps, pr, zs, zr, gs, gr, ks, kr, ss, sr, es, er, fs, fr,
):
    f32, bf16 = jnp.float32, jnp.bfloat16
    rep = lax.axis_index("rep")
    me = lax.axis_index("node")
    pieces, tok_rows, columns = x_in.shape
    key_width = cot_in.shape[2]
    group_tokens = reps * tok_rows
    half = columns // 2
    rep_kinds = (2, 3, 1)
    rep_peer = {k: {"rep": flip(rep, k)} for k in rep_kinds}
    level, side = split(me)
    upper, odd = split(level)
    inner = upper + odd - 2 * upper * odd
    beside = {"node": flip(me, 1)}
    next_to = {"node": flip(me, 2)}
    middle = {"node": 2 * (nodes // 2 - 1 - level) + side}

    def inside(body):
        pl.when(inner == 1)(body)

    def at_end(body):
        pl.when(inner == 0)(body)

    last = nodes // 2 - 1
    source = [level + 1 - 2 * odd, 2 - upper, last - last * upper]
    target = [last - last * upper, 2 + upper - 2 * odd, 1 + odd, level]

    def node_at(z, other):
        return 2 * z + (1 - side if other else side)

    loads = [
        pltpu.make_async_copy(tok.at[:, pl.ds(columns * i, columns)], x_in.at[i], xl.at[i])
        for i in range(pieces)
    ]
    own_cot = pltpu.make_async_copy(cot, cot_in.at[rep], ll.at[0])
    own_sec = pltpu.make_async_copy(sec, sec_own, ll.at[1])
    state = [
        pltpu.make_async_copy(master, master_in, ll.at[2]),
        pltpu.make_async_copy(first, first_in, ll.at[3]),
        pltpu.make_async_copy(second, second_in, ll.at[4]),
    ]
    small = [
        pltpu.make_async_copy(gain_hbm, gain, ll.at[5]),
        pltpu.make_async_copy(signs_hbm, signs, ll.at[6]),
    ]
    for copy in [own_cot] + loads + small + [own_sec] + state:
        copy.start()
    barrier = pltpu.get_barrier_semaphore()
    common = [rep_peer[k] for k in rep_kinds] + [beside, next_to]
    for peer in common:
        pl.semaphore_signal(barrier, inc=1, device_id=peer, device_id_type=MESH)

    @inside
    def _():
        pl.semaphore_signal(barrier, inc=1, device_id=middle, device_id_type=MESH)

    pl.semaphore_wait(barrier, len(common) + inner)

    sent = []
    sent_inside = []
    sent_at_end = []

    def go(copy, where=sent):
        copy.start()
        where.append(copy)
        return copy

    quarter = sec.at[pl.ds(pl.multiple_of(rep * columns, columns), columns)]
    counter = []
    extra = [[], []]

    def fetch(e, h):
        start = pl.multiple_of(flip(rep, 2) * columns + h * half, half)
        peer = next_to if e else beside
        dst = ext.at[e, 2, pl.ds(h * half, half)]
        slot = 2 * h
        extra[e].append(
            go(remote(sec.at[pl.ds(start, half)], dst, es.at[e, slot], er.at[e, slot], peer))
        )

    def weight(z, other, peer, slot, where=sent):
        node = me if z is None else node_at(z, other)
        src = quarter if z is None else sec_in.at[node]
        index = len(counter)
        counter.append(index)
        copy = remote(src, sec_in.at[node], ws.at[index], wr.at[slot], peer)
        where.append(copy)
        return copy

    def arrived(slot):
        block = sec_in.at[me]
        remote(block, block, ws.at[0], wr.at[slot], beside).wait_recv()

    weight(None, 0, next_to, (0, 0)).start()
    weight(None, 0, beside, (0, 3)).start()
    inside(weight(None, 0, middle, (0, 1), sent_inside).start)
    for e in range(2):
        fetch(e, 0)

    cot_moves = {
        2: go(remote(cot, cot_in.at[rep], cs.at[0], cr.at[0], rep_peer[2])),
        1: go(remote(cot, cot_in.at[rep], cs.at[1], cr.at[1], rep_peer[1])),
    }

    for copy in loads + small:
        copy.wait()

    def squares(i, running):
        x = x_in[i].astype(f32)
        x = x * x
        for lane in range(0, columns, 128):
            running = running + x[:, lane : lane + 128]
        return running

    squared = lax.fori_loop(0, pieces, squares, jnp.zeros((tok_rows, 128), f32))
    mean = jnp.sum(squared, axis=-1, keepdims=True) * (1.0 / (pieces * columns))
    inv[...] = jnp.broadcast_to(lax.rsqrt(mean + norm_eps), inv.shape)

    order = [node_at(z, other) for z in target for other in (1, 0)]
    hid_moves = []
    for i, node in enumerate(order):
        moves = []
        for k in rep_kinds + (0,):
            owner = flip(rep, k)
            index = node * reps + owner
            value = (x_in[index].astype(f32) * inv[...] * gain[index]).astype(bf16)
            if k:
                hid[node, owner] = value
                moves.append(
                    go(
                        remote(
                            hid.at[node, owner], hid_in.at[node, rep],
                            hs.at[k - 1, i], hr.at[k - 1, i], rep_peer[k],
                        )
                    )
                )
            else:
                hid_in[node, rep] = value
        hid_moves.append(moves)

    shape = (key_width, key_width)
    parity = lax.broadcasted_iota(jnp.int32, shape, 0) & lax.broadcasted_iota(jnp.int32, shape, 1)
    for shift in (8, 4, 2, 1):
        parity = parity ^ (parity >> shift)
    had[...] = (1 - 2 * (parity & 1)).astype(f32).astype(bf16)
    chunks = key_width // 128
    sign_row = []
    for a in range(2):
        bits = [signs[a * chunks + c : a * chunks + c + 1, :] for c in range(chunks)]
        sign_row.append((1 - 2 * jnp.concatenate(bits, axis=1)).astype(f32))

    cot_moves[2].wait_recv()
    across = cot_in.at[flip(rep, 2)]
    cot_moves[3] = go(remote(across, across, cs.at[2], cr.at[2], rep_peer[1]))
    own_cot.wait()
    cot_moves[1].wait_recv()
    cot_moves[3].wait_recv()
    for a in range(2):
        flipped = (cot_in[...].reshape(group_tokens, key_width).astype(f32) * sign_row[a]).astype(bf16)
        rot[:, a * key_width : (a + 1) * key_width] = (
            jnp.dot(flipped, had[...], preferred_element_type=f32) * scale
        ).astype(bf16)

    def make_term(i):
        for copy in hid_moves[i]:
            copy.wait_recv()
        chunk = hid_in[order[i]].reshape(group_tokens, columns)
        product = lax.dot_general(
            chunk, rot[...], (((0,), (0,)), ((), ())), preferred_element_type=f32
        ).reshape(columns // (2 * PAIR_GAP), 2, PAIR_GAP, 2 * key_width)
        upper = product[:, 0, :, :key_width].reshape(half, key_width)
        lower = product[:, 1, :, key_width:].reshape(half, key_width)
        return upper + lower, upper - lower

    def add_up(dst, *parts):
        value = parts[0].astype(f32)
        for other in parts[1:]:
            value = value + other.astype(f32)
        dst[...] = value.astype(dst.dtype)

    grad_moves = []

    def local_grads():
        own_sec.wait()
        for k in range(reps):
            block = sec_own[pl.ds(k * columns, columns)]
            grad_in[me * reps + k] = lax.dot_general(
                cot_in[rep], block, (((1,), (1,)), ((), ())), preferred_element_type=f32
            ).astype(bf16)

    def use_grads(node, cut=False):
        rows = lax.dot_general(
            cot_in[...].reshape(group_tokens, key_width), sec_in[node], (((1,), (1,)), ((), ())),
            preferred_element_type=f32,
        )
        grad[node] = rows.astype(bf16).reshape(reps, tok_rows, columns)
        slot = len(grad_moves)
        moves = []
        for k in rep_kinds:
            src, dst = grad.at[node, flip(rep, k)], grad_in.at[node * reps + rep]
            if cut and k > 1:
                src, dst = src.at[:, pl.ds(half, half)], dst.at[:, pl.ds(half, half)]
            moves.append(
                go(remote(src, dst, gs.at[k - 1, slot], gr.at[k - 1, slot], rep_peer[k]))
            )
        grad_moves.append((node, moves))
        grad_in[node * reps + rep] = grad[node, rep]

    def use_keys(node, start=False):
        if node is me:
            block = sec_own[pl.ds(pl.multiple_of(rep * columns, columns), columns)]
        else:
            block = sec_in[node]
        product = jnp.dot(
            hid_in[node].reshape(group_tokens, columns), block, preferred_element_type=f32
        )
        if start:
            acc[...] = product
        else:
            acc[...] += product

    extra_nodes = [node_at(level, 1), node_at(source[0], 0)]
    def pass_on(e):
        for copy in extra[e][e:]:
            copy.wait_recv()
        for k, src in ((1, sec_in.at[extra_nodes[e]]), (3, ext.at[e, 2])):
            extra[e].append(go(remote(src, ext.at[e, k], es.at[e, k], er.at[e, k], rep_peer[1])))

    def extra_grads(e):
        node = extra_nodes[e]
        for copy in extra[e][2:]:
            copy.wait_recv()
        for k in range(4):
            block = ext[e, k] if k else sec_in[node]
            grad_in[node * reps + flip(rep, k)] = lax.dot_general(
                cot_in[rep], block, (((1,), (1,)), ((), ())), preferred_element_type=f32
            ).astype(bf16)

    half_moves = []

    def fetch_half():
        extra[1][0].wait_recv()
        src = ext.at[1, 2, pl.ds(0, half)]
        half_moves.append(go(remote(src, ext_half.at[0], fs.at[0], fr.at[0], beside)))

    def pass_half():
        half_moves[0].wait_recv()
        half_moves.append(
            go(remote(ext_half.at[0], ext_half.at[1], fs.at[1], fr.at[1], rep_peer[1]))
        )

    def half_grads():
        node = node_at(source[0], 1)
        half_moves[1].wait_recv()
        for i, k in enumerate((2, 3)):
            grad_in[node * reps + flip(rep, k), :, :half] = lax.dot_general(
                cot_in[rep], ext_half[i], (((1,), (1,)), ((), ())), preferred_element_type=f32
            ).astype(bf16)

    pair_moves = {}

    def to_pair(i):
        upper_half, lower_half = make_term(2 * i)
        rows = upper_half.shape[0] // 2
        for h in range(2):
            term[i, h, :, :key_width] = upper_half[h * rows : (h + 1) * rows].astype(bf16)
            term[i, h, :, key_width:] = lower_half[h * rows : (h + 1) * rows].astype(bf16)
            pair_moves[i, h] = go(
                remote(term.at[i, h], from_pair.at[i, h], ps.at[i, h], pr.at[i, h], beside)
            )

    def keep(i):
        upper_half, lower_half = make_term(2 * i + 1)
        total[i, :, :key_width] = upper_half
        total[i, :, key_width:] = lower_half

    def mine(i, h):
        rows = total.shape[1] // 2
        return total[i, h * rows : (h + 1) * rows]

    def chained(index, h):
        dst = from_chain.at[index, h]
        remote(dst, dst, zs.at[0, h], zr.at[index, h], next_to).wait_recv()
        return from_chain[index, h]

    def pass_sum(i, h, within):
        other = middle if within else next_to
        peer, index = [(other, within), (next_to, 2 + within), (other, 3 + within)][i]
        copy = remote(
            to_chain.at[i, h], from_chain.at[index, h], zs.at[i, h], zr.at[index, h], peer
        )
        (sent_inside if within else sent_at_end).append(copy)

        def body():
            pair_moves[i, h].wait_recv()
            parts = [mine(i, h), from_pair[i, h]]
            if within:
                parts.append(chained(i, h))
            add_up(to_chain.at[i, h], *parts)
            copy.start()

        (inside if within else at_end)(body)

    spread_moves = {}
    norm_root = math.sqrt(2 * key_width)
    master_half = columns // 2

    def spread_block(owner, h):
        return sec_out.at[owner, pl.ds(h * master_half, master_half)]

    def finalize(h):
        pair_moves[3, h].wait_recv()
        rows = total.shape[1] // 2
        total[3, h * rows : (h + 1) * rows] = (
            mine(3, h) + from_pair[3, h].astype(f32) + chained(3, h).astype(f32)
        )

        @inside
        def _():
            total[3, h * rows : (h + 1) * rows] += chained(4, h).astype(f32)

        coded = mine(3, h)
        here = pl.ds(h * (half // 2), half // 2)
        new_first = beta_first * first_in[here] + (1.0 - beta_first) * coded
        new_second = beta_second * second_in[here] + (1.0 - beta_second) * coded * coded
        first_out[here] = new_first
        second_out[here] = new_second
        first_hat = new_first / (1.0 - beta_first**adam_steps)
        second_hat = new_second / (1.0 - beta_second**adam_steps)
        ratio = first_hat / (jnp.sqrt(second_hat) + adam_eps)
        rows = []
        for a in range(2):
            if a:
                mixed = ratio[:, :key_width] - ratio[:, key_width:]
            else:
                mixed = ratio[:, :key_width] + ratio[:, key_width:]
            turned = jnp.zeros_like(mixed)
            for _ in range(3):
                high = mixed.astype(bf16)
                mixed = mixed - high.astype(f32)
                turned = turned + jnp.dot(high, had[...], preferred_element_type=f32)
            rows.append(
                (turned * (1.0 / norm_root) * sign_row[a]).reshape(
                    half // (2 * PAIR_GAP), 1, PAIR_GAP, key_width
                )
            )
        update = jnp.concatenate(rows, axis=1).reshape(master_half, key_width)
        there = pl.ds(h * master_half, master_half)
        old = master_in[there]
        new_master = old - learn_rate * (update + weight_decay * old)
        master_out[there] = new_master
        sec_out[rep, there] = new_master.astype(bf16)
        src = spread_block(rep, h)
        for k in (2, 1):
            spread_moves[k, h] = go(
                remote(src, src, ss.at[k - 1, h], sr.at[k - 1, h], rep_peer[k])
            )

    def spread_on(h):
        spread_moves[2, h].wait_recv()
        src = spread_block(flip(rep, 2), h)
        spread_moves[3, h] = go(remote(src, src, ss.at[2, h], sr.at[2, h], rep_peer[1]))

    to_pair(0)
    local_grads()
    arrived((0, 0))

    first_on = weight(source[0], 0, middle, (0, 2), sent_inside)
    second_on = weight(source[1], 0, next_to, (0, 1), sent_inside)

    @inside
    def _():
        first_on.start()
        arrived((0, 1))
        second_on.start()

    arrived((0, 3))
    at_end(weight(level, 1, next_to, (1, 0), sent_at_end).start)
    across_on = [
        weight(level, 1, middle, (1, 1), sent_inside),
        weight(level, 1, next_to, (1, 0), sent_inside),
    ]

    @inside
    def _():
        for copy in across_on:
            copy.start()


    keep(0)
    pass_sum(0, 0, 0)
    to_pair(1)
    pass_sum(0, 1, 0)

    fifth_on = weight(source[2], 0, next_to, (0, 2), sent_inside)

    @inside
    def _():
        arrived((0, 2))
        fifth_on.start()

    keep(1)
    pass_sum(0, 0, 1)
    pass_sum(1, 0, 0)

    @at_end
    def _():
        arrived((0, 1))

    use_grads(node_at(source[1], 0))
    to_pair(2)
    pass_sum(0, 1, 1)
    pass_sum(1, 1, 0)
    keep(2)
    use_keys(node_at(source[0], 0), True)
    use_keys(node_at(source[1], 0))
    pass_sum(1, 0, 1)
    pass_sum(2, 0, 0)
    arrived((1, 0))
    use_grads(node_at(source[0], 1), True)
    to_pair(3)
    pass_sum(2, 0, 1)
    pass_sum(1, 1, 1)
    pass_sum(2, 1, 0)

    sideways = weight(source[2], 0, beside, (1, 2), sent_at_end)

    @at_end
    def _():
        arrived((0, 2))

    use_grads(node_at(source[2], 0))
    at_end(sideways.start)

    fetch(0, 1)
    fetch_half()
    pass_sum(2, 1, 1)

    third_on = weight(source[0], 1, middle, (1, 2), sent_inside)
    fourth_on = weight(source[1], 1, next_to, (1, 1), sent_inside)

    @inside
    def _():
        third_on.start()
        arrived((1, 1))
        fourth_on.start()

    fetch(1, 1)
    keep(3)
    use_keys(node_at(source[2], 0))
    use_keys(node_at(level, 1))
    use_keys(me)
    use_keys(node_at(source[0], 1))
    for copy in state:
        copy.wait()
    finalize(0)
    finalize(1)

    sooner = node_at(inner * source[1] + (1 - inner) * source[2], 1)
    later = node_at(inner * source[2] + (1 - inner) * source[1], 1)

    @at_end
    def _():
        arrived((1, 2))

    use_grads(sooner)
    use_keys(sooner)
    spread_on(0)
    arrived((1, 2 * inner + 1 - inner))
    use_grads(later)
    use_keys(later)
    for i, k in enumerate((3, 1)):
        owner = flip(rep, k)
        part[i] = acc[pl.ds(pl.multiple_of(owner * tok_rows, tok_rows), tok_rows)].astype(bf16)
    part_move = go(remote(part, part_in, ks.at[0], kr.at[0], rep_peer[1]))
    def overlap(node):
        def add(k, running):
            index = node * reps + k
            value = grad_in[index].astype(f32) * gain[index] * x_in[index].astype(f32)
            for lane in range(0, columns, 128):
                running = running + value[:, lane : lane + 128]
            return running

        return add

    def collect(running, node, moves):
        for copy in moves:
            copy.wait_recv()
        return lax.fori_loop(0, reps, overlap(node), running)

    running = jnp.zeros((tok_rows, 128), f32)
    for entry in [(me, []), grad_moves[0], grad_moves[2]]:
        running = collect(running, *entry)
    part_move.wait_recv()
    away = flip(rep, 2)
    cross[...] = (
        acc[pl.ds(pl.multiple_of(away * tok_rows, tok_rows), tok_rows)] + part_in[0].astype(f32)
    ).astype(bf16)
    cross_move = go(remote(cross, cross_in, ks.at[1], kr.at[1], rep_peer[2]))
    spread_on(1)
    for e in range(2):
        pass_on(e)
    pass_half()
    for e in range(2):
        extra_grads(e)
    half_grads()

    for entry in [(node, []) for node in extra_nodes] + grad_moves[1:2] + grad_moves[3:]:
        running = collect(running, *entry)
    against = jnp.sum(running, axis=-1, keepdims=True) * (1.0 / (pieces * columns))
    one = inv[:, :1]
    factor[...] = jnp.broadcast_to(one * one * one * against, factor.shape)

    late = [cross_move] + [spread_moves[3, h] for h in range(2)]
    for copy in sent:
        if not any(copy is other for other in late):
            copy.wait_send()
    cross_move.wait_recv()
    keys_out[...] = (
        acc[pl.ds(pl.multiple_of(rep * tok_rows, tok_rows), tok_rows)]
        + part_in[1].astype(f32)
        + cross_in[...].astype(f32)
    ).astype(keys_out.dtype)
    for k in (1, 3):
        for h in range(2):
            spread_moves[k, h].wait_recv()
    for copy in late:
        copy.wait_send()

    @inside
    def _():
        for copy in sent_inside:
            copy.wait_send()

    @at_end
    def _():
        for copy in sent_at_end:
            copy.wait_send()


def store_kernel(keys, grad, master, first, second, sec, x, gain, inv, factor, *refs):
    keys_out, grad_out, master_out, first_out, second_out, sec_out, done, sems = refs
    pieces, _, columns = grad.shape
    rows = sec.shape[1]
    pairs = [(keys, keys_out), (master, master_out), (first, first_out), (second, second_out)]
    pairs += [(sec.at[i], sec_out.at[pl.ds(rows * i, rows)]) for i in range(sec.shape[0])]
    moves = [
        pltpu.make_async_copy(src, dst, sems.at[pieces + i]) for i, (src, dst) in enumerate(pairs)
    ]
    for copy in moves:
        copy.start()
    for i in range(pieces):
        scaled = grad[i].astype(jnp.float32) * gain[i]
        done[i] = (inv[...] * scaled - x[i].astype(jnp.float32) * factor[...]).astype(done.dtype)
        moves.append(
            pltpu.make_async_copy(
                done.at[i], grad_out.at[:, pl.ds(columns * i, columns)], sems.at[i]
            )
        )
        moves[-1].start()
    for copy in moves:
        copy.wait()


def fused(nodes, reps, scale, tokens, gain, cot, sec, master, first, second, signs):
    dma = pltpu.SemaphoreType.DMA
    f32, bf16 = jnp.float32, jnp.bfloat16
    tok_rows, model_width = tokens.shape
    key_width = cot.shape[1]
    columns = master.shape[0]
    pieces = model_width // columns
    block = first.shape
    part = (block[0] // 2, block[1])
    group_tokens = reps * tok_rows
    vmem = pltpu.VMEM
    far = functools.partial(pltpu.with_memory_space_constraint, memory_space=pltpu.HBM)
    results = pl.pallas_call(
        functools.partial(fused_kernel, nodes, reps, scale),
        out_shape=(
            vmem(cot.shape, bf16),
            vmem((pieces, tok_rows, columns), bf16),
            vmem(master.shape, f32),
            vmem(block, f32),
            vmem(block, f32),
            vmem((reps,) + master.shape, bf16),
            vmem((pieces, tok_rows, columns), bf16),
            vmem((pieces, 1, columns), f32),
            vmem((tok_rows, columns), f32),
            vmem((tok_rows, columns), f32),
        ),
        in_specs=[HBM] * 8,
        out_specs=(VMEM,) * 10,
        scratch_shapes=[
            vmem((nodes, reps, tok_rows, columns), bf16),
            vmem((nodes, reps, tok_rows, columns), bf16),
            vmem((reps, tok_rows, key_width), bf16),
            vmem((nodes, columns, key_width), bf16),
            vmem(sec.shape, bf16),
            vmem((group_tokens, 2 * key_width), bf16),
            vmem((key_width, key_width), bf16),
            vmem((4, 2) + part, bf16),
            vmem((4,) + block, f32),
            vmem((4, 2) + part, bf16),
            vmem((3, 2) + part, bf16),
            vmem((5, 2) + part, bf16),
            vmem((nodes, reps, tok_rows, columns), bf16),
            vmem((group_tokens, key_width), f32),
            vmem((2, tok_rows, key_width), bf16),
            vmem((2, tok_rows, key_width), bf16),
            vmem((tok_rows, key_width), bf16),
            vmem((tok_rows, key_width), bf16),
            vmem(master.shape, f32),
            vmem(block, f32),
            vmem(block, f32),
            vmem((2, 4, columns, key_width), bf16),
            vmem((2, columns // 2, key_width), bf16),
            vmem((2 * key_width // 128, 128), jnp.int32),
        ]
        + [dma((pieces,)), dma((7,))]
        + [dma((3,))] * 2
        + [dma((3, nodes))] * 2
        + [dma((12,)), dma((2, 4))]
        + [dma((4, 2))] * 2
        + [dma((3, 2)), dma((5, 2))]
        + [dma((3, nodes))] * 2
        + [dma((2,))] * 2
        + [dma((3, 2))] * 2
        + [dma((2, 4))] * 2
        + [dma((2,))] * 2,
        compiler_params=pltpu.CompilerParams(
            collective_id=2, has_side_effects=True, vmem_limit_bytes=48 << 20
        ),
    )(
        far(tokens), far(gain.reshape(pieces, 1, columns)), far(cot), far(sec), far(master),
        far(first), far(second), far(signs.reshape(-1, 128)),
    )
    held = [pltpu.with_memory_space_constraint(value, pltpu.VMEM) for value in results]
    like = jax.ShapeDtypeStruct
    return pl.pallas_call(
        store_kernel,
        out_shape=(
            like(cot.shape, bf16),
            like(tokens.shape, bf16),
            like(master.shape, f32),
            like(block, f32),
            like(block, f32),
            like(sec.shape, bf16),
        ),
        in_specs=[VMEM] * 10,
        out_specs=(ANY,) * 6,
        scratch_shapes=[vmem((pieces, tok_rows, columns), bf16), dma((pieces + 4 + reps,))],
        compiler_params=pltpu.CompilerParams(vmem_limit_bytes=6 << 20),
    )(*held)


def shards(tokens, norm_gain, key_cotangent, secondary, master, moment_first, moment_second, signs):
    tok_rows, model_width = tokens.shape
    key_width = key_cotangent.shape[1]
    nodes = lax.axis_size("node")
    reps = lax.axis_size("rep")
    all_tokens = tok_rows * nodes * reps
    master_rows = master.shape[0]
    rot_scale = 1.0 / (math.sqrt(2 * key_width) * all_tokens)
    aligned = master_rows % 128 == 0
    if aligned and (nodes, reps) == (8, 4):
        return fused(
            nodes, reps, rot_scale, tokens, norm_gain, key_cotangent, secondary, master,
            moment_first, moment_second, signs,
        )
    had_table = sylvester(key_width)
    sign_rows = (1 - 2 * signs).astype(jnp.float32).reshape(2, key_width)
    floats = tokens.astype(jnp.float32)
    inverse = lax.rsqrt(jnp.mean(floats * floats, axis=-1, keepdims=True) + norm_eps)
    normed = floats * inverse
    hidden = (normed * norm_gain).astype(jnp.bfloat16)
    if not aligned:
        hidden = hidden.reshape(tok_rows, nodes * reps, master_rows).transpose(1, 0, 2)
    coded, keys, hidden_grad = step(
        nodes, reps, aligned, rot_scale, hidden, key_cotangent, secondary,
        sign_rows,
    )
    if not aligned:
        hidden_grad = hidden_grad.transpose(1, 0, 2).reshape(tok_rows, model_width)
    hidden_grad = hidden_grad.astype(jnp.float32)
    new_first = beta_first * moment_first + (1.0 - beta_first) * coded
    new_second = beta_second * moment_second + (1.0 - beta_second) * coded * coded
    first_hat = new_first / (1.0 - beta_first**adam_steps)
    second_hat = new_second / (1.0 - beta_second**adam_steps)
    ratio = first_hat / (jnp.sqrt(second_hat) + adam_eps)
    lower = ratio[:, :key_width]
    upper = ratio[:, key_width:]
    norm_root = math.sqrt(2 * key_width)
    row_even = (
        jnp.dot(lower + upper, had_table, precision=lax.Precision.HIGHEST)
        / norm_root
        * sign_rows[0]
    )
    row_odd = (
        jnp.dot(lower - upper, had_table, precision=lax.Precision.HIGHEST)
        / norm_root
        * sign_rows[1]
    )
    groups = master_rows // (2 * PAIR_GAP)
    update = jnp.stack(
        [
            row_even.reshape(groups, PAIR_GAP, key_width),
            row_odd.reshape(groups, PAIR_GAP, key_width),
        ],
        axis=1,
    ).reshape(master_rows, key_width)
    new_master = master - learn_rate * (update + weight_decay * master)
    new_secondary = spread(reps, new_master.astype(jnp.bfloat16)).reshape(
        reps * master_rows, key_width
    )
    scaled = hidden_grad * norm_gain
    token_grad = (
        inverse * (scaled - normed * jnp.mean(scaled * normed, axis=-1, keepdims=True))
    ).astype(jnp.bfloat16)
    return (keys, token_grad, new_master, new_first, new_second, new_secondary)


def solution(mesh):
    return jax.shard_map(
        shards,
        mesh=mesh,
        in_specs=(
            P(("node", "rep"), None),
            P(),
            P(("node", "rep"), None),
            P("node", None),
            P(("node", "rep"), None),
            P(("node", "rep"), None),
            P(("node", "rep"), None),
            P(),
        ),
        out_specs=(
            P(("node", "rep"), None),
            P(("node", "rep"), None),
            P(("node", "rep"), None),
            P(("node", "rep"), None),
            P(("node", "rep"), None),
            P("node", None),
        ),
        check_vma=False,
    )
```
